32 devices in a mesh: ctx: 8 (over z, y), head: 4 (over x, core).
Axes of the slice: x: 2, y: 2, z: 4, core: 2. Of those that a mesh axis runs over, the one named last changes fastest.
Arguments:
- x_in: bfloat16 [1024, 8192], P(('ctx', 'head')), may hold values from -6 to 6
- b_in: bfloat16 [1024, 1024], P(('ctx', 'head')), may hold values from -6 to 6
- c_in: bfloat16 [1024, 1024], P(('ctx', 'head')), may hold values from -6 to 6
- dt_in: bfloat16 [1024, 128], P(('ctx', 'head')), may hold values from -5 to 8
- z_in: bfloat16 [1024, 8192], P(('ctx', 'head')), may hold values from -6 to 6
- conv_x: float32 [4, 8192], replicated, may hold values from -3 to 3
- input_state_taps: float32 [4, 1024], replicated, may hold values from -3 to 3
- conv_c: float32 [4, 1024], replicated, may hold values from -3 to 3
- dt_bias: float32 [128], replicated, may hold values from -0.5 to 0.5
- a_log: float32 [128], replicated, may hold values from -20 to -2
- norm_gain: float32 [8192], replicated, may hold values from 0.1 to 1.9
Outputs:
- y_out: bfloat16 [1024, 8192], P(('ctx', 'head'))
The draws below stay inside these ranges and needn't reach their ends.
All inputs are finite; a program needn't handle non-finite values.
Results may differ from the reference program's by a relative error of at most 0.0052.
Values may be sent and summed in bfloat16 or wider, within the bound.
No kernel may reach another device: no remote copies, remote signals or barrier semaphores. Data moves between devices by JAX's collectives and lax.ppermute only.
A program may use at most 192 MiB of HBM per device.

```python
import math
import jax
import jax.numpy as jnp
from jax import lax

HEADS = 128
HEAD_DIM = 64
STATE = 128
GROUPS = 8
KERNEL = 4
BLOCK = 128
TOK_DEV = 128
SEQ = 1024


def draw_dt_in(key, part):
    keys = jax.random.split(key, 3)
    random_jitter = jax.random.truncated_normal(keys[0], -3.0, 3.0, (SEQ, HEADS), jnp.float32) * 0.8
    position_shift = jax.random.uniform(keys[1], (SEQ // TOK_DEV, 1, HEADS), jnp.float32, -2.0, 0.0)
    position_shift = jnp.broadcast_to(position_shift, (SEQ // TOK_DEV, TOK_DEV, HEADS)).reshape(SEQ, HEADS)
    spots = jax.random.randint(keys[2], (4,), 0, SEQ)
    flagged_entries = jnp.any(jnp.arange(SEQ)[:, None] == spots[None, :], axis=1)
    sudden_spike = jnp.where(flagged_entries, 5.0, 0.0)[:, None]
    return (random_jitter + position_shift + sudden_spike).astype(jnp.bfloat16)


def draw_a_log(key, part):
    keys = jax.random.split(key, 3)
    share = 0.5
    quick_pick = jax.random.uniform(keys[0], (HEADS,), jnp.float32) < share
    quick = jax.random.uniform(keys[1], (HEADS,), jnp.float32, math.log(0.04), math.log(0.1))
    slow = jax.random.uniform(keys[2], (HEADS,), jnp.float32, math.log(0.5), math.log(2.0)) - math.log(SEQ)
    return jnp.where(quick_pick, quick, slow).astype(jnp.float32)


def block_levels(stream_key, extent, cuts, least, largest):
    def one(axis_at, blocks):
        draws = jax.random.uniform(jax.random.fold_in(jax.random.fold_in(stream_key, 6), axis_at), (blocks,), jnp.float32, least / len(cuts), largest / len(cuts))
        return jnp.repeat(jnp.exp(draws), extent[axis_at] // blocks).reshape((-1,) + (1,) * (len(extent) - axis_at - 1))

    level = one(*cuts[0])
    for cut in cuts[1:]:
        level = level * one(*cut)
    return level


def noise(key, extent, deviation, most, cuts=(), held_as=jnp.bfloat16):
    array = deviation * jax.random.normal(key, extent, jnp.float32)
    if cuts:
        array = array * block_levels(key, extent, cuts, -0.22, 0.18)
    return jnp.clip(array, -most, most).astype(held_as)


def setup_inputs(seed: int = 0) -> dict:
    arg_keys = jax.random.split(jax.random.key(seed), 12)
    x_in = noise(arg_keys[0], (SEQ, HEADS * HEAD_DIM), 1.0, 6.0, ((0, 32),))
    b_in = noise(arg_keys[1], (SEQ, GROUPS * STATE), 1.0, 6.0, ((0, 32),))
    c_in = noise(arg_keys[2], (SEQ, GROUPS * STATE), 1.0, 6.0, ((0, 32),))
    dt_in = draw_dt_in(jax.random.fold_in(arg_keys[11], 71), 0)
    z_in = noise(arg_keys[4], (SEQ, HEADS * HEAD_DIM), 1.0, 6.0, ((0, 32),))
    conv_x = noise(arg_keys[5], (KERNEL, HEADS * HEAD_DIM), KERNEL ** -0.5, 3.0, (), jnp.float32)
    input_state_taps = noise(arg_keys[6], (KERNEL, GROUPS * STATE), KERNEL ** -0.5, 3.0, (), jnp.float32)
    conv_c = noise(arg_keys[7], (KERNEL, GROUPS * STATE), KERNEL ** -0.5, 3.0, (), jnp.float32)
    dt_bias = jnp.clip(jax.random.uniform(arg_keys[8], (HEADS,), jnp.float32, -0.5, 0.5), -0.5, 0.5)
    a_log = draw_a_log(jax.random.fold_in(arg_keys[11], 71), 0)
    norm_gain = jnp.clip(1.0 + 0.18 * jax.random.normal(arg_keys[10], (HEADS * HEAD_DIM,), jnp.float32), 0.1, 1.9)
    return dict(x_in=x_in, b_in=b_in, c_in=c_in, dt_in=dt_in, z_in=z_in, conv_x=conv_x, input_state_taps=input_state_taps, conv_c=conv_c, dt_bias=dt_bias, a_log=a_log, norm_gain=norm_gain)


eps_norm = 1e-05

def conv_block(window, weights):
    count = window.shape[0] - KERNEL + 1
    total = jnp.zeros((count, window.shape[1]), jnp.float32)
    for position_shift in range(KERNEL):
        total = total + weights[position_shift] * window[position_shift:position_shift + count].astype(jnp.float32)
    return jax.nn.silu(total).astype(jnp.bfloat16)

def pad_front(values):
    return jnp.concatenate([jnp.zeros((KERNEL - 1, values.shape[1]), values.dtype), values], 0)

def reference(x_in, b_in, c_in, dt_in, z_in, conv_x, input_state_taps, conv_c, dt_bias, a_log, norm_gain):
    high = lax.Precision.HIGHEST
    x_pad, b_pad, c_pad = (pad_front(x_in), pad_front(b_in), pad_front(c_in))
    rate = -jnp.exp(a_log)
    per = HEADS // GROUPS
    causal = lax.broadcasted_iota(jnp.int32, (BLOCK, BLOCK), 0) >= lax.broadcasted_iota(jnp.int32, (BLOCK, BLOCK), 1)

    def step(state, index):
        start = (index * BLOCK).astype(jnp.int32)
        xc = conv_block(lax.dynamic_slice_in_dim(x_pad, start, BLOCK + KERNEL - 1, 0), conv_x).reshape(BLOCK, HEADS, HEAD_DIM)
        bc = conv_block(lax.dynamic_slice_in_dim(b_pad, start, BLOCK + KERNEL - 1, 0), input_state_taps).reshape(BLOCK, GROUPS, STATE)
        cc = conv_block(lax.dynamic_slice_in_dim(c_pad, start, BLOCK + KERNEL - 1, 0), conv_c).reshape(BLOCK, GROUPS, STATE)
        dt = jax.nn.softplus(lax.dynamic_slice_in_dim(dt_in, start, BLOCK, 0).astype(jnp.float32) + dt_bias)
        cum = jnp.cumsum(dt * rate, axis=0)
        scores = jnp.einsum('tgn,sgn->gts', cc.astype(jnp.float32), bc.astype(jnp.float32), precision=high)
        scores = jnp.repeat(scores, per, axis=0)
        cum_h = cum.T
        gap = jnp.where(causal[None], cum_h[:, :, None] - cum_h[:, None, :], 0.0)
        mix = jnp.where(causal[None], scores * jnp.exp(gap) * dt.T[:, None, :], 0.0).astype(jnp.bfloat16)
        intra = jnp.einsum('hts,shp->thp', mix.astype(jnp.float32), xc.astype(jnp.float32), precision=high)
        carried = jnp.einsum('tgn,gqpn->tgqp', cc.astype(jnp.float32), state.reshape(GROUPS, per, HEAD_DIM, STATE), precision=high)
        carried = carried.reshape(BLOCK, HEADS, HEAD_DIM) * jnp.exp(cum)[:, :, None]
        y = lax.optimization_barrier((intra + carried).astype(jnp.bfloat16))
        tail = jnp.exp(cum[-1][None, :] - cum) * dt
        weighted = (xc.astype(jnp.float32) * tail[:, :, None]).reshape(BLOCK, GROUPS, per, HEAD_DIM)
        fresh = jnp.einsum('tgqp,tgn->gqpn', weighted, bc.astype(jnp.float32), precision=high).reshape(HEADS, HEAD_DIM, STATE)
        state = jnp.exp(cum[-1])[:, None, None] * state + fresh
        gate = lax.dynamic_slice_in_dim(z_in, start, BLOCK, 0).astype(jnp.float32)
        gated = y.reshape(BLOCK, HEADS * HEAD_DIM).astype(jnp.float32) * jax.nn.silu(gate)
        shaped = gated.reshape(BLOCK, GROUPS, -1)
        scale = lax.rsqrt(lax.optimization_barrier(jnp.mean(shaped * shaped, axis=-1, keepdims=True)) + eps_norm)
        result = ((shaped * scale).reshape(BLOCK, HEADS * HEAD_DIM) * norm_gain).astype(jnp.bfloat16)
        return (state, result)
    first = jnp.zeros((HEADS, HEAD_DIM, STATE), jnp.float32)
    _, outputs = lax.scan(step, first, jnp.arange(SEQ // BLOCK, dtype=jnp.int32))
    return outputs.reshape(SEQ, HEADS * HEAD_DIM)
```

```python
import functools
import jax
import jax.numpy as jnp
from jax import lax
from jax.experimental import pallas as pl
from jax.experimental.pallas import tpu as pltpu
from jax.sharding import Mesh
from jax.sharding import PartitionSpec as P

HEAD_DIM = 64
STATE = 128
GROUPS = 8
BLOCK = 128
OWN = 8
WIDE = OWN * HEAD_DIM
CONV = WIDE + 2 * STATE
LANES = 128

eps_norm = 1e-05
F32 = jnp.float32
BF16 = jnp.bfloat16


def dot(a, b):
    return jnp.dot(a, b, preferred_element_type=F32)


def parts_of(values, count):
    out = []
    for k in range(count):
        piece = values.astype(BF16)
        out.append(piece)
        if k + 1 < count:
            values = values - piece.astype(F32)
    return out


def silu(v):
    return v * jax.nn.sigmoid(v)


def expander(mine):
    row = lax.broadcasted_iota(jnp.int32, (LANES, WIDE), 0)
    col = lax.broadcasted_iota(jnp.int32, (LANES, WIDE), 1)
    return (row - mine * OWN == col // HEAD_DIM).astype(F32).astype(BF16)


def expand(values, spread):
    return sum(dot(piece, spread) for piece in parts_of(values, 2))


def pack_body(x_ref, b_ref, c_ref, dt_ref, out_ref):
    count = out_ref.shape[0]
    share = count // (b_ref.shape[1] // STATE)
    for k in range(count):
        g = k // share
        out_ref[k, :, :WIDE] = x_ref[:, k * WIDE : (k + 1) * WIDE]
        out_ref[k, :, WIDE : WIDE + STATE] = b_ref[:, g * STATE : (g + 1) * STATE]
        out_ref[k, :, WIDE + STATE : CONV] = c_ref[:, g * STATE : (g + 1) * STATE]
        out_ref[k, :, CONV:] = dt_ref[...]


def conv_block(win, taps, out_ref):
    tap_x, tap_b, tap_c = taps
    lead = tap_x.shape[0] - 1
    for lo in range(0, CONV, LANES):
        if lo < WIDE:
            tap, at = tap_x, lo
        else:
            tap, at = (tap_b, 0) if lo == WIDE else (tap_c, 0)
        total = jnp.zeros((BLOCK, LANES), F32)
        for k in range(lead + 1):
            first = 8 - lead + k
            total = total + tap[k : k + 1, at : at + LANES] * win[first : first + BLOCK, lo : lo + LANES]
        out_ref[:, lo : lo + LANES] = silu(total).astype(BF16)


def fresh_state(xbc, cum, dt, spread):
    last = cum[BLOCK - 1 :, :]
    tail = expand(jnp.exp(last - cum) * dt, spread)
    weighted = xbc[:, :WIDE].astype(F32) * tail
    turned = xbc[:, WIDE : WIDE + STATE].T
    return sum(dot(turned, piece) for piece in parts_of(weighted, 2))


def fade_of(cum, spread):
    last = jnp.broadcast_to(jnp.exp(cum[BLOCK - 1 :, :]), (8, LANES))
    return expand(last, spread)[:1]


def intra_block(xbc, cum, dt, mine, rows, put):
    b = xbc[:, WIDE : WIDE + STATE]
    c = xbc[:, WIDE + STATE : CONV]
    scores = lax.dot_general(c, b, (((1,), (1,)), ((), ())), preferred_element_type=F32)
    t_at = lax.broadcasted_iota(jnp.int32, (BLOCK, BLOCK), 0)
    s_at = lax.broadcasted_iota(jnp.int32, (BLOCK, BLOCK), 1)
    scores = jnp.where(t_at >= s_at, scores, 0.0)
    rows[0] = cum.T
    rows[1] = dt.T
    first = pl.multiple_of(mine * OWN, OWN)
    cum_rows = rows[0, pl.ds(first, OWN), :]
    dt_rows = rows[1, pl.ds(first, OWN), :]
    cum_cols = pltpu.roll(cum, lax.rem(LANES - mine * OWN, LANES), 1)
    left = lax.broadcasted_iota(jnp.int32, (BLOCK, LANES), 1) < HEAD_DIM
    zero = jnp.zeros((BLOCK, LANES), BF16)
    for q in range(WIDE // LANES):
        x = xbc[:, q * LANES : (q + 1) * LANES]
        total = None
        for half in range(2):
            h = 2 * q + half
            gap = jnp.minimum(cum_cols[:, h : h + 1] - cum_rows[h : h + 1, :], 0.0)
            mix = (scores * jnp.exp(gap) * dt_rows[h : h + 1, :]).astype(BF16)
            term = dot(mix, jnp.where(left if half == 0 else ~left, x, zero))
            total = term if total is None else total + term
        put(q, total)


def states_body(
    mine_ref, r_ref, halo_ref, tap_x, tap_b, tap_c, bias_ref, log_ref,
    xbc_ref, dt_ref, cum_ref, s_ref, send_ref, fade_ref, win, state, total_fade,
):
    j = pl.program_id(0)
    spread = expander(mine_ref[0])

    @pl.when(j == 0)
    def _():
        win[0:8] = halo_ref[...]
        state[...] = jnp.zeros_like(state)
        total_fade[...] = jnp.ones_like(total_fade)

    @pl.when(j > 0)
    def _():
        win[0:8] = win[BLOCK : BLOCK + 8]

    win[8 : 8 + BLOCK] = r_ref[:, :CONV].astype(F32)
    conv_block(win, (tap_x, tap_b, tap_c), xbc_ref)
    raw = r_ref[:, CONV:].astype(F32) + bias_ref[...]
    dt = jnp.maximum(raw, 0.0) + jnp.log1p(jnp.exp(-jnp.abs(raw)))
    t_at = lax.broadcasted_iota(jnp.int32, (BLOCK, BLOCK), 0)
    s_at = lax.broadcasted_iota(jnp.int32, (BLOCK, BLOCK), 1)
    lower = (t_at >= s_at).astype(F32).astype(BF16)
    cum = sum(dot(lower, piece) for piece in parts_of(dt * -jnp.exp(log_ref[...]), 3))
    dt_ref[...] = dt
    cum_ref[...] = cum
    fresh = fresh_state(xbc_ref, cum, dt, spread)
    fade = fade_of(cum, spread)
    s_ref[0] = fresh
    state[...] = fade * state[...] + fresh
    total_fade[...] = total_fade[...] * fade

    @pl.when(j == pl.num_programs(0) - 1)
    def _():
        send_ref[:STATE] = state[...].astype(BF16)
        send_ref[STATE : STATE + 16] = r_ref[BLOCK - 16 :, :WIDE]
        send_ref[STATE + 16 :, : 2 * STATE] = r_ref[BLOCK - 16 :, WIDE:CONV]
        send_ref[STATE + 16 :, 2 * STATE :] = jnp.zeros((16, WIDE - 2 * STATE), BF16)
        fade_ref[...] = jnp.broadcast_to(total_fade[...], (8, WIDE))


def intra_body(mine_ref, xbc_ref, dt_ref, cum_ref, y_ref, rows):
    def put(q, values):
        y_ref[:, q * LANES : (q + 1) * LANES] = values

    intra_block(xbc_ref, cum_ref[...], dt_ref[...], mine_ref[0], rows, put)


def carry_body(
    mine_ref, r_ref, got_ref, tap_x, tap_b, tap_c, xbc_ref, dt_ref, cum_ref, s_ref, part_ref,
    y_ref, win, first, rows, state, intra, fresh,
):
    j = pl.program_id(0)
    mine = mine_ref[0]
    spread = expander(mine)
    cum = cum_ref[...]
    dt = dt_ref[...]

    @pl.when(j == 0)
    def _():
        state[...] = got_ref[:STATE].astype(F32)
        win[0:8, :WIDE] = got_ref[STATE : STATE + 16].astype(F32)[8:]
        win[0:8, WIDE:] = got_ref[STATE + 16 :, : 2 * STATE].astype(F32)[8:]
        win[8 : 8 + BLOCK] = r_ref[:, :CONV].astype(F32)
        conv_block(win, (tap_x, tap_b, tap_c), first)

        def put(q, values):
            intra[:, q * LANES : (q + 1) * LANES] = values

        intra_block(first, cum, dt, mine, rows, put)
        fresh[...] = fresh_state(first, cum, dt, spread)

    @pl.when(j > 0)
    def _():
        first[:, WIDE + STATE :] = xbc_ref[:, WIDE + STATE :]
        intra[...] = part_ref[...]
        fresh[...] = s_ref[0]

    entering = state[...]
    c = first[:, WIDE + STATE :]
    carried = sum(dot(c, piece) for piece in parts_of(entering, 2))
    y_ref[...] = (intra[...] + carried * expand(jnp.exp(cum), spread)).astype(BF16)
    state[...] = fade_of(cum, spread) * entering + fresh[...]


def norm_body(y_ref, z_ref, gain_ref, out_ref):
    count = y_ref.shape[0]
    share = GROUPS * y_ref.shape[0] * WIDE // (GROUPS * out_ref.shape[1])
    per = 1024 // WIDE
    for g in range(count // per):
        gated = []
        square = 0.0
        for k in range(per):
            at = (g * per + k) * WIDE
            z = z_ref[:, at : at + WIDE].astype(F32)
            v = y_ref[g * per + k].astype(F32) * silu(z)
            gated.append(v)
            square = square + jnp.sum(v * v, axis=1, keepdims=True)
        scale = lax.rsqrt(square / (per * WIDE) + eps_norm)
        for k in range(per):
            at = (g * per + k) * WIDE
            out_ref[:, at : at + WIDE] = (gated[k] * scale * gain_ref[:, at : at + WIDE]).astype(BF16)


def shift(block, axis, distance):
    size = lax.axis_size(axis)
    return lax.ppermute(block, axis, [(i, i + distance) for i in range(size - distance)])


def shards(x_in, b_in, c_in, dt_in, z_in, conv_x, input_state_taps, conv_c, dt_bias, a_log, norm_gain):
    outer, inner, head = (lax.axis_size(a) for a in ("outer", "inner", "head"))
    dests = inner * head
    rows = x_in.shape[0]
    tokens = rows * dests
    blocks = tokens // BLOCK
    lead = conv_x.shape[0] - 1
    mine = (lax.axis_index("inner") * head + lax.axis_index("head")).astype(jnp.int32).reshape(1)
    share = dests * STATE // b_in.shape[1]
    params = functools.partial(pltpu.CompilerParams, vmem_limit_bytes=32 * 2**20)

    step = 4
    sent = pl.pallas_call(
        pack_body,
        grid=(dests // step,),
        in_specs=[
            pl.BlockSpec((rows, step * WIDE), lambda i: (0, i)),
            pl.BlockSpec((rows, step * STATE // share), lambda i: (0, i)),
            pl.BlockSpec((rows, step * STATE // share), lambda i: (0, i)),
            pl.BlockSpec((rows, LANES), lambda i: (0, 0)),
        ],
        out_specs=pl.BlockSpec((step, rows, CONV + LANES), lambda i: (i, 0, 0)),
        out_shape=jax.ShapeDtypeStruct((dests, rows, CONV + LANES), BF16),
        compiler_params=params(),
        name="pack",
    )(x_in, b_in, c_in, dt_in)
    got = lax.all_to_all(sent, ("inner", "head"), 0, 0, tiled=True).reshape(tokens, CONV + LANES)

    if outer > 2:
        halo = shift(got[-8:, :CONV], "outer", 1).astype(F32)
    else:
        halo = jnp.zeros((8, CONV), F32)
    tap_specs = [
        pl.BlockSpec((lead + 1, WIDE), lambda i, m: (0, m[0])),
        pl.BlockSpec((lead + 1, STATE), lambda i, m: (0, m[0] // share)),
        pl.BlockSpec((lead + 1, STATE), lambda i, m: (0, m[0] // share)),
    ]
    taps = (conv_x, input_state_taps, conv_c)

    def per_block(width, ahead=0):
        return pl.BlockSpec((BLOCK, width), lambda i, m: (i + ahead, 0))

    def whole(*shape):
        return pl.BlockSpec(shape, lambda i, m: (0,) * len(shape))

    extra = STATE + 32
    xbc, dt, cum, fresh, total, fade = pl.pallas_call(
        states_body,
        grid_spec=pltpu.PrefetchScalarGridSpec(
            num_scalar_prefetch=1,
            grid=(blocks,),
            in_specs=[per_block(CONV + LANES), whole(8, CONV), *tap_specs, whole(1, LANES), whole(1, LANES)],
            out_specs=[
                per_block(CONV), per_block(LANES), per_block(LANES),
                pl.BlockSpec((1, STATE, WIDE), lambda i, m: (i, 0, 0)),
                whole(extra, WIDE), whole(8, WIDE),
            ],
            scratch_shapes=[
                pltpu.VMEM((BLOCK + 8, CONV), F32),
                pltpu.VMEM((STATE, WIDE), F32),
                pltpu.VMEM((1, WIDE), F32),
            ],
        ),
        out_shape=[
            jax.ShapeDtypeStruct((tokens, CONV), BF16),
            jax.ShapeDtypeStruct((tokens, LANES), F32),
            jax.ShapeDtypeStruct((tokens, LANES), F32),
            jax.ShapeDtypeStruct((blocks, STATE, WIDE), F32),
            jax.ShapeDtypeStruct((extra, WIDE), BF16),
            jax.ShapeDtypeStruct((8, WIDE), F32),
        ],
        compiler_params=params(),
        name="states",
    )(mine, got, halo, *taps, dt_bias.reshape(1, -1), a_log.reshape(1, -1))

    before = shift(total, "outer", 1)
    reach = 1
    if outer > 2:
        entering, held = before[:STATE].astype(F32), shift(fade, "outer", 1)
        while reach < outer - 1:
            entering = entering + held[:1] * shift(entering, "outer", reach)
            held = held * shift(held, "outer", reach)
            reach *= 2
        before = jnp.concatenate([entering.astype(BF16), before[STATE:]], 0)

    part = pl.pallas_call(
        intra_body,
        grid_spec=pltpu.PrefetchScalarGridSpec(
            num_scalar_prefetch=1,
            grid=(blocks - 1,),
            in_specs=[per_block(CONV, 1), per_block(LANES, 1), per_block(LANES, 1)],
            out_specs=per_block(WIDE),
            scratch_shapes=[pltpu.VMEM((2, LANES, BLOCK), F32)],
        ),
        out_shape=jax.ShapeDtypeStruct((tokens - BLOCK, WIDE), F32),
        compiler_params=params(),
        cost_estimate=pl.CostEstimate(
            flops=2 * blocks * OWN * BLOCK * BLOCK * 160,
            bytes_accessed=tokens * (CONV * 2 + LANES * 8 + WIDE * 4),
            transcendentals=blocks * OWN * BLOCK * BLOCK,
        ),
        name="intra",
    )(mine, xbc, dt, cum)

    y = pl.pallas_call(
        carry_body,
        grid_spec=pltpu.PrefetchScalarGridSpec(
            num_scalar_prefetch=1,
            grid=(blocks,),
            in_specs=[
                whole(BLOCK, CONV + LANES), whole(extra, WIDE), *tap_specs,
                per_block(CONV), per_block(LANES), per_block(LANES),
                pl.BlockSpec((1, STATE, WIDE), lambda i, m: (i, 0, 0)),
                pl.BlockSpec((BLOCK, WIDE), lambda i, m: (jnp.maximum(i - 1, 0), 0)),
            ],
            out_specs=per_block(WIDE),
            scratch_shapes=[
                pltpu.VMEM((BLOCK + 8, CONV), F32),
                pltpu.VMEM((BLOCK, CONV), BF16),
                pltpu.VMEM((2, LANES, BLOCK), F32),
                pltpu.VMEM((STATE, WIDE), F32),
                pltpu.VMEM((BLOCK, WIDE), F32),
                pltpu.VMEM((STATE, WIDE), F32),
            ],
        ),
        out_shape=jax.ShapeDtypeStruct((tokens, WIDE), BF16),
        compiler_params=params(),
        name="carry",
    )(mine, got, before, *taps, xbc, dt, cum, fresh, part)

    home = lax.all_to_all(y.reshape(dests, rows, WIDE), ("inner", "head"), 0, 0, tiled=True)
    return pl.pallas_call(
        norm_body,
        grid=(dests // step,),
        in_specs=[
            pl.BlockSpec((step, rows, WIDE), lambda i: (i, 0, 0)),
            pl.BlockSpec((rows, step * WIDE), lambda i: (0, i)),
            pl.BlockSpec((1, step * WIDE), lambda i: (0, i)),
        ],
        out_specs=pl.BlockSpec((rows, step * WIDE), lambda i: (0, i)),
        out_shape=jax.ShapeDtypeStruct((rows, dests * WIDE), BF16),
        compiler_params=params(),
        name="norm",
    )(home, z_in, norm_gain.reshape(1, -1))


def solution(mesh):
    ctx, head = mesh.devices.shape
    inner = max(1, GROUPS * 16 // (OWN * head))
    cut = Mesh(mesh.devices.reshape(ctx // inner, inner, head), ("outer", "inner", "head"))
    rows = P(("outer", "inner", "head"), None)
    return jax.shard_map(
        shards,
        mesh=cut,
        in_specs=(rows,) * 5 + (P(),) * 6,
        out_specs=rows,
        check_vma=False,
    )
```

```python
import jax
import jax.numpy as jnp
from jax import lax
from jax.experimental import pallas as pl
from jax.experimental.pallas import tpu as pltpu
from jax.sharding import Mesh
from jax.sharding import PartitionSpec as P

HEAD_DIM = 64
STATE = 128
GROUPS = 8
BLOCK = 128
OWN = 8
WIDE = OWN * HEAD_DIM
LANES = 128
TILES = WIDE // LANES
TOP = 8

eps_norm = 1e-05
F32 = jnp.float32
BF16 = jnp.bfloat16
IN_VMEM = pl.BlockSpec(memory_space=pltpu.VMEM)
IN_SMEM = pl.BlockSpec(memory_space=pltpu.SMEM)


def dot(a, b):
    return jnp.dot(a, b, preferred_element_type=F32)


def dot_t(a, b):
    return lax.dot_general(a, b, (((0,), (0,)), ((), ())), preferred_element_type=F32)


def iota(shape, axis):
    return lax.broadcasted_iota(jnp.int32, shape, axis)


def parts_of(values, count):
    out = []
    for k in range(count):
        piece = values.astype(BF16).astype(F32)
        out.append(piece)
        if k + 1 < count:
            values = values - piece
    return out


def stacked(values, count):
    return jnp.concatenate(parts_of(values, count), 0).astype(BF16)


def one_hot(rows, width):
    shape = (rows, OWN * width)
    return (iota(shape, 0) % OWN == iota(shape, 1) // width).astype(F32).astype(BF16)


def expand(values):
    return dot_t(stacked(values, 2), one_hot(2 * OWN, HEAD_DIM))


def silu(v):
    return v * jax.nn.sigmoid(v)


def conv(window, tap):
    total = tap[0:1] * window(0)
    for k in range(1, tap.shape[0]):
        total = total + tap[k : k + 1] * window(k)
    return silu(total)


def tap_tiles(mine, share, tap_x, tap_b, tap_c):
    at_x = pl.multiple_of(mine * WIDE, WIDE)
    at_s = pl.multiple_of(mine // share * STATE, STATE)
    return [tap_x[:, pl.ds(at_x + q * LANES, LANES)] for q in range(TILES)] + [
        tap_b[:, pl.ds(at_s, STATE)],
        tap_c[:, pl.ds(at_s, STATE)],
    ]


def pack_body(mine_ref, x_hbm, b_hbm, c_hbm, dt_hbm, out_hbm, x_v, b_v, c_v, dt_v, turn, out_v, sem_in, sem_out):
    count, total, _ = out_v.shape
    rows = x_v.shape[0]
    share = count * STATE // b_v.shape[1]
    cuts = 4
    step = count // cuts
    wide = step * WIDE
    small = [
        pltpu.make_async_copy(src, dst, sem_in.at[k])
        for k, (src, dst) in enumerate(((dt_hbm, dt_v), (b_hbm, b_v), (c_hbm, c_v)))
    ]
    large = [
        pltpu.make_async_copy(x_hbm.at[:, pl.ds(i * wide, wide)], x_v.at[:, pl.ds(i * wide, wide)], sem_in.at[3 + i])
        for i in range(cuts)
    ]
    for copy in small + large:
        copy.start()
    small[0].wait()
    turn[...] = jnp.zeros_like(turn)
    at = pl.multiple_of(lax.rem(mine_ref[0], BLOCK // rows) * rows, rows)
    turn[pl.ds(at, rows), :] = dt_v[...].astype(F32)
    heads = turn[...].T
    for k in range(count):
        out_v[k, (TILES + 2) * rows :, :] = heads[k * OWN : (k + 1) * OWN].astype(BF16)
    small[1].wait()
    small[2].wait()
    for k in range(count):
        g = k // share
        out_v[k, TILES * rows : (TILES + 1) * rows, :] = b_v[:, g * STATE : (g + 1) * STATE]
        out_v[k, (TILES + 1) * rows : (TILES + 2) * rows, :] = c_v[:, g * STATE : (g + 1) * STATE]
    out = []
    for i in range(cuts):
        large[i].wait()
        for k in range(i * step, (i + 1) * step):
            for q in range(TILES):
                lo = k * WIDE + q * LANES
                out_v[k, q * rows : (q + 1) * rows, :] = x_v[:, lo : lo + LANES]
        copy = pltpu.make_async_copy(out_v.at[pl.ds(i * step, step)], out_hbm.at[pl.ds(i * step, step)], sem_out.at[i])
        copy.start()
        out.append(copy)
    for copy in out:
        copy.wait()


def gate_body(z_ref, out_ref):
    for lo in range(0, z_ref.shape[1], WIDE):
        out_ref[:, lo : lo + WIDE] = silu(z_ref[:, lo : lo + WIDE].astype(F32))


def states_body(
    share, mine_ref, got_ref, halo_ref, tap_x, tap_b, tap_c, bias_ref, log_ref,
    xb_ref, dt_ref, cum_ref, s_ref, send_ref, fade_ref, win,
):
    mine = mine_ref[0]
    sources, total, _ = got_ref.shape
    rows = (total - OWN) // (TILES + 2)
    blocks = sources * rows // BLOCK
    per = BLOCK // rows

    own = iota((OWN, LANES), 0) + mine * OWN == iota((OWN, LANES), 1)
    bias = jnp.sum(jnp.where(own, bias_ref[...], 0.0), axis=1, keepdims=True)
    rate = -jnp.exp(jnp.sum(jnp.where(own, log_ref[...], 0.0), axis=1, keepdims=True))
    upto = (iota((BLOCK, BLOCK), 0) <= iota((BLOCK, BLOCK), 1)).astype(F32).astype(BF16)
    for j in range(blocks):
        raw = got_ref[j * per, (TILES + 2) * rows :, :].astype(F32)
        for s in range(1, per):
            raw = raw + got_ref[j * per + s, (TILES + 2) * rows :, :].astype(F32)
        raw = raw + bias
        dt = jnp.maximum(raw, 0.0) + jnp.log1p(jnp.exp(-jnp.abs(raw)))
        sums = dot(stacked(dt * rate, 4), upto)
        cum = sums[:OWN] + sums[OWN : 2 * OWN] + sums[2 * OWN : 3 * OWN]
        dt_ref[j] = dt
        cum_ref[j] = cum

    taps = tap_tiles(mine, share, tap_x, tap_b, tap_c)
    first = TOP - taps[0].shape[0] + 1
    for q in range(TILES + 1):
        win[q, :TOP] = halo_ref[:, q * LANES : (q + 1) * LANES]
        for s in range(sources):
            at = TOP + s * rows
            win[q, at : at + rows] = got_ref[s, q * rows : (q + 1) * rows, :].astype(F32)
    state = None
    for j in range(blocks):
        at = j * BLOCK
        for q in range(TILES + 1):
            done = conv(lambda k: win[q, at + first + k : at + first + k + BLOCK], taps[q])
            xb_ref[at : at + BLOCK, q * LANES : (q + 1) * LANES] = done.astype(BF16)
        cum = cum_ref[j]
        last = cum[:, BLOCK - 1 :]
        tail = expand(jnp.exp(last - cum) * dt_ref[j])
        fade = expand(jnp.broadcast_to(jnp.exp(last), (OWN, LANES)))[:1]
        b = xb_ref[at : at + BLOCK, WIDE:]
        weighted = xb_ref[at : at + BLOCK, :WIDE].astype(F32) * tail
        twice = jnp.concatenate([b, b], 0)
        if j == 0:
            top = iota((BLOCK, WIDE), 0) < TOP
            head = dot_t(twice, stacked(jnp.where(top, weighted, 0.0), 2))
            weighted = jnp.where(top, 0.0, weighted)
        fresh = dot_t(twice, stacked(weighted, 2))
        s_ref[j] = fresh
        state = fresh + head if j == 0 else fade * state + fresh
        whole = fade if j == 0 else whole * fade
    send_ref[:STATE] = state.astype(BF16)
    ends = [got_ref[sources - 1, q * rows : (q + 1) * rows, :].astype(F32)[rows - TOP :] for q in range(TILES + 2)]
    ends += [jnp.zeros_like(ends[0])] * (TILES - 2)
    send_ref[STATE:] = jnp.concatenate(
        [jnp.concatenate(ends[:TILES], 1), jnp.concatenate(ends[TILES:], 1)], 0
    ).astype(BF16)
    fade_ref[...] = jnp.broadcast_to(whole, (8, WIDE))


def intra_body(
    share, mine_ref, got_ref, halo_ref, tap_x, tap_b, tap_c, xb_ref, dt_ref, cum_ref,
    c_ref, part_ref, win, turn,
):
    sources, total, _ = got_ref.shape
    rows = (total - OWN) // (TILES + 2)
    blocks = sources * rows // BLOCK
    tap = tap_tiles(mine_ref[0], share, tap_x, tap_b, tap_c)[-1]
    first = TOP - tap.shape[0] + 1
    q = TILES + 1
    win[:TOP] = halo_ref[:, q * LANES : (q + 1) * LANES]
    for s in range(sources):
        at = TOP + s * rows
        win[at : at + rows] = got_ref[s, q * rows : (q + 1) * rows, :].astype(F32)
    turn[...] = jnp.zeros_like(turn)
    for j in range(blocks):
        turn[j * OWN : (j + 1) * OWN] = cum_ref[j]
    cols = turn[...].T
    t_at = iota((BLOCK, BLOCK), 0)
    s_at = iota((BLOCK, BLOCK), 1)
    left = iota((BLOCK, LANES), 1) < HEAD_DIM
    zero = jnp.zeros((BLOCK, LANES), BF16)
    for j in range(blocks):
        at = j * BLOCK
        c = conv(lambda k: win[at + first + k : at + first + k + BLOCK], tap).astype(BF16)
        c_ref[at : at + BLOCK] = c
        b = xb_ref[at : at + BLOCK, WIDE:]
        scores = lax.dot_general(c, b, (((1,), (1,)), ((), ())), preferred_element_type=F32)
        keep = t_at >= s_at
        if j == 0:
            keep = keep & (s_at >= TOP)
        scores = jnp.where(keep, scores, 0.0)
        cum = cum_ref[j]
        dt = dt_ref[j]
        for q in range(TILES):
            x = xb_ref[at : at + BLOCK, q * LANES : (q + 1) * LANES]
            mixes = []
            for h in (2 * q, 2 * q + 1):
                col = j * OWN + h
                gap = jnp.minimum(cols[:, col : col + 1] - cum[h : h + 1], 0.0)
                mixes.append((scores * jnp.exp(gap) * dt[h : h + 1]).astype(BF16))
            both = jnp.concatenate([jnp.where(left, x, zero), jnp.where(left, zero, x)], 0)
            part_ref[at : at + BLOCK, q * LANES : (q + 1) * LANES] = dot(jnp.concatenate(mixes, 1), both)


def carry_body(
    share, mine_ref, got_ref, before_ref, tap_x, tap_b, tap_c, dt_ref, cum_ref, s_ref, c_ref, part_ref,
    y_ref, win, c_first,
):
    sources, total, _ = got_ref.shape
    rows = (total - OWN) // (TILES + 2)
    blocks = sources * rows // BLOCK
    taps = tap_tiles(mine_ref[0], share, tap_x, tap_b, tap_c)
    first = TOP - taps[0].shape[0] + 1

    halo = before_ref[STATE:].astype(F32)
    tops = []
    for q in range(TILES + 2):
        if q < TILES:
            win[q, :TOP] = halo[:TOP, q * LANES : (q + 1) * LANES]
        else:
            win[q, :TOP] = halo[TOP:, (q - TILES) * LANES : (q - TILES + 1) * LANES]
        win[q, TOP:] = got_ref[0, q * rows : (q + 1) * rows, :].astype(F32)[:TOP]
        done = conv(lambda k: win[q, first + k : first + k + TOP], taps[q])
        tops.append(done.astype(BF16).astype(F32))
    x_top = jnp.concatenate(tops[:TILES], 1)
    b_top = tops[TILES]
    c_first[...] = c_ref[:BLOCK].astype(F32)
    c_first[:TOP] = tops[TILES + 1]
    c = c_first[...].astype(BF16)
    wide = OWN * TOP
    scores = lax.dot_general(
        c, jnp.concatenate([b_top] * OWN, 0).astype(BF16), (((1,), (1,)), ((), ())), preferred_element_type=F32
    )
    cum = cum_ref[0]
    dt = dt_ref[0]
    spread = one_hot(4 * OWN, TOP)
    cum_t = dot_t(stacked(cum, 4), spread)
    same = iota((TOP, wide), 0) == iota((TOP, wide), 1) % TOP
    cum_s = jnp.sum(jnp.where(same, cum_t[:TOP], 0.0), axis=0, keepdims=True)
    dt_s = jnp.sum(jnp.where(same, dot_t(stacked(dt, 4), spread)[:TOP], 0.0), axis=0, keepdims=True)
    mix = scores * jnp.exp(jnp.minimum(cum_t - cum_s, 0.0)) * dt_s
    mix = jnp.where(iota((BLOCK, wide), 0) >= iota((BLOCK, wide), 1) % TOP, mix, 0.0).astype(BF16)
    shape = (wide, WIDE)
    own = iota(shape, 0) // TOP == iota(shape, 1) // HEAD_DIM
    added = dot(mix, jnp.where(own, jnp.concatenate([x_top] * OWN, 0), 0.0).astype(BF16))
    tail = expand(jnp.exp(cum[:, BLOCK - 1 :] - cum) * dt)[:TOP]
    b_twice = jnp.concatenate([b_top, b_top], 0).astype(BF16)
    head = dot_t(b_twice, stacked(x_top * tail, 2))

    state = before_ref[:STATE].astype(F32)
    for j in range(blocks):
        at = j * BLOCK
        grown = expand(jnp.exp(cum_ref[j]))
        if j > 0:
            c = c_ref[at : at + BLOCK]
        carried = dot(jnp.concatenate([c, c], 1), stacked(state, 2))
        part = part_ref[at : at + BLOCK]
        if j == 0:
            part = part + added
        y_ref[at : at + BLOCK] = (part + carried * grown).astype(BF16)
        if j + 1 < blocks:
            state = grown[BLOCK - 1 :] * state + s_ref[j]
            if j == 0:
                state = state + head


def norm_body(y_ref, gate_ref, gain_ref, out_ref):
    count = y_ref.shape[0]
    per = count // GROUPS
    for g in range(GROUPS):
        gated = []
        square = 0.0
        for k in range(g * per, (g + 1) * per):
            v = y_ref[k].astype(F32) * gate_ref[:, k * WIDE : (k + 1) * WIDE]
            gated.append(v)
            square = square + jnp.sum(v * v, axis=1, keepdims=True)
        scale = lax.rsqrt(square / (per * WIDE) + eps_norm)
        for k in range(g * per, (g + 1) * per):
            at = k * WIDE
            gain = gain_ref[:, at : at + WIDE]
            out_ref[:, at : at + WIDE] = (gated[k - g * per] * scale * gain).astype(BF16)


def shift(block, axis, distance):
    size = lax.axis_size(axis)
    return lax.ppermute(block, axis, [(i, i + distance) for i in range(size - distance)])


def kernel(body, name, ins, outs, scratch=(), cost=None, out_specs=None):
    return pl.pallas_call(
        body,
        in_specs=ins,
        out_specs=out_specs or [IN_VMEM] * len(outs),
        out_shape=outs,
        scratch_shapes=list(scratch),
        compiler_params=pltpu.CompilerParams(vmem_limit_bytes=40 * 2**20),
        cost_estimate=cost,
        name=name,
    )


def shards(x_in, b_in, c_in, dt_in, z_in, conv_x, input_state_taps, conv_c, dt_bias, a_log, norm_gain):
    outer, inner, head = (lax.axis_size(a) for a in ("outer", "inner", "head"))
    dests = inner * head
    rows = x_in.shape[0]
    tokens = rows * dests
    blocks = tokens // BLOCK
    mine = (lax.axis_index("inner") * head + lax.axis_index("head")).astype(jnp.int32).reshape(1)
    share = dests * STATE // b_in.shape[1]

    def of(dtype, *shape):
        return jax.ShapeDtypeStruct(shape, dtype)

    def bind(body):
        def bound(*refs):
            return body(share, *refs)

        return bound

    total = (TILES + 2) * rows + OWN
    hbm = pl.BlockSpec(memory_space=pltpu.HBM)
    [sent] = kernel(
        pack_body, "pack", [IN_SMEM] + [hbm] * 4, [of(BF16, dests, total, LANES)],
        [
            pltpu.VMEM(x_in.shape, BF16), pltpu.VMEM(b_in.shape, BF16), pltpu.VMEM(c_in.shape, BF16),
            pltpu.VMEM(dt_in.shape, BF16), pltpu.VMEM((BLOCK, LANES), F32), pltpu.VMEM((dests, total, LANES), BF16),
            pltpu.SemaphoreType.DMA((7,)), pltpu.SemaphoreType.DMA((4,)),
        ],
        out_specs=[hbm],
    )(mine, x_in, b_in, c_in, dt_in)
    got = lax.all_to_all(sent, ("inner", "head"), 0, 0, tiled=True)
    [gate] = kernel(
        gate_body, "gate", [IN_VMEM], [of(F32, *z_in.shape)],
        cost=pl.CostEstimate(flops=5 * z_in.size, bytes_accessed=6 * z_in.size, transcendentals=z_in.size),
    )(z_in)

    if outer > 2:
        ends = got[-1, : (TILES + 2) * rows].reshape(TILES + 2, rows, LANES)[:, -TOP:]
        halo = shift(ends, "outer", 1).transpose(1, 0, 2).reshape(TOP, -1).astype(F32)
    else:
        halo = jnp.zeros((TOP, (TILES + 2) * LANES), F32)
    taps = (conv_x, input_state_taps, conv_c)

    extra = STATE + 2 * TOP
    xb, dt, cum, fresh, send, fade = kernel(
        bind(states_body), "states", [IN_SMEM] + [IN_VMEM] * 7,
        [
            of(BF16, tokens, WIDE + STATE), of(F32, blocks, OWN, BLOCK), of(F32, blocks, OWN, BLOCK),
            of(F32, blocks, STATE, WIDE), of(BF16, extra, WIDE), of(F32, 8, WIDE),
        ],
        [pltpu.VMEM((TILES + 1, TOP + tokens, LANES), F32)],
    )(mine, got, halo, *taps, dt_bias.reshape(1, -1), a_log.reshape(1, -1))

    before = shift(send, "outer", 1)
    if outer > 2:
        entering, held, reach = before[:STATE].astype(F32), shift(fade, "outer", 1), 1
        while reach < outer - 1:
            entering = entering + held[:1] * shift(entering, "outer", reach)
            held = held * shift(held, "outer", reach)
            reach *= 2
        before = jnp.concatenate([entering.astype(BF16), before[STATE:]], 0)

    c, part = kernel(
        bind(intra_body), "intra", [IN_SMEM] + [IN_VMEM] * 8,
        [of(BF16, tokens, STATE), of(F32, tokens, WIDE)],
        [pltpu.VMEM((TOP + tokens, LANES), F32), pltpu.VMEM((BLOCK, LANES), F32)],
        pl.CostEstimate(
            flops=2 * blocks * OWN * BLOCK * BLOCK * 160,
            bytes_accessed=tokens * WIDE * 8,
            transcendentals=blocks * OWN * BLOCK * BLOCK,
        ),
    )(mine, got, halo, *taps, xb, dt, cum)

    [y] = kernel(
        bind(carry_body), "carry", [IN_SMEM] + [IN_VMEM] * 10, [of(BF16, tokens, WIDE)],
        [pltpu.VMEM((TILES + 2, 2 * TOP, LANES), F32), pltpu.VMEM((BLOCK, STATE), F32)],
    )(mine, got, before, *taps, dt, cum, fresh, c, part)

    home = lax.all_to_all(y.reshape(dests, rows, WIDE), ("inner", "head"), 0, 0, tiled=True)
    [out] = kernel(
        norm_body, "norm", [IN_VMEM] * 3, [of(BF16, rows, dests * WIDE)],
    )(home, gate, norm_gain.reshape(1, -1))
    return out


def solution(mesh):
    ctx, head = mesh.devices.shape
    inner = max(1, GROUPS * 16 // (OWN * head))
    cut = Mesh(mesh.devices.reshape(ctx // inner, inner, head), ("outer", "inner", "head"))
    rows = P(("outer", "inner", "head"), None)
    return jax.shard_map(
        shards,
        mesh=cut,
        in_specs=(rows,) * 5 + (P(),) * 6,
        out_specs=rows,
        check_vma=False,
    )
```

```python
import jax
import jax.numpy as jnp
from jax import lax
from jax.experimental import pallas as pl
from jax.experimental.pallas import tpu as pltpu
from jax.sharding import Mesh
from jax.sharding import PartitionSpec as P

HEAD_DIM = 64
STATE = 128
GROUPS = 8
BLOCK = 128
OWN = 8
WIDE = OWN * HEAD_DIM
LANES = 128
TILES = WIDE // LANES
TOP = 8

eps_norm = 1e-05
F32 = jnp.float32
BF16 = jnp.bfloat16
IN_VMEM = pl.BlockSpec(memory_space=pltpu.VMEM)
IN_SMEM = pl.BlockSpec(memory_space=pltpu.SMEM)


def dot(a, b):
    return jnp.dot(a, b, preferred_element_type=F32)


def dot_t(a, b):
    return lax.dot_general(a, b, (((0,), (0,)), ((), ())), preferred_element_type=F32)


def iota(shape, axis):
    return lax.broadcasted_iota(jnp.int32, shape, axis)


def parts_of(values, count):
    out = []
    for k in range(count):
        piece = values.astype(BF16).astype(F32)
        out.append(piece)
        if k + 1 < count:
            values = values - piece
    return out


def stacked(values, count):
    return jnp.concatenate(parts_of(values, count), 0).astype(BF16)


def one_hot(rows, width):
    shape = (rows, OWN * width)
    return (iota(shape, 0) % OWN == iota(shape, 1) // width).astype(F32).astype(BF16)


def expand(values):
    return dot_t(stacked(values, 2), one_hot(2 * OWN, HEAD_DIM))


def silu(v):
    return v * jax.nn.sigmoid(v)


def conv(window, tap):
    total = tap[0:1] * window(0)
    for k in range(1, tap.shape[0]):
        total = total + tap[k : k + 1] * window(k)
    return silu(total)


def tiles_of(own_ref):
    return [own_ref[:lead_of(own_ref), q * LANES : (q + 1) * LANES] for q in range(TILES + 2)]


def lead_of(own_ref):
    return own_ref.shape[0] - 2 * OWN


def pack_body(
    mine_ref, x_hbm, b_hbm, c_hbm, dt_hbm, tap_x, tap_b, tap_c, bias_hbm, log_hbm,
    out_v, own_ref, x_v, b_v, c_v, dt_v, turn, x_tap, s_taps, heads_v, sem_in, sem_own,
):
    mine = mine_ref[0]
    count = out_v.shape[0]
    rows = x_v.shape[0]
    share = count * STATE // b_v.shape[1]
    cuts = 4
    step = count // cuts
    wide = step * WIDE
    small = [
        pltpu.make_async_copy(src, dst, sem_in.at[k])
        for k, (src, dst) in enumerate(((dt_hbm, dt_v), (b_hbm, b_v), (c_hbm, c_v)))
    ]
    large = [
        pltpu.make_async_copy(x_hbm.at[:, pl.ds(i * wide, wide)], x_v.at[:, pl.ds(i * wide, wide)], sem_in.at[3 + i])
        for i in range(cuts)
    ]
    at_x = pl.multiple_of(mine * WIDE, WIDE)
    at_s = pl.multiple_of(mine // share * STATE, STATE)
    own = [
        pltpu.make_async_copy(src, dst, sem_own.at[k])
        for k, (src, dst) in enumerate((
            (tap_x.at[:, pl.ds(at_x, WIDE)], x_tap),
            (tap_b.at[:, pl.ds(at_s, STATE)], s_taps.at[0]),
            (tap_c.at[:, pl.ds(at_s, STATE)], s_taps.at[1]),
            (bias_hbm, heads_v.at[0]),
            (log_hbm, heads_v.at[1]),
        ))
    ]
    for copy in small + large + own:
        copy.start()
    small[0].wait()
    turn[...] = jnp.zeros_like(turn)
    at = pl.multiple_of(lax.rem(mine, BLOCK // rows) * rows, rows)
    turn[pl.ds(at, rows), :] = dt_v[...].astype(F32)
    heads = turn[...].T
    for k in range(count):
        out_v[k, (TILES + 2) * rows :, :] = heads[k * OWN : (k + 1) * OWN].astype(BF16)
    small[1].wait()
    small[2].wait()
    for k in range(count):
        g = k // share
        out_v[k, TILES * rows : (TILES + 1) * rows, :] = b_v[:, g * STATE : (g + 1) * STATE]
        out_v[k, (TILES + 1) * rows : (TILES + 2) * rows, :] = c_v[:, g * STATE : (g + 1) * STATE]
    for i in range(cuts):
        large[i].wait()
        for k in range(i * step, (i + 1) * step):
            for q in range(TILES):
                lo = k * WIDE + q * LANES
                out_v[k, q * rows : (q + 1) * rows, :] = x_v[:, lo : lo + LANES]
    for copy in own:
        copy.wait()
    taps = x_tap.shape[0]
    own_ref[:taps, :WIDE] = x_tap[...]
    own_ref[:taps, WIDE : WIDE + STATE] = s_taps[0]
    own_ref[:taps, WIDE + STATE :] = s_taps[1]
    mask = iota((OWN, LANES), 0) + mine * OWN == iota((OWN, LANES), 1)
    for k in range(2):
        column = jnp.sum(jnp.where(mask, heads_v[k], 0.0), axis=1, keepdims=True)
        at = taps + k * OWN
        own_ref[at : at + OWN, :LANES] = jnp.broadcast_to(column, (OWN, LANES))


def gate_body(z_ref, out_ref):
    for lo in range(0, z_ref.shape[1], WIDE):
        out_ref[:, lo : lo + WIDE] = silu(z_ref[:, lo : lo + WIDE].astype(F32))


def states_body(
    got_ref, halo_ref, own_ref, xb_ref, dt_ref, cum_ref, s_ref, send_ref, fade_ref, win,
):
    sources, total, _ = got_ref.shape
    rows = (total - OWN) // (TILES + 2)
    blocks = sources * rows // BLOCK
    per = BLOCK // rows

    lead = lead_of(own_ref)
    bias = own_ref[lead : lead + OWN, :LANES]
    rate = -jnp.exp(own_ref[lead + OWN :, :LANES])
    upto = (iota((BLOCK, BLOCK), 0) <= iota((BLOCK, BLOCK), 1)).astype(F32).astype(BF16)
    for j in range(blocks):
        raw = got_ref[j * per, (TILES + 2) * rows :, :].astype(F32)
        for s in range(1, per):
            raw = raw + got_ref[j * per + s, (TILES + 2) * rows :, :].astype(F32)
        raw = raw + bias
        dt = jnp.maximum(raw, 0.0) + jnp.log1p(jnp.exp(-jnp.abs(raw)))
        sums = dot(stacked(dt * rate, 4), upto)
        cum = sums[:OWN] + sums[OWN : 2 * OWN] + sums[2 * OWN : 3 * OWN]
        dt_ref[j] = dt
        cum_ref[j] = cum

    taps = tiles_of(own_ref)
    first = TOP - lead + 1
    for q in range(TILES + 1):
        win[q, :TOP] = halo_ref[:, q * LANES : (q + 1) * LANES]
        for s in range(sources):
            at = TOP + s * rows
            win[q, at : at + rows] = got_ref[s, q * rows : (q + 1) * rows, :].astype(F32)
    state = None
    for j in range(blocks):
        at = j * BLOCK
        for q in range(TILES + 1):
            done = conv(lambda k: win[q, at + first + k : at + first + k + BLOCK], taps[q])
            xb_ref[at : at + BLOCK, q * LANES : (q + 1) * LANES] = done.astype(BF16)
        cum = cum_ref[j]
        last = cum[:, BLOCK - 1 :]
        tail = expand(jnp.exp(last - cum) * dt_ref[j])
        fade = expand(jnp.broadcast_to(jnp.exp(last), (OWN, LANES)))[:1]
        b = xb_ref[at : at + BLOCK, WIDE:]
        weighted = xb_ref[at : at + BLOCK, :WIDE].astype(F32) * tail
        twice = jnp.concatenate([b, b], 0)
        if j == 0:
            top = iota((BLOCK, WIDE), 0) < TOP
            head = dot_t(twice, stacked(jnp.where(top, weighted, 0.0), 2))
            weighted = jnp.where(top, 0.0, weighted)
        fresh = dot_t(twice, stacked(weighted, 2))
        s_ref[j] = fresh
        state = fresh + head if j == 0 else fade * state + fresh
        whole = fade if j == 0 else whole * fade
    send_ref[:STATE] = state.astype(BF16)
    ends = [got_ref[sources - 1, q * rows : (q + 1) * rows, :].astype(F32)[rows - TOP :] for q in range(TILES + 2)]
    ends += [jnp.zeros_like(ends[0])] * (TILES - 2)
    half = TOP // 2
    upper = pltpu.roll(jnp.concatenate(ends[:TILES], 1), half, 0)
    keep = iota((TOP, WIDE), 0) < half
    send_ref[STATE:] = jnp.where(keep, upper, jnp.concatenate(ends[TILES:], 1)).astype(BF16)
    fade_ref[...] = jnp.broadcast_to(whole, (8, WIDE))


def intra_body(
    got_ref, halo_ref, own_ref, xb_ref, dt_ref, cum_ref, s_ref,
    c_ref, part_ref, grown_ref, factor_ref, tail_ref, win, turn,
):
    sources, total, _ = got_ref.shape
    rows = (total - OWN) // (TILES + 2)
    blocks = sources * rows // BLOCK
    tap = tiles_of(own_ref)[-1]
    first = TOP - tap.shape[0] + 1
    q = TILES + 1
    win[:TOP] = halo_ref[:, q * LANES : (q + 1) * LANES]
    for s in range(sources):
        at = TOP + s * rows
        win[at : at + rows] = got_ref[s, q * rows : (q + 1) * rows, :].astype(F32)
    turn[...] = jnp.zeros_like(turn)
    for j in range(blocks):
        turn[j * OWN : (j + 1) * OWN] = cum_ref[j]
    cols = turn[...].T
    t_at = iota((BLOCK, BLOCK), 0)
    s_at = iota((BLOCK, BLOCK), 1)
    left = iota((BLOCK, LANES), 1) < HEAD_DIM
    zero = jnp.zeros((BLOCK, LANES), BF16)
    past = jnp.zeros((OWN, 1), F32)
    for j in range(blocks):
        at = j * BLOCK
        c = conv(lambda k: win[at + first + k : at + first + k + BLOCK], tap).astype(BF16)
        c_ref[at : at + BLOCK] = c
        b = xb_ref[at : at + BLOCK, WIDE:]
        scores = lax.dot_general(c, b, (((1,), (1,)), ((), ())), preferred_element_type=F32)
        keep = t_at >= s_at
        if j == 0:
            keep = keep & (s_at >= TOP)
        scores = jnp.where(keep, scores, 0.0)
        cum = cum_ref[j]
        dt = dt_ref[j]
        grown = expand(jnp.exp(cum))
        if j < 2:
            grown_ref[at : at + BLOCK] = grown
        else:
            past = past + cum_ref[j - 1][:, BLOCK - 1 :]
            grown_ref[at : at + BLOCK] = expand(jnp.exp(cum + past))
        if j > 0:
            local = s_ref[0] if j == 1 else fade * local + s_ref[j - 1]
            carried = dot(jnp.concatenate([c, c], 1), stacked(local, 2)) * grown
        fade = grown[BLOCK - 1 :]
        for q in range(TILES):
            lo = q * LANES
            x = xb_ref[at : at + BLOCK, lo : lo + LANES]
            mixes = []
            for h in (2 * q, 2 * q + 1):
                col = j * OWN + h
                gap = jnp.minimum(cols[:, col : col + 1] - cum[h : h + 1], 0.0)
                mixes.append((scores * jnp.exp(gap) * dt[h : h + 1]).astype(BF16))
            both = jnp.concatenate([jnp.where(left, x, zero), jnp.where(left, zero, x)], 0)
            part = dot(jnp.concatenate(mixes, 1), both)
            part_ref[at : at + BLOCK, lo : lo + LANES] = part if j == 0 else part + carried[:, lo : lo + LANES]

    cum = cum_ref[0]
    dt = dt_ref[0]
    wide = OWN * TOP
    spread = one_hot(4 * OWN, TOP)
    cum_t = dot_t(stacked(cum, 4), spread)
    same = iota((TOP, wide), 0) == iota((TOP, wide), 1) % TOP
    cum_s = jnp.sum(jnp.where(same, cum_t[:TOP], 0.0), axis=0, keepdims=True)
    dt_s = jnp.sum(jnp.where(same, dot_t(stacked(dt, 4), spread)[:TOP], 0.0), axis=0, keepdims=True)
    decay = jnp.exp(jnp.minimum(cum_t - cum_s, 0.0))
    seen = iota((BLOCK, wide), 0) >= iota((BLOCK, wide), 1) % TOP
    factor_ref[0] = jnp.where(seen, decay, 0.0)
    factor_ref[1] = jnp.broadcast_to(dt_s, (BLOCK, wide))
    tail_ref[...] = expand(jnp.exp(cum[:, BLOCK - 1 :] - cum) * dt)[:TOP]


def carry_body(got_ref, before_ref, own_ref, c_ref, part_ref, grown_ref, factor_ref, tail_ref, y_ref, win, c_first):
    sources, total, _ = got_ref.shape
    rows = (total - OWN) // (TILES + 2)
    blocks = sources * rows // BLOCK
    taps = tiles_of(own_ref)
    first = TOP - taps[0].shape[0] + 1

    halo = before_ref[STATE:].astype(F32)
    upper = pltpu.roll(halo, TOP // 2, 0)
    tops = []
    for q in range(TILES + 2):
        lo = q * LANES
        win[q, :TOP] = upper[:, lo : lo + LANES] if q < TILES else halo[:, lo - WIDE : lo - WIDE + LANES]
        win[q, TOP:] = got_ref[0, q * rows : (q + 1) * rows, :].astype(F32)[:TOP]
        done = conv(lambda k: win[q, first + k : first + k + TOP], taps[q])
        tops.append(done.astype(BF16).astype(F32))
    x_top = jnp.concatenate(tops[:TILES], 1)
    b_top = tops[TILES]
    b_twice = jnp.concatenate([b_top, b_top], 0).astype(BF16)
    head = dot_t(b_twice, stacked(x_top * tail_ref[...], 2))
    state = before_ref[:STATE]
    later = stacked(grown_ref[BLOCK - 1 : BLOCK] * state.astype(F32) + head, 2)

    c_first[...] = c_ref[:BLOCK].astype(F32)
    c_first[:TOP] = tops[TILES + 1]
    c = c_first[...].astype(BF16)
    wide = OWN * TOP
    scores = lax.dot_general(
        c, jnp.concatenate([b_top] * OWN, 0).astype(BF16), (((1,), (1,)), ((), ())), preferred_element_type=F32
    )
    mix = (scores * factor_ref[0] * factor_ref[1]).astype(BF16)
    shape = (wide, WIDE)
    own = iota(shape, 0) // TOP == iota(shape, 1) // HEAD_DIM
    added = dot(mix, jnp.where(own, jnp.concatenate([x_top] * OWN, 0), 0.0).astype(BF16))
    y_ref[:BLOCK] = (part_ref[:BLOCK] + added + dot(c, state) * grown_ref[:BLOCK]).astype(BF16)
    for j in range(1, blocks):
        at = j * BLOCK
        c = c_ref[at : at + BLOCK]
        carried = dot(jnp.concatenate([c, c], 1), later)
        y_ref[at : at + BLOCK] = (part_ref[at : at + BLOCK] + carried * grown_ref[at : at + BLOCK]).astype(BF16)


def norm_body(y_ref, gate_ref, gain_ref, out_ref):
    count = y_ref.shape[0]
    per = count // GROUPS
    for g in range(GROUPS):
        gated = []
        square = 0.0
        for k in range(g * per, (g + 1) * per):
            v = y_ref[k].astype(F32) * gate_ref[:, k * WIDE : (k + 1) * WIDE]
            gated.append(v)
            square = square + jnp.sum(v * v, axis=1, keepdims=True)
        scale = lax.rsqrt(square / (per * WIDE) + eps_norm)
        for k in range(g * per, (g + 1) * per):
            at = k * WIDE
            gain = gain_ref[:, at : at + WIDE]
            out_ref[:, at : at + WIDE] = (gated[k - g * per] * scale * gain).astype(BF16)


def shift(block, axis, distance):
    size = lax.axis_size(axis)
    return lax.ppermute(block, axis, [(i, i + distance) for i in range(size - distance)])


def kernel(body, name, ins, outs, scratch=(), cost=None, out_specs=None):
    return pl.pallas_call(
        body,
        in_specs=ins,
        out_specs=out_specs or [IN_VMEM] * len(outs),
        out_shape=outs,
        scratch_shapes=list(scratch),
        compiler_params=pltpu.CompilerParams(vmem_limit_bytes=40 * 2**20),
        cost_estimate=cost,
        name=name,
    )


def shards(x_in, b_in, c_in, dt_in, z_in, conv_x, input_state_taps, conv_c, dt_bias, a_log, norm_gain):
    outer, inner, head = (lax.axis_size(a) for a in ("outer", "inner", "head"))
    dests = inner * head
    rows = x_in.shape[0]
    tokens = rows * dests
    blocks = tokens // BLOCK
    mine = (lax.axis_index("inner") * head + lax.axis_index("head")).astype(jnp.int32).reshape(1)

    def of(dtype, *shape):
        return jax.ShapeDtypeStruct(shape, dtype)

    total = (TILES + 2) * rows + OWN
    lead = conv_x.shape[0]
    hbm = pl.BlockSpec(memory_space=pltpu.HBM)
    operands = (x_in, b_in, c_in, dt_in, conv_x, input_state_taps, conv_c, dt_bias.reshape(1, -1), a_log.reshape(1, -1))
    sent, own = kernel(
        pack_body, "pack", [IN_SMEM] + [hbm] * len(operands),
        [of(BF16, dests, total, LANES), of(F32, lead + 2 * OWN, WIDE + 2 * STATE)],
        [
            pltpu.VMEM(x_in.shape, BF16), pltpu.VMEM(b_in.shape, BF16), pltpu.VMEM(c_in.shape, BF16),
            pltpu.VMEM(dt_in.shape, BF16), pltpu.VMEM((BLOCK, LANES), F32),
            pltpu.VMEM((lead, WIDE), F32), pltpu.VMEM((2, lead, STATE), F32), pltpu.VMEM((2, 1, LANES), F32),
            pltpu.SemaphoreType.DMA((7,)), pltpu.SemaphoreType.DMA((5,)),
        ],
    )(mine, *(pltpu.with_memory_space_constraint(a, pltpu.HBM) for a in operands))
    got = lax.all_to_all(sent, ("inner", "head"), 0, 0, tiled=True)
    [gate] = kernel(
        gate_body, "gate", [IN_VMEM], [of(F32, *z_in.shape)],
        cost=pl.CostEstimate(flops=5 * z_in.size, bytes_accessed=6 * z_in.size, transcendentals=z_in.size),
    )(z_in)

    if outer > 2:
        ends = got[-1, : (TILES + 2) * rows].reshape(TILES + 2, rows, LANES)[:, -TOP:]
        halo = shift(ends, "outer", 1).transpose(1, 0, 2).reshape(TOP, -1).astype(F32)
    else:
        halo = jnp.zeros((TOP, (TILES + 2) * LANES), F32)

    extra = STATE + TOP
    xb, dt, cum, fresh, send, fade = kernel(
        states_body, "states", [IN_VMEM] * 3,
        [
            of(BF16, tokens, WIDE + STATE), of(F32, blocks, OWN, BLOCK), of(F32, blocks, OWN, BLOCK),
            of(F32, blocks, STATE, WIDE), of(BF16, extra, WIDE), of(F32, 8, WIDE),
        ],
        [pltpu.VMEM((TILES + 1, TOP + tokens, LANES), F32)],
    )(got, halo, own)

    before = shift(send, "outer", 1)
    if outer > 2:
        entering, held, reach = before[:STATE].astype(F32), shift(fade, "outer", 1), 1
        while reach < outer - 1:
            entering = entering + held[:1] * shift(entering, "outer", reach)
            held = held * shift(held, "outer", reach)
            reach *= 2
        before = jnp.concatenate([entering.astype(BF16), before[STATE:]], 0)

    wide = OWN * TOP
    c, part, grown, factor, tail = kernel(
        intra_body, "intra", [IN_VMEM] * 7,
        [
            of(BF16, tokens, STATE), of(F32, tokens, WIDE), of(F32, tokens, WIDE),
            of(F32, 2, BLOCK, wide), of(F32, TOP, WIDE),
        ],
        [pltpu.VMEM((TOP + tokens, LANES), F32), pltpu.VMEM((BLOCK, LANES), F32)],
        pl.CostEstimate(
            flops=2 * blocks * OWN * BLOCK * BLOCK * 160,
            bytes_accessed=tokens * WIDE * 12,
            transcendentals=blocks * OWN * BLOCK * BLOCK,
        ),
    )(got, halo, own, xb, dt, cum, fresh)

    [y] = kernel(
        carry_body, "carry", [IN_VMEM] * 8, [of(BF16, tokens, WIDE)],
        [pltpu.VMEM((TILES + 2, 2 * TOP, LANES), F32), pltpu.VMEM((BLOCK, STATE), F32)],
    )(got, before, own, c, part, grown, factor, tail)

    home = lax.all_to_all(y.reshape(dests, rows, WIDE), ("inner", "head"), 0, 0, tiled=True)
    [out] = kernel(
        norm_body, "norm", [IN_VMEM] * 3, [of(BF16, rows, dests * WIDE)],
    )(home, gate, norm_gain.reshape(1, -1))
    return out


def solution(mesh):
    ctx, head = mesh.devices.shape
    inner = max(1, GROUPS * 16 // (OWN * head))
    cut = Mesh(mesh.devices.reshape(ctx // inner, inner, head), ("outer", "inner", "head"))
    rows = P(("outer", "inner", "head"), None)
    return jax.shard_map(
        shards,
        mesh=cut,
        in_specs=(rows,) * 5 + (P(),) * 6,
        out_specs=rows,
        check_vma=False,
    )
```

```python
import jax
import jax.numpy as jnp
from jax import lax
from jax.experimental import pallas as pl
from jax.experimental.pallas import tpu as pltpu
from jax.sharding import Mesh
from jax.sharding import PartitionSpec as P

HEAD_DIM = 64
STATE = 128
GROUPS = 8
BLOCK = 128
OWN = 8
WIDE = OWN * HEAD_DIM
LANES = 128
TILES = WIDE // LANES
TOP = 8

eps_norm = 1e-05
F32 = jnp.float32
BF16 = jnp.bfloat16
IN_VMEM = pl.BlockSpec(memory_space=pltpu.VMEM)
IN_SMEM = pl.BlockSpec(memory_space=pltpu.SMEM)


def dot(a, b):
    return jnp.dot(a, b, preferred_element_type=F32)


def dot_t(a, b):
    return lax.dot_general(a, b, (((0,), (0,)), ((), ())), preferred_element_type=F32)


def iota(shape, axis):
    return lax.broadcasted_iota(jnp.int32, shape, axis)


def parts_of(values, count):
    out = []
    for k in range(count):
        piece = values.astype(BF16).astype(F32)
        out.append(piece)
        if k + 1 < count:
            values = values - piece
    return out


def stacked(values, count):
    return jnp.concatenate(parts_of(values, count), 0).astype(BF16)


def one_hot(rows, width):
    shape = (rows, OWN * width)
    return (iota(shape, 0) % OWN == iota(shape, 1) // width).astype(F32).astype(BF16)


def expand(values):
    return dot_t(stacked(values, 2), one_hot(2 * OWN, HEAD_DIM))


def silu(v):
    return v * jax.nn.sigmoid(v)


def conv(window, tap):
    total = tap[0:1] * window(0)
    for k in range(1, tap.shape[0]):
        total = total + tap[k : k + 1] * window(k)
    return silu(total)


def tiles_of(own_ref):
    return [own_ref[:lead_of(own_ref), q * LANES : (q + 1) * LANES] for q in range(TILES + 2)]


def lead_of(own_ref):
    return own_ref.shape[0] - 2 * OWN


def pack_body(
    mine_ref, x_hbm, b_hbm, c_hbm, dt_hbm, tap_x, tap_b, tap_c, bias_hbm, log_hbm,
    out_v, own_ref, x_v, b_v, c_v, dt_v, turn, x_tap, s_taps, heads_v, sem_in, sem_own,
):
    mine = mine_ref[0]
    count = out_v.shape[0]
    rows = x_v.shape[0]
    share = count * STATE // b_v.shape[1]
    cuts = 4
    step = count // cuts
    wide = step * WIDE
    small = [
        pltpu.make_async_copy(src, dst, sem_in.at[k])
        for k, (src, dst) in enumerate(((dt_hbm, dt_v), (b_hbm, b_v), (c_hbm, c_v)))
    ]
    large = [
        pltpu.make_async_copy(x_hbm.at[:, pl.ds(i * wide, wide)], x_v.at[:, pl.ds(i * wide, wide)], sem_in.at[3 + i])
        for i in range(cuts)
    ]
    at_x = pl.multiple_of(mine * WIDE, WIDE)
    at_s = pl.multiple_of(mine // share * STATE, STATE)
    own = [
        pltpu.make_async_copy(src, dst, sem_own.at[k])
        for k, (src, dst) in enumerate((
            (tap_x.at[:, pl.ds(at_x, WIDE)], x_tap),
            (tap_b.at[:, pl.ds(at_s, STATE)], s_taps.at[0]),
            (tap_c.at[:, pl.ds(at_s, STATE)], s_taps.at[1]),
            (bias_hbm, heads_v.at[0]),
            (log_hbm, heads_v.at[1]),
        ))
    ]
    for copy in small + large + own:
        copy.start()
    small[0].wait()
    turn[...] = jnp.zeros_like(turn)
    at = pl.multiple_of(lax.rem(mine, BLOCK // rows) * rows, rows)
    turn[pl.ds(at, rows), :] = dt_v[...].astype(F32)
    heads = turn[...].T
    for k in range(count):
        out_v[k, (TILES + 2) * rows :, :] = heads[k * OWN : (k + 1) * OWN].astype(BF16)
    small[1].wait()
    small[2].wait()
    for k in range(count):
        g = k // share
        out_v[k, TILES * rows : (TILES + 1) * rows, :] = b_v[:, g * STATE : (g + 1) * STATE]
        out_v[k, (TILES + 1) * rows : (TILES + 2) * rows, :] = c_v[:, g * STATE : (g + 1) * STATE]
    for i in range(cuts):
        large[i].wait()
        for k in range(i * step, (i + 1) * step):
            for q in range(TILES):
                lo = k * WIDE + q * LANES
                out_v[k, q * rows : (q + 1) * rows, :] = x_v[:, lo : lo + LANES]
    for copy in own:
        copy.wait()
    taps = x_tap.shape[0]
    own_ref[:taps, :WIDE] = x_tap[...]
    own_ref[:taps, WIDE : WIDE + STATE] = s_taps[0]
    own_ref[:taps, WIDE + STATE :] = s_taps[1]
    mask = iota((OWN, LANES), 0) + mine * OWN == iota((OWN, LANES), 1)
    for k in range(2):
        column = jnp.sum(jnp.where(mask, heads_v[k], 0.0), axis=1, keepdims=True)
        at = taps + k * OWN
        own_ref[at : at + OWN, :LANES] = jnp.broadcast_to(column, (OWN, LANES))


def gate_body(z_ref, out_ref):
    for lo in range(0, z_ref.shape[1], WIDE):
        out_ref[:, lo : lo + WIDE] = silu(z_ref[:, lo : lo + WIDE].astype(F32))


def sizes_of(got_ref):
    sources, total, _ = got_ref.shape
    rows = (total - OWN) // (TILES + 2)
    return sources, rows, sources * rows // BLOCK


def fill(win, got_ref, halo_ref, tiles):
    sources, rows, _ = sizes_of(got_ref)
    for q in range(tiles):
        win[q, :TOP] = halo_ref[:, q * LANES : (q + 1) * LANES]
        for s in range(sources):
            at = TOP + s * rows
            win[q, at : at + rows] = got_ref[s, q * rows : (q + 1) * rows, :].astype(F32)


def conv_tile(win, taps, j, q):
    first = j * BLOCK + TOP - taps[q].shape[0] + 1
    return conv(lambda k: win[q, first + k : first + k + BLOCK], taps[q]).astype(BF16)


def steps_of(got_ref, own_ref):
    _, rows, blocks = sizes_of(got_ref)
    per = BLOCK // rows
    lead = lead_of(own_ref)
    raws = []
    for j in range(blocks):
        raw = got_ref[j * per, (TILES + 2) * rows :, :].astype(F32)
        for s in range(1, per):
            raw = raw + got_ref[j * per + s, (TILES + 2) * rows :, :].astype(F32)
        raws.append(raw + own_ref[lead : lead + OWN, :LANES])
    raw = jnp.concatenate(raws, 0)
    dt = jnp.maximum(raw, 0.0) + jnp.log1p(jnp.exp(-jnp.abs(raw)))
    rate = jnp.concatenate([-jnp.exp(own_ref[lead + OWN :, :LANES])] * blocks, 0)
    upto = (iota((BLOCK, BLOCK), 0) <= iota((BLOCK, BLOCK), 1)).astype(F32).astype(BF16)
    sums = dot(stacked(dt * rate, 4), upto)
    n = blocks * OWN
    cum = sums[:n] + sums[n : 2 * n] + sums[2 * n : 3 * n] + sums[3 * n :]
    return [[v[j * OWN : (j + 1) * OWN] for j in range(blocks)] for v in (dt, cum)]


def total_body(sends_ref, got_ref, halo_ref, own_ref, send_ref, fade_ref, win):
    @pl.when(sends_ref[0] != 0)
    def _():
        sources, rows, blocks = sizes_of(got_ref)
        dts, cums = steps_of(got_ref, own_ref)
        taps = tiles_of(own_ref)
        fill(win, got_ref, halo_ref, TILES + 1)
        state = jnp.zeros((STATE, WIDE), F32)
        after = jnp.zeros((OWN, 1), F32)
        for j in reversed(range(blocks)):
            after = after + cums[j][:, BLOCK - 1 :]
            tail = expand(jnp.exp(after - cums[j]) * dts[j])
            x = jnp.concatenate([conv_tile(win, taps, j, q) for q in range(TILES)], 1)
            b = conv_tile(win, taps, j, TILES)
            state = state + dot_t(jnp.concatenate([b, b], 0), stacked(x.astype(F32) * tail, 2))
        fade_ref[...] = expand(jnp.broadcast_to(jnp.exp(after), (OWN, LANES)))[:8]
        send_ref[:STATE] = state.astype(BF16)
        ends = [got_ref[sources - 1, q * rows : (q + 1) * rows, :].astype(F32)[rows - TOP :] for q in range(TILES + 2)]
        ends += [jnp.zeros_like(ends[0])] * (TILES - 2)
        half = TOP // 2
        upper = pltpu.roll(jnp.concatenate(ends[:TILES], 1), half, 0)
        keep = iota((TOP, WIDE), 0) < half
        send_ref[STATE:] = jnp.where(keep, upper, jnp.concatenate(ends[TILES:], 1)).astype(BF16)


def local_body(
    got_ref, halo_ref, own_ref, order_ref, c_ref, part_ref, grown_ref, factor_ref, tail_ref, win, turn,
):
    _, _, blocks = sizes_of(got_ref)
    dts, cums = steps_of(got_ref, own_ref)
    taps = tiles_of(own_ref)
    fill(win, got_ref, halo_ref, TILES + 2)
    turn[...] = jnp.zeros_like(turn)
    for j in range(blocks):
        turn[j * OWN : (j + 1) * OWN] = cums[j]
    cols = turn[...].T
    t_at = iota((BLOCK, BLOCK), 0)
    s_at = iota((BLOCK, BLOCK), 1)
    left = iota((BLOCK, LANES), 1) < HEAD_DIM
    zero = jnp.zeros((BLOCK, LANES), BF16)
    past = jnp.zeros((OWN, 1), F32)
    local = None
    for j in range(blocks):
        at = j * BLOCK
        x = [conv_tile(win, taps, j, q) for q in range(TILES)]
        b = conv_tile(win, taps, j, TILES)
        c = conv_tile(win, taps, j, TILES + 1)
        c_ref[at : at + BLOCK] = c
        scores = lax.dot_general(c, b, (((1,), (1,)), ((), ())), preferred_element_type=F32)
        keep = t_at >= s_at
        if j == 0:
            keep = keep & (s_at >= TOP)
        scores = jnp.where(keep, scores, 0.0)
        cum, dt = cums[j], dts[j]
        last = cum[:, BLOCK - 1 :]
        grown = expand(jnp.exp(cum))
        if j < 2:
            grown_ref[at : at + BLOCK] = grown
        else:
            past = past + cums[j - 1][:, BLOCK - 1 :]
            grown_ref[at : at + BLOCK] = expand(jnp.exp(cum + past))
        if j > 0:
            carried = dot(jnp.concatenate([c, c], 1), stacked(local, 2)) * grown
        for q in range(TILES):
            lo = q * LANES
            mixes = []
            for h in (2 * q, 2 * q + 1):
                col = j * OWN + h
                gap = jnp.minimum(cols[:, col : col + 1] - cum[h : h + 1], 0.0)
                mixes.append((scores * jnp.exp(gap) * dt[h : h + 1]).astype(BF16))
            both = jnp.concatenate([jnp.where(left, x[q], zero), jnp.where(left, zero, x[q])], 0)
            part = dot(jnp.concatenate(mixes, 1), both)
            part_ref[at : at + BLOCK, lo : lo + LANES] = part if j == 0 else part + carried[:, lo : lo + LANES]
        tail = expand(jnp.exp(last - cum) * dt)
        if j == 0:
            tail_ref[...] = tail[:TOP]
            tail = jnp.where(iota((BLOCK, WIDE), 0) < TOP, 0.0, tail)
        if j + 1 < blocks:
            weighted = stacked(jnp.concatenate(x, 1).astype(F32) * tail, 2)
            fresh = dot_t(jnp.concatenate([b, b], 0), weighted)
            local = fresh if j == 0 else grown[BLOCK - 1 :] * local + fresh

    wide = OWN * TOP
    spread = one_hot(4 * OWN, TOP)
    cum_t = dot_t(stacked(cums[0], 4), spread)
    same = iota((TOP, wide), 0) == iota((TOP, wide), 1) % TOP
    cum_s = jnp.sum(jnp.where(same, cum_t[:TOP], 0.0), axis=0, keepdims=True)
    dt_s = jnp.sum(jnp.where(same, dot_t(stacked(dts[0], 4), spread)[:TOP], 0.0), axis=0, keepdims=True)
    decay = jnp.exp(jnp.minimum(cum_t - cum_s, 0.0))
    seen = iota((BLOCK, wide), 0) >= iota((BLOCK, wide), 1) % TOP
    factor_ref[0] = jnp.where(seen, decay, 0.0)
    factor_ref[1] = jnp.broadcast_to(dt_s, (BLOCK, wide))


def carry_body(got_ref, before_ref, own_ref, c_ref, part_ref, grown_ref, factor_ref, tail_ref, y_ref, win, c_first):
    _, rows, blocks = sizes_of(got_ref)
    taps = tiles_of(own_ref)
    first = TOP - taps[0].shape[0] + 1

    halo = before_ref[STATE:].astype(F32)
    upper = pltpu.roll(halo, TOP // 2, 0)
    tops = []
    for q in range(TILES + 2):
        lo = q * LANES
        win[q, :TOP] = upper[:, lo : lo + LANES] if q < TILES else halo[:, lo - WIDE : lo - WIDE + LANES]
        win[q, TOP:] = got_ref[0, q * rows : (q + 1) * rows, :].astype(F32)[:TOP]
        done = conv(lambda k: win[q, first + k : first + k + TOP], taps[q])
        tops.append(done.astype(BF16).astype(F32))
    x_top = jnp.concatenate(tops[:TILES], 1)
    b_top = tops[TILES]
    b_twice = jnp.concatenate([b_top, b_top], 0).astype(BF16)
    head = dot_t(b_twice, stacked(x_top * tail_ref[...], 2))
    state = before_ref[:STATE]
    later = stacked(grown_ref[BLOCK - 1 : BLOCK] * state.astype(F32) + head, 2)

    c_first[...] = c_ref[:BLOCK].astype(F32)
    c_first[:TOP] = tops[TILES + 1]
    c = c_first[...].astype(BF16)
    wide = OWN * TOP
    scores = lax.dot_general(
        c, jnp.concatenate([b_top] * OWN, 0).astype(BF16), (((1,), (1,)), ((), ())), preferred_element_type=F32
    )
    mix = (scores * factor_ref[0] * factor_ref[1]).astype(BF16)
    shape = (wide, WIDE)
    own = iota(shape, 0) // TOP == iota(shape, 1) // HEAD_DIM
    added = dot(mix, jnp.where(own, jnp.concatenate([x_top] * OWN, 0), 0.0).astype(BF16))
    y_ref[:BLOCK] = (part_ref[:BLOCK] + added + dot(c, state) * grown_ref[:BLOCK]).astype(BF16)
    for j in range(1, blocks):
        at = j * BLOCK
        c = c_ref[at : at + BLOCK]
        carried = dot(jnp.concatenate([c, c], 1), later)
        y_ref[at : at + BLOCK] = (part_ref[at : at + BLOCK] + carried * grown_ref[at : at + BLOCK]).astype(BF16)


def norm_body(y_ref, gate_ref, gain_ref, out_hbm, out_v, sem):
    count = y_ref.shape[0]
    per = count // GROUPS
    copies = []
    for g in range(GROUPS):
        gated = []
        square = 0.0
        for k in range(g * per, (g + 1) * per):
            v = y_ref[k].astype(F32) * gate_ref[:, k * WIDE : (k + 1) * WIDE]
            gated.append(v)
            square = square + jnp.sum(v * v, axis=1, keepdims=True)
        scale = lax.rsqrt(square / (per * WIDE) + eps_norm)
        for k in range(g * per, (g + 1) * per):
            at = k * WIDE
            gain = gain_ref[:, at : at + WIDE]
            out_v[:, at : at + WIDE] = (gated[k - g * per] * scale * gain).astype(BF16)
        part = pl.ds(g * per * WIDE, per * WIDE)
        copies.append(pltpu.make_async_copy(out_v.at[:, part], out_hbm.at[:, part], sem.at[g]))
        copies[-1].start()
    for copy in copies:
        copy.wait()


def shift(block, axis, distance):
    size = lax.axis_size(axis)
    return lax.ppermute(block, axis, [(i, i + distance) for i in range(size - distance)])


def kernel(body, name, ins, outs, scratch=(), cost=None, out_specs=None):
    return pl.pallas_call(
        body,
        in_specs=ins,
        out_specs=out_specs or [IN_VMEM] * len(outs),
        out_shape=outs,
        scratch_shapes=list(scratch),
        compiler_params=pltpu.CompilerParams(vmem_limit_bytes=40 * 2**20),
        cost_estimate=cost,
        name=name,
    )


def shards(x_in, b_in, c_in, dt_in, z_in, conv_x, input_state_taps, conv_c, dt_bias, a_log, norm_gain):
    outer, inner, head = (lax.axis_size(a) for a in ("outer", "inner", "head"))
    dests = inner * head
    rows = x_in.shape[0]
    tokens = rows * dests
    blocks = tokens // BLOCK
    mine = (lax.axis_index("inner") * head + lax.axis_index("head")).astype(jnp.int32).reshape(1)

    def of(dtype, *shape):
        return jax.ShapeDtypeStruct(shape, dtype)

    total = (TILES + 2) * rows + OWN
    lead = conv_x.shape[0]
    hbm = pl.BlockSpec(memory_space=pltpu.HBM)
    operands = (x_in, b_in, c_in, dt_in, conv_x, input_state_taps, conv_c, dt_bias.reshape(1, -1), a_log.reshape(1, -1))
    sent, own = kernel(
        pack_body, "pack", [IN_SMEM] + [hbm] * len(operands),
        [of(BF16, dests, total, LANES), of(F32, lead + 2 * OWN, WIDE + 2 * STATE)],
        [
            pltpu.VMEM(x_in.shape, BF16), pltpu.VMEM(b_in.shape, BF16), pltpu.VMEM(c_in.shape, BF16),
            pltpu.VMEM(dt_in.shape, BF16), pltpu.VMEM((BLOCK, LANES), F32),
            pltpu.VMEM((lead, WIDE), F32), pltpu.VMEM((2, lead, STATE), F32), pltpu.VMEM((2, 1, LANES), F32),
            pltpu.SemaphoreType.DMA((7,)), pltpu.SemaphoreType.DMA((5,)),
        ],
    )(mine, *(pltpu.with_memory_space_constraint(a, pltpu.HBM) for a in operands))
    got = lax.all_to_all(sent, ("inner", "head"), 0, 0, tiled=True)
    [gate] = kernel(
        gate_body, "gate", [IN_VMEM], [of(F32, *z_in.shape)],
        cost=pl.CostEstimate(flops=5 * z_in.size, bytes_accessed=6 * z_in.size, transcendentals=z_in.size),
    )(z_in)

    if outer > 2:
        ends = got[-1, : (TILES + 2) * rows].reshape(TILES + 2, rows, LANES)[:, -TOP:]
        halo = shift(ends, "outer", 1).transpose(1, 0, 2).reshape(TOP, -1).astype(F32)
    else:
        halo = jnp.zeros((TOP, (TILES + 2) * LANES), F32)

    extra = STATE + TOP
    sends = (lax.axis_index("outer") < outer - 1).astype(jnp.int32).reshape(1)
    send, fade = kernel(
        total_body, "total", [IN_SMEM] + [IN_VMEM] * 3,
        [of(BF16, extra, WIDE), of(F32, 8, WIDE)],
        [pltpu.VMEM((TILES + 1, TOP + tokens, LANES), F32)],
    )(sends, got, halo, own)

    before = shift(send, "outer", 1)
    if outer > 2:
        entering, held, reach = before[:STATE].astype(F32), shift(fade, "outer", 1), 1
        while reach < outer - 1:
            entering = entering + held[:1] * shift(entering, "outer", reach)
            held = held * shift(held, "outer", reach)
            reach *= 2
        before = jnp.concatenate([entering.astype(BF16), before[STATE:]], 0)

    wide = OWN * TOP
    c, part, grown, factor, tail = kernel(
        local_body, "local", [IN_VMEM] * 4,
        [
            of(BF16, tokens, STATE), of(F32, tokens, WIDE), of(F32, tokens, WIDE),
            of(F32, 2, BLOCK, wide), of(F32, TOP, WIDE),
        ],
        [pltpu.VMEM((TILES + 2, TOP + tokens, LANES), F32), pltpu.VMEM((BLOCK, LANES), F32)],
        pl.CostEstimate(
            flops=2 * blocks * OWN * BLOCK * BLOCK * 160,
            bytes_accessed=tokens * WIDE * 12,
            transcendentals=blocks * OWN * BLOCK * BLOCK,
        ),
    )(got, halo, own, fade)

    [y] = kernel(
        carry_body, "carry", [IN_VMEM] * 8, [of(BF16, tokens, WIDE)],
        [pltpu.VMEM((TILES + 2, 2 * TOP, LANES), F32), pltpu.VMEM((BLOCK, STATE), F32)],
    )(got, before, own, c, part, grown, factor, tail)

    home = lax.all_to_all(y.reshape(dests, rows, WIDE), ("inner", "head"), 0, 0, tiled=True)
    [out] = kernel(
        norm_body, "norm", [IN_VMEM] * 3, [of(BF16, rows, dests * WIDE)],
        [pltpu.VMEM((rows, dests * WIDE), BF16), pltpu.SemaphoreType.DMA((GROUPS,))], out_specs=[hbm],
    )(home, gate, norm_gain.reshape(1, -1))
    return out


def solution(mesh):
    ctx, head = mesh.devices.shape
    inner = max(1, GROUPS * 16 // (OWN * head))
    cut = Mesh(mesh.devices.reshape(ctx // inner, inner, head), ("outer", "inner", "head"))
    rows = P(("outer", "inner", "head"), None)
    return jax.shard_map(
        shards,
        mesh=cut,
        in_specs=(rows,) * 5 + (P(),) * 6,
        out_specs=rows,
        check_vma=False,
    )
```

```python
import jax
import jax.numpy as jnp
from jax import lax
from jax.experimental import pallas as pl
from jax.experimental.pallas import tpu as pltpu
from jax.sharding import Mesh
from jax.sharding import PartitionSpec as P

HEAD_DIM = 64
STATE = 128
GROUPS = 8
BLOCK = 128
OWN = 8
WIDE = OWN * HEAD_DIM
LANES = 128
TILES = WIDE // LANES
TOP = 8

eps_norm = 1e-05
F32 = jnp.float32
BF16 = jnp.bfloat16
IN_VMEM = pl.BlockSpec(memory_space=pltpu.VMEM)
IN_SMEM = pl.BlockSpec(memory_space=pltpu.SMEM)


def dot(a, b):
    return jnp.dot(a, b, preferred_element_type=F32)


def dot_t(a, b):
    return lax.dot_general(a, b, (((0,), (0,)), ((), ())), preferred_element_type=F32)


def iota(shape, axis):
    return lax.broadcasted_iota(jnp.int32, shape, axis)


def parts_of(values, count):
    out = []
    for k in range(count):
        piece = values.astype(BF16).astype(F32)
        out.append(piece)
        if k + 1 < count:
            values = values - piece
    return out


def stacked(values, count):
    return jnp.concatenate(parts_of(values, count), 0).astype(BF16)


def one_hot(rows, width):
    shape = (rows, OWN * width)
    return (iota(shape, 0) % OWN == iota(shape, 1) // width).astype(F32).astype(BF16)


def expand(values):
    return dot_t(stacked(values, 2), one_hot(2 * OWN, HEAD_DIM))


def silu(v):
    return v * jax.nn.sigmoid(v)


def conv(window, tap):
    total = tap[0:1] * window(0)
    for k in range(1, tap.shape[0]):
        total = total + tap[k : k + 1] * window(k)
    return silu(total)


def tiles_of(own_ref):
    return [own_ref[:lead_of(own_ref), q * LANES : (q + 1) * LANES] for q in range(TILES + 2)]


def lead_of(own_ref):
    return own_ref.shape[0] - 2 * OWN


def pack_body(
    place_ref, x_hbm, b_hbm, c_hbm, dt_hbm, tap_x, tap_b, tap_c, bias_hbm, log_hbm,
    out_v, own_ref, x_v, b_v, c_v, dt_v, turn, x_tap, s_taps, heads_v, sem_in, sem_own,
):
    mine = place_ref[0] // 2
    count = out_v.shape[0]
    rows = x_v.shape[0]
    share = count * STATE // b_v.shape[1]
    cuts = 4
    step = count // cuts
    wide = step * WIDE
    small = [
        pltpu.make_async_copy(src, dst, sem_in.at[k])
        for k, (src, dst) in enumerate(((dt_hbm, dt_v), (b_hbm, b_v), (c_hbm, c_v)))
    ]
    large = [
        pltpu.make_async_copy(x_hbm.at[:, pl.ds(i * wide, wide)], x_v.at[:, pl.ds(i * wide, wide)], sem_in.at[3 + i])
        for i in range(cuts)
    ]
    at_x = pl.multiple_of(mine * WIDE, WIDE)
    at_s = pl.multiple_of(mine // share * STATE, STATE)
    own = [
        pltpu.make_async_copy(src, dst, sem_own.at[k])
        for k, (src, dst) in enumerate((
            (tap_x.at[:, pl.ds(at_x, WIDE)], x_tap),
            (tap_b.at[:, pl.ds(at_s, STATE)], s_taps.at[0]),
            (tap_c.at[:, pl.ds(at_s, STATE)], s_taps.at[1]),
            (bias_hbm, heads_v.at[0]),
            (log_hbm, heads_v.at[1]),
        ))
    ]
    for copy in small + large + own:
        copy.start()
    small[0].wait()
    turn[...] = jnp.zeros_like(turn)
    at = pl.multiple_of(lax.rem(mine, BLOCK // rows) * rows, rows)
    turn[pl.ds(at, rows), :] = dt_v[...].astype(F32)
    heads = turn[...].T
    for k in range(count):
        out_v[k, (TILES + 2) * rows :, :] = heads[k * OWN : (k + 1) * OWN].astype(BF16)
    small[1].wait()
    small[2].wait()
    for k in range(count):
        g = k // share
        out_v[k, TILES * rows : (TILES + 1) * rows, :] = b_v[:, g * STATE : (g + 1) * STATE]
        out_v[k, (TILES + 1) * rows : (TILES + 2) * rows, :] = c_v[:, g * STATE : (g + 1) * STATE]
    for i in range(cuts):
        large[i].wait()
        for k in range(i * step, (i + 1) * step):
            for q in range(TILES):
                lo = k * WIDE + q * LANES
                out_v[k, q * rows : (q + 1) * rows, :] = x_v[:, lo : lo + LANES]
    for copy in own:
        copy.wait()
    taps = x_tap.shape[0]
    own_ref[:taps, :WIDE] = x_tap[...]
    own_ref[:taps, WIDE : WIDE + STATE] = s_taps[0]
    own_ref[:taps, WIDE + STATE :] = s_taps[1]
    mask = iota((OWN, LANES), 0) + mine * OWN == iota((OWN, LANES), 1)
    for k in range(2):
        column = jnp.sum(jnp.where(mask, heads_v[k], 0.0), axis=1, keepdims=True)
        at = taps + k * OWN
        own_ref[at : at + OWN, :LANES] = jnp.broadcast_to(column, (OWN, LANES))


def sizes_of(got_ref):
    sources, total, _ = got_ref.shape
    rows = (total - OWN) // (TILES + 2)
    return sources, rows, sources * rows // BLOCK


def fill(win, got_ref, halo_ref, tiles):
    sources, rows, _ = sizes_of(got_ref)
    for q in range(tiles):
        win[q, :TOP] = halo_ref[:, q * LANES : (q + 1) * LANES]
        for s in range(sources):
            at = TOP + s * rows
            win[q, at : at + rows] = got_ref[s, q * rows : (q + 1) * rows, :].astype(F32)


def conv_tile(win, taps, j, q):
    first = j * BLOCK + TOP - taps[q].shape[0] + 1
    return conv(lambda k: win[q, first + k : first + k + BLOCK], taps[q]).astype(BF16)


def steps_of(got_ref, own_ref):
    _, rows, blocks = sizes_of(got_ref)
    per = BLOCK // rows
    lead = lead_of(own_ref)
    raws = []
    for j in range(blocks):
        raw = got_ref[j * per, (TILES + 2) * rows :, :].astype(F32)
        for s in range(1, per):
            raw = raw + got_ref[j * per + s, (TILES + 2) * rows :, :].astype(F32)
        raws.append(raw + own_ref[lead : lead + OWN, :LANES])
    raw = jnp.concatenate(raws, 0)
    dt = jnp.maximum(raw, 0.0) + jnp.log1p(jnp.exp(-jnp.abs(raw)))
    rate = jnp.concatenate([-jnp.exp(own_ref[lead + OWN :, :LANES])] * blocks, 0)
    upto = (iota((BLOCK, BLOCK), 0) <= iota((BLOCK, BLOCK), 1)).astype(F32).astype(BF16)
    sums = dot(stacked(dt * rate, 4), upto)
    n = blocks * OWN
    cum = sums[:n] + sums[n : 2 * n] + sums[2 * n : 3 * n] + sums[3 * n :]
    return [[v[j * OWN : (j + 1) * OWN] for j in range(blocks)] for v in (dt, cum)]


def total_body(place_ref, got_ref, halo_ref, own_ref, send_ref, fade_ref, win):
    @pl.when(lax.rem(place_ref[0], 2) != 0)
    def _():
        sources, rows, blocks = sizes_of(got_ref)
        dts, cums = steps_of(got_ref, own_ref)
        taps = tiles_of(own_ref)
        fill(win, got_ref, halo_ref, TILES + 1)
        state = jnp.zeros((STATE, WIDE), F32)
        after = jnp.zeros((OWN, 1), F32)
        for j in reversed(range(blocks)):
            after = after + cums[j][:, BLOCK - 1 :]
            tail = expand(jnp.exp(after - cums[j]) * dts[j])
            x = jnp.concatenate([conv_tile(win, taps, j, q) for q in range(TILES)], 1)
            b = conv_tile(win, taps, j, TILES)
            state = state + dot_t(jnp.concatenate([b, b], 0), stacked(x.astype(F32) * tail, 2))
        fade_ref[...] = expand(jnp.broadcast_to(jnp.exp(after), (OWN, LANES)))[:8]
        send_ref[:STATE] = state.astype(BF16)
        ends = [got_ref[sources - 1, q * rows : (q + 1) * rows, :].astype(F32)[rows - TOP :] for q in range(TILES + 2)]
        ends += [jnp.zeros_like(ends[0])] * (TILES - 2)
        half = TOP // 2
        upper = pltpu.roll(jnp.concatenate(ends[:TILES], 1), half, 0)
        keep = iota((TOP, WIDE), 0) < half
        send_ref[STATE:] = jnp.where(keep, upper, jnp.concatenate(ends[TILES:], 1)).astype(BF16)


def local_body(
    got_ref, halo_ref, own_ref, z_ref, order_ref,
    c_ref, part_ref, grown_ref, factor_ref, tail_ref, gate_ref, win, turn,
):
    for lo in range(0, z_ref.shape[1], WIDE):
        gate_ref[:, lo : lo + WIDE] = silu(z_ref[:, lo : lo + WIDE].astype(F32))
    _, _, blocks = sizes_of(got_ref)
    dts, cums = steps_of(got_ref, own_ref)
    taps = tiles_of(own_ref)
    fill(win, got_ref, halo_ref, TILES + 2)
    turn[...] = jnp.zeros_like(turn)
    for j in range(blocks):
        turn[j * OWN : (j + 1) * OWN] = cums[j]
    cols = turn[...].T
    t_at = iota((BLOCK, BLOCK), 0)
    s_at = iota((BLOCK, BLOCK), 1)
    left = iota((BLOCK, LANES), 1) < HEAD_DIM
    zero = jnp.zeros((BLOCK, LANES), BF16)
    past = jnp.zeros((OWN, 1), F32)
    local = None
    for j in range(blocks):
        at = j * BLOCK
        x = [conv_tile(win, taps, j, q) for q in range(TILES)]
        b = conv_tile(win, taps, j, TILES)
        c = conv_tile(win, taps, j, TILES + 1)
        c_ref[at : at + BLOCK] = c
        scores = lax.dot_general(c, b, (((1,), (1,)), ((), ())), preferred_element_type=F32)
        keep = t_at >= s_at
        if j == 0:
            keep = keep & (s_at >= TOP)
        scores = jnp.where(keep, scores, 0.0)
        cum, dt = cums[j], dts[j]
        last = cum[:, BLOCK - 1 :]
        grown = expand(jnp.exp(cum))
        if j < 2:
            grown_ref[at : at + BLOCK] = grown
        else:
            past = past + cums[j - 1][:, BLOCK - 1 :]
            grown_ref[at : at + BLOCK] = expand(jnp.exp(cum + past))
        if j > 0:
            carried = dot(jnp.concatenate([c, c], 1), stacked(local, 2)) * grown
        for q in range(TILES):
            lo = q * LANES
            mixes = []
            for h in (2 * q, 2 * q + 1):
                col = j * OWN + h
                gap = jnp.minimum(cols[:, col : col + 1] - cum[h : h + 1], 0.0)
                mixes.append((scores * jnp.exp(gap) * dt[h : h + 1]).astype(BF16))
            both = jnp.concatenate([jnp.where(left, x[q], zero), jnp.where(left, zero, x[q])], 0)
            part = dot(jnp.concatenate(mixes, 1), both)
            part_ref[at : at + BLOCK, lo : lo + LANES] = part if j == 0 else part + carried[:, lo : lo + LANES]
        tail = expand(jnp.exp(last - cum) * dt)
        if j == 0:
            tail_ref[...] = tail[:TOP]
            tail = jnp.where(iota((BLOCK, WIDE), 0) < TOP, 0.0, tail)
        if j + 1 < blocks:
            weighted = stacked(jnp.concatenate(x, 1).astype(F32) * tail, 2)
            fresh = dot_t(jnp.concatenate([b, b], 0), weighted)
            local = fresh if j == 0 else grown[BLOCK - 1 :] * local + fresh

    wide = OWN * TOP
    spread = one_hot(4 * OWN, TOP)
    cum_t = dot_t(stacked(cums[0], 4), spread)
    same = iota((TOP, wide), 0) == iota((TOP, wide), 1) % TOP
    cum_s = jnp.sum(jnp.where(same, cum_t[:TOP], 0.0), axis=0, keepdims=True)
    dt_s = jnp.sum(jnp.where(same, dot_t(stacked(dts[0], 4), spread)[:TOP], 0.0), axis=0, keepdims=True)
    decay = jnp.exp(jnp.minimum(cum_t - cum_s, 0.0))
    seen = iota((BLOCK, wide), 0) >= iota((BLOCK, wide), 1) % TOP
    factor_ref[0] = jnp.where(seen, decay, 0.0)
    factor_ref[1] = jnp.broadcast_to(dt_s, (BLOCK, wide))


def carry_body(got_ref, before_ref, own_ref, c_ref, part_ref, grown_ref, factor_ref, tail_ref, y_ref, win, c_first):
    _, rows, blocks = sizes_of(got_ref)
    taps = tiles_of(own_ref)
    first = TOP - taps[0].shape[0] + 1

    halo = before_ref[STATE:].astype(F32)
    upper = pltpu.roll(halo, TOP // 2, 0)
    tops = []
    for q in range(TILES + 2):
        lo = q * LANES
        win[q, :TOP] = upper[:, lo : lo + LANES] if q < TILES else halo[:, lo - WIDE : lo - WIDE + LANES]
        win[q, TOP:] = got_ref[0, q * rows : (q + 1) * rows, :].astype(F32)[:TOP]
        done = conv(lambda k: win[q, first + k : first + k + TOP], taps[q])
        tops.append(done.astype(BF16).astype(F32))
    x_top = jnp.concatenate(tops[:TILES], 1)
    b_top = tops[TILES]
    b_twice = jnp.concatenate([b_top, b_top], 0).astype(BF16)
    head = dot_t(b_twice, stacked(x_top * tail_ref[...], 2))
    state = before_ref[:STATE]
    later = stacked(grown_ref[BLOCK - 1 : BLOCK] * state.astype(F32) + head, 2)

    c_first[...] = c_ref[:BLOCK].astype(F32)
    c_first[:TOP] = tops[TILES + 1]
    c = c_first[...].astype(BF16)
    wide = OWN * TOP
    scores = lax.dot_general(
        c, jnp.concatenate([b_top] * OWN, 0).astype(BF16), (((1,), (1,)), ((), ())), preferred_element_type=F32
    )
    mix = (scores * factor_ref[0] * factor_ref[1]).astype(BF16)
    shape = (wide, WIDE)
    own = iota(shape, 0) // TOP == iota(shape, 1) // HEAD_DIM
    added = dot(mix, jnp.where(own, jnp.concatenate([x_top] * OWN, 0), 0.0).astype(BF16))
    y_ref[:BLOCK] = (part_ref[:BLOCK] + added + dot(c, state) * grown_ref[:BLOCK]).astype(BF16)
    for j in range(1, blocks):
        at = j * BLOCK
        c = c_ref[at : at + BLOCK]
        carried = dot(jnp.concatenate([c, c], 1), later)
        y_ref[at : at + BLOCK] = (part_ref[at : at + BLOCK] + carried * grown_ref[at : at + BLOCK]).astype(BF16)


def norm_body(y_ref, gate_ref, gain_ref, out_hbm, out_v, sem):
    count = y_ref.shape[0]
    per = count // GROUPS
    copies = []
    for g in range(GROUPS):
        gated = []
        square = 0.0
        for k in range(g * per, (g + 1) * per):
            v = y_ref[k].astype(F32) * gate_ref[:, k * WIDE : (k + 1) * WIDE]
            gated.append(v)
            square = square + jnp.sum(v * v, axis=1, keepdims=True)
        scale = lax.rsqrt(square / (per * WIDE) + eps_norm)
        for k in range(g * per, (g + 1) * per):
            at = k * WIDE
            gain = gain_ref[:, at : at + WIDE]
            out_v[:, at : at + WIDE] = (gated[k - g * per] * scale * gain).astype(BF16)
        part = pl.ds(g * per * WIDE, per * WIDE)
        copies.append(pltpu.make_async_copy(out_v.at[:, part], out_hbm.at[:, part], sem.at[g]))
        copies[-1].start()
    for copy in copies:
        copy.wait()


def shift(block, axis, distance):
    size = lax.axis_size(axis)
    return lax.ppermute(block, axis, [(i, i + distance) for i in range(size - distance)])


def kernel(body, name, ins, outs, scratch=(), cost=None, out_specs=None):
    return pl.pallas_call(
        body,
        in_specs=ins,
        out_specs=out_specs or [IN_VMEM] * len(outs),
        out_shape=outs,
        scratch_shapes=list(scratch),
        compiler_params=pltpu.CompilerParams(vmem_limit_bytes=40 * 2**20),
        cost_estimate=cost,
        name=name,
    )


def shards(x_in, b_in, c_in, dt_in, z_in, conv_x, input_state_taps, conv_c, dt_bias, a_log, norm_gain):
    outer, inner, head = (lax.axis_size(a) for a in ("outer", "inner", "head"))
    dests = inner * head
    rows = x_in.shape[0]
    tokens = rows * dests
    blocks = tokens // BLOCK
    mine = lax.axis_index("inner") * head + lax.axis_index("head")
    place = (mine * 2 + (lax.axis_index("outer") < outer - 1)).astype(jnp.int32).reshape(1)

    def of(dtype, *shape):
        return jax.ShapeDtypeStruct(shape, dtype)

    total = (TILES + 2) * rows + OWN
    lead = conv_x.shape[0]
    hbm = pl.BlockSpec(memory_space=pltpu.HBM)
    operands = (x_in, b_in, c_in, dt_in, conv_x, input_state_taps, conv_c, dt_bias.reshape(1, -1), a_log.reshape(1, -1))
    sent, own = kernel(
        pack_body, "pack", [IN_SMEM] + [hbm] * len(operands),
        [of(BF16, dests, total, LANES), of(F32, lead + 2 * OWN, WIDE + 2 * STATE)],
        [
            pltpu.VMEM(x_in.shape, BF16), pltpu.VMEM(b_in.shape, BF16), pltpu.VMEM(c_in.shape, BF16),
            pltpu.VMEM(dt_in.shape, BF16), pltpu.VMEM((BLOCK, LANES), F32),
            pltpu.VMEM((lead, WIDE), F32), pltpu.VMEM((2, lead, STATE), F32), pltpu.VMEM((2, 1, LANES), F32),
            pltpu.SemaphoreType.DMA((7,)), pltpu.SemaphoreType.DMA((5,)),
        ],
    )(place, *(pltpu.with_memory_space_constraint(a, pltpu.HBM) for a in operands))
    got = lax.all_to_all(sent, ("inner", "head"), 0, 0, tiled=True)
    if outer > 2:
        ends = got[-1, : (TILES + 2) * rows].reshape(TILES + 2, rows, LANES)[:, -TOP:]
        halo = shift(ends, "outer", 1).transpose(1, 0, 2).reshape(TOP, -1).astype(F32)
    else:
        halo = jnp.zeros((TOP, (TILES + 2) * LANES), F32)

    extra = STATE + TOP
    send, fade = kernel(
        total_body, "total", [IN_SMEM] + [IN_VMEM] * 3,
        [of(BF16, extra, WIDE), of(F32, 8, WIDE)],
        [pltpu.VMEM((TILES + 1, TOP + tokens, LANES), F32)],
    )(place, got, halo, own)

    before = shift(send, "outer", 1)
    if outer > 2:
        entering, held, reach = before[:STATE].astype(F32), shift(fade, "outer", 1), 1
        while reach < outer - 1:
            entering = entering + held[:1] * shift(entering, "outer", reach)
            held = held * shift(held, "outer", reach)
            reach *= 2
        before = jnp.concatenate([entering.astype(BF16), before[STATE:]], 0)

    wide = OWN * TOP
    c, part, grown, factor, tail, gate = kernel(
        local_body, "local", [IN_VMEM] * 5,
        [
            of(BF16, tokens, STATE), of(F32, tokens, WIDE), of(F32, tokens, WIDE),
            of(F32, 2, BLOCK, wide), of(F32, TOP, WIDE), of(F32, *z_in.shape),
        ],
        [pltpu.VMEM((TILES + 2, TOP + tokens, LANES), F32), pltpu.VMEM((BLOCK, LANES), F32)],
        pl.CostEstimate(
            flops=2 * blocks * OWN * BLOCK * BLOCK * 160,
            bytes_accessed=tokens * WIDE * 12,
            transcendentals=blocks * OWN * BLOCK * BLOCK,
        ),
    )(got, halo, own, z_in, fade)

    [y] = kernel(
        carry_body, "carry", [IN_VMEM] * 8, [of(BF16, tokens, WIDE)],
        [pltpu.VMEM((TILES + 2, 2 * TOP, LANES), F32), pltpu.VMEM((BLOCK, STATE), F32)],
    )(got, before, own, c, part, grown, factor, tail)

    home = lax.all_to_all(y.reshape(dests, rows, WIDE), ("inner", "head"), 0, 0, tiled=True)
    [out] = kernel(
        norm_body, "norm", [IN_VMEM] * 3, [of(BF16, rows, dests * WIDE)],
        [pltpu.VMEM((rows, dests * WIDE), BF16), pltpu.SemaphoreType.DMA((GROUPS,))], out_specs=[hbm],
    )(home, gate, norm_gain.reshape(1, -1))
    return out


def solution(mesh):
    ctx, head = mesh.devices.shape
    inner = max(1, GROUPS * 16 // (OWN * head))
    cut = Mesh(mesh.devices.reshape(ctx // inner, inner, head), ("outer", "inner", "head"))
    rows = P(("outer", "inner", "head"), None)
    return jax.shard_map(
        shards,
        mesh=cut,
        in_specs=(rows,) * 5 + (P(),) * 6,
        out_specs=rows,
        check_vma=False,
    )
```

```python
import functools
import jax
import jax.numpy as jnp
from jax import lax
from jax.experimental import pallas as pl
from jax.experimental.pallas import tpu as pltpu
from jax.sharding import Mesh
from jax.sharding import PartitionSpec as P

HEAD_DIM = 64
STATE = 128
GROUPS = 8
BLOCK = 128
OWN = 8
WIDE = OWN * HEAD_DIM
LANES = 128
TILES = WIDE // LANES
TOP = 8

eps_norm = 1e-05
F32 = jnp.float32
BF16 = jnp.bfloat16
IN_VMEM = pl.BlockSpec(memory_space=pltpu.VMEM)
IN_SMEM = pl.BlockSpec(memory_space=pltpu.SMEM)


def dot(a, b):
    return jnp.dot(a, b, preferred_element_type=F32)


def dot_t(a, b):
    return lax.dot_general(a, b, (((0,), (0,)), ((), ())), preferred_element_type=F32)


def iota(shape, axis):
    return lax.broadcasted_iota(jnp.int32, shape, axis)


def parts_of(values, count):
    out = []
    for k in range(count):
        piece = values.astype(BF16).astype(F32)
        out.append(piece)
        if k + 1 < count:
            values = values - piece
    return out


def stacked(values, count):
    return jnp.concatenate(parts_of(values, count), 0).astype(BF16)


def one_hot(rows, width):
    shape = (rows, OWN * width)
    return (iota(shape, 0) % OWN == iota(shape, 1) // width).astype(F32).astype(BF16)


def expand(values):
    return dot_t(stacked(values, 2), one_hot(2 * OWN, HEAD_DIM))


def silu(v):
    return v * jax.nn.sigmoid(v)


def conv(window, tap):
    total = tap[0:1] * window(0)
    for k in range(1, tap.shape[0]):
        total = total + tap[k : k + 1] * window(k)
    return silu(total)


def tiles_of(own_ref):
    return [own_ref[:lead_of(own_ref), q * LANES : (q + 1) * LANES] for q in range(TILES + 2)]


def lead_of(own_ref):
    return own_ref.shape[0] - 2 * OWN


def pack_body(
    mine_ref, x_hbm, b_hbm, c_hbm, dt_hbm, tap_x, tap_b, tap_c, bias_hbm, log_hbm,
    out_v, own_ref, x_v, b_v, c_v, dt_v, turn, x_tap, s_taps, heads_v, sem_in, sem_own,
):
    mine = mine_ref[0]
    count = out_v.shape[0]
    rows = x_v.shape[0]
    share = count * STATE // b_v.shape[1]
    cuts = 4
    step = count // cuts
    wide = step * WIDE
    small = [
        pltpu.make_async_copy(src, dst, sem_in.at[k])
        for k, (src, dst) in enumerate(((dt_hbm, dt_v), (b_hbm, b_v), (c_hbm, c_v)))
    ]
    large = [
        pltpu.make_async_copy(x_hbm.at[:, pl.ds(i * wide, wide)], x_v.at[:, pl.ds(i * wide, wide)], sem_in.at[3 + i])
        for i in range(cuts)
    ]
    at_x = pl.multiple_of(mine * WIDE, WIDE)
    at_s = pl.multiple_of(mine // share * STATE, STATE)
    own = [
        pltpu.make_async_copy(src, dst, sem_own.at[k])
        for k, (src, dst) in enumerate((
            (tap_x.at[:, pl.ds(at_x, WIDE)], x_tap),
            (tap_b.at[:, pl.ds(at_s, STATE)], s_taps.at[0]),
            (tap_c.at[:, pl.ds(at_s, STATE)], s_taps.at[1]),
            (bias_hbm, heads_v.at[0]),
            (log_hbm, heads_v.at[1]),
        ))
    ]
    for copy in small + large + own:
        copy.start()
    small[0].wait()
    turn[...] = jnp.zeros_like(turn)
    at = pl.multiple_of(lax.rem(mine, BLOCK // rows) * rows, rows)
    turn[pl.ds(at, rows), :] = dt_v[...].astype(F32)
    heads = turn[...].T
    for k in range(count):
        out_v[k, (TILES + 2) * rows :, :] = heads[k * OWN : (k + 1) * OWN].astype(BF16)
    small[1].wait()
    small[2].wait()
    for k in range(count):
        g = k // share
        out_v[k, TILES * rows : (TILES + 1) * rows, :] = b_v[:, g * STATE : (g + 1) * STATE]
        out_v[k, (TILES + 1) * rows : (TILES + 2) * rows, :] = c_v[:, g * STATE : (g + 1) * STATE]
    for i in range(cuts):
        large[i].wait()
        for k in range(i * step, (i + 1) * step):
            for q in range(TILES):
                lo = k * WIDE + q * LANES
                out_v[k, q * rows : (q + 1) * rows, :] = x_v[:, lo : lo + LANES]
    for copy in own:
        copy.wait()
    taps = x_tap.shape[0]
    own_ref[:taps, :WIDE] = x_tap[...]
    own_ref[:taps, WIDE : WIDE + STATE] = s_taps[0]
    own_ref[:taps, WIDE + STATE :] = s_taps[1]
    mask = iota((OWN, LANES), 0) + mine * OWN == iota((OWN, LANES), 1)
    for k in range(2):
        column = jnp.sum(jnp.where(mask, heads_v[k], 0.0), axis=1, keepdims=True)
        at = taps + k * OWN
        own_ref[at : at + OWN, :LANES] = jnp.broadcast_to(column, (OWN, LANES))


def sizes_of(got_ref):
    sources, total, _ = got_ref.shape
    rows = (total - OWN) // (TILES + 2)
    return sources, rows, sources * rows // BLOCK


def fill(win, got_ref, halo_ref, tiles):
    sources, rows, _ = sizes_of(got_ref)
    for q in range(tiles):
        win[q, :TOP] = halo_ref[:, q * LANES : (q + 1) * LANES]
        for s in range(sources):
            at = TOP + s * rows
            win[q, at : at + rows] = got_ref[s, q * rows : (q + 1) * rows, :].astype(F32)


def conv_tile(win, taps, j, q):
    first = j * BLOCK + TOP - taps[q].shape[0] + 1
    return conv(lambda k: win[q, first + k : first + k + BLOCK], taps[q]).astype(BF16)


def steps_of(got_ref, own_ref):
    _, rows, blocks = sizes_of(got_ref)
    per = BLOCK // rows
    lead = lead_of(own_ref)
    raws = []
    for j in range(blocks):
        raw = got_ref[j * per, (TILES + 2) * rows :, :].astype(F32)
        for s in range(1, per):
            raw = raw + got_ref[j * per + s, (TILES + 2) * rows :, :].astype(F32)
        raws.append(raw + own_ref[lead : lead + OWN, :LANES])
    raw = jnp.concatenate(raws, 0)
    dt = jnp.maximum(raw, 0.0) + jnp.log1p(jnp.exp(-jnp.abs(raw)))
    rate = jnp.concatenate([-jnp.exp(own_ref[lead + OWN :, :LANES])] * blocks, 0)
    upto = (iota((BLOCK, BLOCK), 0) <= iota((BLOCK, BLOCK), 1)).astype(F32).astype(BF16)
    sums = dot(stacked(dt * rate, 4), upto)
    n = blocks * OWN
    cum = sums[:n] + sums[n : 2 * n] + sums[2 * n : 3 * n] + sums[3 * n :]
    return [[v[j * OWN : (j + 1) * OWN] for j in range(blocks)] for v in (dt, cum)]


def total_body(got_ref, halo_ref, own_ref, send_ref, other_ref, win, sem, *, last_but_one):
    sources, rows, blocks = sizes_of(got_ref)
    if last_but_one:
        copy = pltpu.make_async_copy(got_ref, other_ref, sem)
        copy.start()
    dts, cums = steps_of(got_ref, own_ref)
    taps = tiles_of(own_ref)
    fill(win, got_ref, halo_ref, TILES + 1)
    state = jnp.zeros((STATE, WIDE), F32)
    after = jnp.zeros((OWN, 1), F32)
    for j in reversed(range(blocks)):
        after = after + cums[j][:, BLOCK - 1 :]
        tail = expand(jnp.exp(after - cums[j]) * dts[j])
        x = jnp.concatenate([conv_tile(win, taps, j, q) for q in range(TILES)], 1)
        b = conv_tile(win, taps, j, TILES)
        state = state + dot_t(jnp.concatenate([b, b], 0), stacked(x.astype(F32) * tail, 2))
    send_ref[:STATE] = state.astype(BF16)
    ends = [got_ref[sources - 1, q * rows : (q + 1) * rows, :].astype(F32)[rows - TOP :] for q in range(TILES + 2)]
    ends += [jnp.zeros_like(ends[0])] * (TILES - 2)
    half = TOP // 2
    upper = pltpu.roll(jnp.concatenate(ends[:TILES], 1), half, 0)
    keep = iota((TOP, WIDE), 0) < half
    send_ref[STATE:] = jnp.where(keep, upper, jnp.concatenate(ends[TILES:], 1)).astype(BF16)
    if last_but_one:
        copy.wait()
    else:
        other_ref[...] = expand(jnp.broadcast_to(jnp.exp(after), (OWN, LANES)))[:8]


def local_body(
    got_ref, halo_ref, own_ref, c_ref, part_ref, growth_ref, factor_ref, tail_ref, top_ref, win, turn,
):
    _, _, blocks = sizes_of(got_ref)
    dts, cums = steps_of(got_ref, own_ref)
    taps = tiles_of(own_ref)
    fill(win, got_ref, halo_ref, TILES + 2)
    for q in range(TILES + 2):
        top_ref[q] = win[q, TOP : 2 * TOP]
    turn[...] = jnp.zeros_like(turn)
    for j in range(blocks):
        turn[j * OWN : (j + 1) * OWN] = cums[j]
    cols = turn[...].T
    t_at = iota((BLOCK, BLOCK), 0)
    s_at = iota((BLOCK, BLOCK), 1)
    left = iota((BLOCK, LANES), 1) < HEAD_DIM
    zero = jnp.zeros((BLOCK, LANES), BF16)
    past = jnp.zeros((OWN, 1), F32)
    local = None
    for j in range(blocks):
        at = j * BLOCK
        x = [conv_tile(win, taps, j, q) for q in range(TILES)]
        b = conv_tile(win, taps, j, TILES)
        c = conv_tile(win, taps, j, TILES + 1)
        c_ref[at : at + BLOCK] = c
        scores = lax.dot_general(c, b, (((1,), (1,)), ((), ())), preferred_element_type=F32)
        keep = t_at >= s_at
        if j == 0:
            keep = keep & (s_at >= TOP)
        scores = jnp.where(keep, scores, 0.0)
        cum, dt = cums[j], dts[j]
        last = cum[:, BLOCK - 1 :]
        grown = expand(jnp.exp(cum))
        if j > 1:
            past = past + cums[j - 1][:, BLOCK - 1 :]
        growth_ref[j] = jnp.exp(cum + past)
        if j > 0:
            carried = dot(jnp.concatenate([c, c], 1), stacked(local, 2)) * grown
        for q in range(TILES):
            lo = q * LANES
            mixes = []
            for h in (2 * q, 2 * q + 1):
                col = j * OWN + h
                gap = jnp.minimum(cols[:, col : col + 1] - cum[h : h + 1], 0.0)
                mixes.append((scores * jnp.exp(gap) * dt[h : h + 1]).astype(BF16))
            both = jnp.concatenate([jnp.where(left, x[q], zero), jnp.where(left, zero, x[q])], 0)
            part = dot(jnp.concatenate(mixes, 1), both)
            part_ref[at : at + BLOCK, lo : lo + LANES] = part if j == 0 else part + carried[:, lo : lo + LANES]
        tail = expand(jnp.exp(last - cum) * dt)
        if j == 0:
            tail_ref[...] = tail[:TOP]
            tail = jnp.where(iota((BLOCK, WIDE), 0) < TOP, 0.0, tail)
        if j + 1 < blocks:
            weighted = stacked(jnp.concatenate(x, 1).astype(F32) * tail, 2)
            fresh = dot_t(jnp.concatenate([b, b], 0), weighted)
            local = fresh if j == 0 else grown[BLOCK - 1 :] * local + fresh

    wide = OWN * TOP
    spread = one_hot(4 * OWN, TOP)
    cum_t = dot_t(stacked(cums[0], 4), spread)
    same = iota((TOP, wide), 0) == iota((TOP, wide), 1) % TOP
    cum_s = jnp.sum(jnp.where(same, cum_t[:TOP], 0.0), axis=0, keepdims=True)
    dt_s = jnp.sum(jnp.where(same, dot_t(stacked(dts[0], 4), spread)[:TOP], 0.0), axis=0, keepdims=True)
    decay = jnp.exp(jnp.minimum(cum_t - cum_s, 0.0))
    seen = iota((BLOCK, wide), 0) >= iota((BLOCK, wide), 1) % TOP
    factor_ref[0] = jnp.where(seen, decay, 0.0)
    factor_ref[1] = jnp.broadcast_to(dt_s, (BLOCK, wide))


def carry_body(before_ref, own_ref, c_ref, part_ref, growth_ref, factor_ref, tail_ref, top_ref, y_ref, win, c_first):
    blocks = c_ref.shape[0] // BLOCK
    taps = tiles_of(own_ref)
    first = TOP - taps[0].shape[0] + 1

    halo = before_ref[STATE:].astype(F32)
    upper = pltpu.roll(halo, TOP // 2, 0)
    tops = []
    for q in range(TILES + 2):
        lo = q * LANES
        win[q, :TOP] = upper[:, lo : lo + LANES] if q < TILES else halo[:, lo - WIDE : lo - WIDE + LANES]
        win[q, TOP:] = top_ref[q]
        done = conv(lambda k: win[q, first + k : first + k + TOP], taps[q])
        tops.append(done.astype(BF16).astype(F32))
    x_top = jnp.concatenate(tops[:TILES], 1)
    b_top = tops[TILES]
    b_twice = jnp.concatenate([b_top, b_top], 0).astype(BF16)
    head = dot_t(b_twice, stacked(x_top * tail_ref[...], 2))
    state = before_ref[:STATE]
    grown = expand(growth_ref[0])
    later = stacked(grown[BLOCK - 1 :] * state.astype(F32) + head, 2)

    c_first[...] = c_ref[:BLOCK].astype(F32)
    c_first[:TOP] = tops[TILES + 1]
    c = c_first[...].astype(BF16)
    wide = OWN * TOP
    scores = lax.dot_general(
        c, jnp.concatenate([b_top] * OWN, 0).astype(BF16), (((1,), (1,)), ((), ())), preferred_element_type=F32
    )
    mix = (scores * factor_ref[0] * factor_ref[1]).astype(BF16)
    shape = (wide, WIDE)
    own = iota(shape, 0) // TOP == iota(shape, 1) // HEAD_DIM
    added = dot(mix, jnp.where(own, jnp.concatenate([x_top] * OWN, 0), 0.0).astype(BF16))
    y_ref[:BLOCK] = (part_ref[:BLOCK] + added + dot(c, state) * grown).astype(BF16)
    for j in range(1, blocks):
        at = j * BLOCK
        c = c_ref[at : at + BLOCK]
        carried = dot(jnp.concatenate([c, c], 1), later)
        y_ref[at : at + BLOCK] = (part_ref[at : at + BLOCK] + carried * expand(growth_ref[j])).astype(BF16)


def norm_body(y_ref, z_ref, gain_ref, out_hbm, out_v, sem):
    count = y_ref.shape[0]
    per = count // GROUPS
    copies = []
    for g in range(GROUPS):
        gated = []
        square = 0.0
        for k in range(g * per, (g + 1) * per):
            v = y_ref[k].astype(F32) * silu(z_ref[:, k * WIDE : (k + 1) * WIDE].astype(F32))
            gated.append(v)
            square = square + jnp.sum(v * v, axis=1, keepdims=True)
        scale = lax.rsqrt(square / (per * WIDE) + eps_norm)
        for k in range(g * per, (g + 1) * per):
            at = k * WIDE
            gain = gain_ref[:, at : at + WIDE]
            out_v[:, at : at + WIDE] = (gated[k - g * per] * scale * gain).astype(BF16)
        part = pl.ds(g * per * WIDE, per * WIDE)
        copies.append(pltpu.make_async_copy(out_v.at[:, part], out_hbm.at[:, part], sem.at[g]))
        copies[-1].start()
    for copy in copies:
        copy.wait()


def shift(block, axis, distance):
    size = lax.axis_size(axis)
    return lax.ppermute(block, axis, [(i, i + distance) for i in range(size - distance)])


def kernel(body, name, ins, outs, scratch=(), cost=None, out_specs=None):
    return pl.pallas_call(
        body,
        in_specs=ins,
        out_specs=out_specs or [IN_VMEM] * len(outs),
        out_shape=outs,
        scratch_shapes=list(scratch),
        compiler_params=pltpu.CompilerParams(vmem_limit_bytes=16 * 2**20),
        cost_estimate=cost,
        name=name,
    )


def shards(x_in, b_in, c_in, dt_in, z_in, conv_x, input_state_taps, conv_c, dt_bias, a_log, norm_gain):
    outer, inner, head = (lax.axis_size(a) for a in ("outer", "inner", "head"))
    dests = inner * head
    rows = x_in.shape[0]
    tokens = rows * dests
    blocks = tokens // BLOCK
    mine = (lax.axis_index("inner") * head + lax.axis_index("head")).astype(jnp.int32).reshape(1)

    def of(dtype, *shape):
        return jax.ShapeDtypeStruct(shape, dtype)

    total = (TILES + 2) * rows + OWN
    lead = conv_x.shape[0]
    hbm = pl.BlockSpec(memory_space=pltpu.HBM)
    operands = (x_in, b_in, c_in, dt_in, conv_x, input_state_taps, conv_c, dt_bias.reshape(1, -1), a_log.reshape(1, -1))
    sent, own = kernel(
        pack_body, "pack", [IN_SMEM] + [hbm] * len(operands),
        [of(BF16, dests, total, LANES), of(F32, lead + 2 * OWN, WIDE + 2 * STATE)],
        [
            pltpu.VMEM(x_in.shape, BF16), pltpu.VMEM(b_in.shape, BF16), pltpu.VMEM(c_in.shape, BF16),
            pltpu.VMEM(dt_in.shape, BF16), pltpu.VMEM((BLOCK, LANES), F32),
            pltpu.VMEM((lead, WIDE), F32), pltpu.VMEM((2, lead, STATE), F32), pltpu.VMEM((2, 1, LANES), F32),
            pltpu.SemaphoreType.DMA((7,)), pltpu.SemaphoreType.DMA((5,)),
        ],
    )(mine, *(pltpu.with_memory_space_constraint(a, pltpu.HBM) for a in operands))

    def exchanged(array):
        return lax.all_to_all(array, ("inner", "head"), 0, 0, tiled=True)

    extra = STATE + TOP
    wide = OWN * TOP

    def total_of(got, halo):
        last_but_one = outer == 2
        return kernel(
            functools.partial(total_body, last_but_one=last_but_one), "total", [IN_VMEM] * 3,
            [of(BF16, extra, WIDE), of(BF16, *got.shape) if last_but_one else of(F32, 8, WIDE)],
            [pltpu.VMEM((TILES + 1, TOP + tokens, LANES), F32), pltpu.SemaphoreType.DMA],
            out_specs=[IN_VMEM, hbm if last_but_one else IN_VMEM],
        )(got, halo, own)

    def local_of(got, halo):
        return kernel(
            local_body, "local", [IN_VMEM] * 3,
            [
                of(BF16, tokens, STATE), of(F32, tokens, WIDE), of(F32, blocks, OWN, BLOCK), of(F32, 2, BLOCK, wide),
                of(F32, TOP, WIDE), of(F32, TILES + 2, TOP, LANES),
            ],
            [pltpu.VMEM((TILES + 2, TOP + tokens, LANES), F32), pltpu.VMEM((BLOCK, LANES), F32)],
            pl.CostEstimate(
                flops=2 * blocks * OWN * BLOCK * BLOCK * 160,
                bytes_accessed=tokens * WIDE * 12,
                transcendentals=blocks * OWN * BLOCK * BLOCK,
            ),
        )(got, halo, own)

    if outer == 2:
        halo = jnp.zeros((TOP, (TILES + 2) * LANES), F32)
        leads = lax.axis_index("outer") == 0
        send, kept = lax.cond(
            leads,
            lambda array: tuple(total_of(exchanged(array), halo)),
            lambda array: (jnp.zeros((extra, WIDE), BF16), array),
            sent,
        )
        before = shift(send, "outer", 1)
        c, part, growth, factor, tail, top = lax.cond(
            leads,
            lambda array, kept: tuple(local_of(kept, halo)),
            lambda array, kept: tuple(local_of(exchanged(array), halo)),
            sent, kept,
        )
    else:
        got = exchanged(sent)
        ends = got[-1, : (TILES + 2) * rows].reshape(TILES + 2, rows, LANES)[:, -TOP:]
        halo = shift(ends, "outer", 1).transpose(1, 0, 2).reshape(TOP, -1).astype(F32)
        send, fade = total_of(got, halo)
        before = shift(send, "outer", 1)
        entering, held, reach = before[:STATE].astype(F32), shift(fade, "outer", 1), 1
        while reach < outer - 1:
            entering = entering + held[:1] * shift(entering, "outer", reach)
            held = held * shift(held, "outer", reach)
            reach *= 2
        before = jnp.concatenate([entering.astype(BF16), before[STATE:]], 0)
        c, part, growth, factor, tail, top = local_of(got, halo)

    [y] = kernel(
        carry_body, "carry", [IN_VMEM] * 8, [of(BF16, tokens, WIDE)],
        [pltpu.VMEM((TILES + 2, 2 * TOP, LANES), F32), pltpu.VMEM((BLOCK, STATE), F32)],
    )(before, own, c, part, growth, factor, tail, top)

    home = lax.all_to_all(y.reshape(dests, rows, WIDE), ("inner", "head"), 0, 0, tiled=True)
    [out] = kernel(
        norm_body, "norm", [IN_VMEM] * 3, [of(BF16, rows, dests * WIDE)],
        [pltpu.VMEM((rows, dests * WIDE), BF16), pltpu.SemaphoreType.DMA((GROUPS,))], out_specs=[hbm],
    )(home, z_in, norm_gain.reshape(1, -1))
    return out


def solution(mesh):
    ctx, head = mesh.devices.shape
    inner = max(1, GROUPS * 16 // (OWN * head))
    cut = Mesh(mesh.devices.reshape(ctx // inner, inner, head), ("outer", "inner", "head"))
    rows = P(("outer", "inner", "head"), None)
    return jax.shard_map(
        shards,
        mesh=cut,
        in_specs=(rows,) * 5 + (P(),) * 6,
        out_specs=rows,
        check_vma=False,
    )
```

```python
import functools
import jax
import jax.numpy as jnp
from jax import lax
from jax.experimental import pallas as pl
from jax.experimental.pallas import tpu as pltpu
from jax.sharding import Mesh
from jax.sharding import PartitionSpec as P

HEAD_DIM = 64
STATE = 128
GROUPS = 8
BLOCK = 128
OWN = 8
WIDE = OWN * HEAD_DIM
LANES = 128
TILES = WIDE // LANES
TOP = 8

eps_norm = 1e-05
F32 = jnp.float32
BF16 = jnp.bfloat16
IN_VMEM = pl.BlockSpec(memory_space=pltpu.VMEM)
AXES = ("outer", "inner", "head")


def dot(a, b):
    return jnp.dot(a, b, preferred_element_type=F32)


def dot_t(a, b):
    return lax.dot_general(a, b, (((0,), (0,)), ((), ())), preferred_element_type=F32)


def iota(shape, axis):
    return lax.broadcasted_iota(jnp.int32, shape, axis)


def parts_of(values, count):
    out = []
    for k in range(count):
        piece = values.astype(BF16).astype(F32)
        out.append(piece)
        if k + 1 < count:
            values = values - piece
    return out


def stacked(values, count):
    return jnp.concatenate(parts_of(values, count), 0).astype(BF16)


def one_hot(rows, width):
    shape = (rows, OWN * width)
    return (iota(shape, 0) % OWN == iota(shape, 1) // width).astype(F32).astype(BF16)


def expand(values):
    return dot_t(stacked(values, 2), one_hot(2 * OWN, HEAD_DIM))


def silu(v):
    return v * jax.nn.sigmoid(v)


def conv(window, tap):
    total = tap[0:1] * window(0)
    for k in range(1, tap.shape[0]):
        total = total + tap[k : k + 1] * window(k)
    return silu(total)


def turned():
    return lax.rem(lax.axis_index("outer"), 2) * (lax.axis_size("inner") * lax.axis_size("head") // 2)


def holder(block, turn, count):
    return block + turn if block < count // 2 else block - turn


def tiles_of(own_ref):
    return [own_ref[:lead_of(own_ref), q * LANES : (q + 1) * LANES] for q in range(TILES + 2)]


def lead_of(own_ref):
    return own_ref.shape[0] - 2 * OWN


def pack_body(
    x_hbm, b_hbm, c_hbm, dt_hbm, tap_x, tap_b, tap_c, bias_hbm, log_hbm, gain_hbm,
    out_v, own_ref, gain_ref, x_v, b_v, c_v, dt_v, turn, x_tap, s_taps, heads_v, sem_in, sem_own,
):
    place = lax.axis_index("inner") * lax.axis_size("head") + lax.axis_index("head")
    count = out_v.shape[0]
    half_turn = turned()
    mine = lax.rem(place + half_turn, count)
    rows = x_v.shape[0]
    share = count * STATE // b_v.shape[1]
    cuts = 4
    step = count // cuts
    wide = step * WIDE
    small = [
        pltpu.make_async_copy(src, dst, sem_in.at[k])
        for k, (src, dst) in enumerate(((dt_hbm, dt_v), (b_hbm, b_v), (c_hbm, c_v)))
    ]
    large = [
        pltpu.make_async_copy(x_hbm.at[:, pl.ds(i * wide, wide)], x_v.at[:, pl.ds(i * wide, wide)], sem_in.at[3 + i])
        for i in range(cuts)
    ]
    at_x = pl.multiple_of(mine * WIDE, WIDE)
    at_s = pl.multiple_of(mine // share * STATE, STATE)
    own = [
        pltpu.make_async_copy(src, dst, sem_own.at[k])
        for k, (src, dst) in enumerate((
            (tap_x.at[:, pl.ds(at_x, WIDE)], x_tap),
            (tap_b.at[:, pl.ds(at_s, STATE)], s_taps.at[0]),
            (tap_c.at[:, pl.ds(at_s, STATE)], s_taps.at[1]),
            (bias_hbm, heads_v.at[0]),
            (log_hbm, heads_v.at[1]),
            (gain_hbm, gain_ref),
        ))
    ]
    for copy in small + large + own:
        copy.start()
    small[0].wait()
    turn[...] = jnp.zeros_like(turn)
    at = pl.multiple_of(lax.rem(place, BLOCK // rows) * rows, rows)
    turn[pl.ds(at, rows), :] = dt_v[...].astype(F32)
    heads = turn[...].T
    small[1].wait()
    small[2].wait()
    for block in range(count):
        k = holder(block, half_turn, count)
        at = block // share * STATE
        out_v[k, TILES * rows : (TILES + 1) * rows, :] = b_v[:, at : at + STATE]
        out_v[k, (TILES + 1) * rows : (TILES + 2) * rows, :] = c_v[:, at : at + STATE]
        out_v[k, (TILES + 2) * rows :, :] = heads[block * OWN : (block + 1) * OWN].astype(BF16)
    for i in range(cuts):
        large[i].wait()
        for block in range(i * step, (i + 1) * step):
            k = holder(block, half_turn, count)
            for q in range(TILES):
                lo = block * WIDE + q * LANES
                out_v[k, q * rows : (q + 1) * rows, :] = x_v[:, lo : lo + LANES]
    for copy in own:
        copy.wait()
    taps = x_tap.shape[0]
    own_ref[:taps, :WIDE] = x_tap[...]
    own_ref[:taps, WIDE : WIDE + STATE] = s_taps[0]
    own_ref[:taps, WIDE + STATE :] = s_taps[1]
    mask = iota((OWN, LANES), 0) + mine * OWN == iota((OWN, LANES), 1)
    for k in range(2):
        column = jnp.sum(jnp.where(mask, heads_v[k], 0.0), axis=1, keepdims=True)
        at = taps + k * OWN
        own_ref[at : at + OWN, :LANES] = jnp.broadcast_to(column, (OWN, LANES))


def sizes_of(got_ref):
    sources, total, _ = got_ref.shape
    rows = (total - OWN) // (TILES + 2)
    return sources, rows, sources * rows // BLOCK


def fill(win, got_ref, halo_ref, tiles):
    sources, rows, _ = sizes_of(got_ref)
    for q in range(tiles):
        win[q, :TOP] = halo_ref[:, q * LANES : (q + 1) * LANES]
        for s in range(sources):
            at = TOP + s * rows
            win[q, at : at + rows] = got_ref[s, q * rows : (q + 1) * rows, :].astype(F32)


def conv_tile(win, taps, j, q):
    first = j * BLOCK + TOP - taps[q].shape[0] + 1
    return conv(lambda k: win[q, first + k : first + k + BLOCK], taps[q]).astype(BF16)


def steps_of(got_ref, own_ref):
    _, rows, blocks = sizes_of(got_ref)
    per = BLOCK // rows
    lead = lead_of(own_ref)
    at = got_ref.shape[1] - OWN
    raws = []
    for j in range(blocks):
        raw = got_ref[j * per, at:, :].astype(F32)
        for s in range(1, per):
            raw = raw + got_ref[j * per + s, at:, :].astype(F32)
        raws.append(raw + own_ref[lead : lead + OWN, :LANES])
    raw = jnp.concatenate(raws, 0)
    dt = jnp.maximum(raw, 0.0) + jnp.log1p(jnp.exp(-jnp.abs(raw)))
    rate = jnp.concatenate([-jnp.exp(own_ref[lead + OWN :, :LANES])] * blocks, 0)
    upto = (iota((BLOCK, BLOCK), 0) <= iota((BLOCK, BLOCK), 1)).astype(F32).astype(BF16)
    sums = dot(stacked(dt * rate, 4), upto)
    n = blocks * OWN
    cum = sums[:n] + sums[n : 2 * n] + sums[2 * n : 3 * n] + sums[3 * n :]
    return [[v[j * OWN : (j + 1) * OWN] for j in range(blocks)] for v in (dt, cum)]


def total_body(got_ref, halo_ref, own_ref, send_ref, other_ref, win, sem, *, last_but_one):
    sources, rows, blocks = sizes_of(got_ref)
    if last_but_one:
        copy = pltpu.make_async_copy(got_ref, other_ref, sem)
        copy.start()
    dts, cums = steps_of(got_ref, own_ref)
    taps = tiles_of(own_ref)
    fill(win, got_ref, halo_ref, TILES + 1)
    state = jnp.zeros((STATE, WIDE), F32)
    after = jnp.zeros((OWN, 1), F32)
    for j in reversed(range(blocks)):
        after = after + cums[j][:, BLOCK - 1 :]
        tail = expand(jnp.exp(after - cums[j]) * dts[j])
        x = jnp.concatenate([conv_tile(win, taps, j, q) for q in range(TILES)], 1)
        b = conv_tile(win, taps, j, TILES)
        state = state + dot_t(jnp.concatenate([b, b], 0), stacked(x.astype(F32) * tail, 2))
    send_ref[:STATE] = state.astype(BF16)
    ends = [got_ref[sources - 1, q * rows : (q + 1) * rows, :].astype(F32)[rows - TOP :] for q in range(TILES + 2)]
    ends += [jnp.zeros_like(ends[0])] * (TILES - 2)
    half = TOP // 2
    upper = pltpu.roll(jnp.concatenate(ends[:TILES], 1), half, 0)
    keep = iota((TOP, WIDE), 0) < half
    send_ref[STATE:] = jnp.where(keep, upper, jnp.concatenate(ends[TILES:], 1)).astype(BF16)
    if last_but_one:
        copy.wait()
    else:
        other_ref[...] = expand(jnp.broadcast_to(jnp.exp(after), (OWN, LANES)))[:8]


def local_body(
    got_ref, halo_ref, own_ref, z_hbm,
    c_ref, part_ref, growth_ref, factor_ref, tail_ref, top_ref, z_ref, order_ref, win, turn, sem,
):
    fetch = pltpu.make_async_copy(z_hbm, z_ref, sem)
    fetch.start()
    _, _, blocks = sizes_of(got_ref)
    dts, cums = steps_of(got_ref, own_ref)
    taps = tiles_of(own_ref)
    fill(win, got_ref, halo_ref, TILES + 2)
    for q in range(TILES + 2):
        top_ref[q] = win[q, TOP : 2 * TOP]
    turn[...] = jnp.zeros_like(turn)
    for j in range(blocks):
        turn[j * OWN : (j + 1) * OWN] = cums[j]
    cols = turn[...].T
    t_at = iota((BLOCK, BLOCK), 0)
    s_at = iota((BLOCK, BLOCK), 1)
    left = iota((BLOCK, LANES), 1) < HEAD_DIM
    zero = jnp.zeros((BLOCK, LANES), BF16)
    past = jnp.zeros((OWN, 1), F32)
    local = None
    for j in range(blocks):
        at = j * BLOCK
        x = [conv_tile(win, taps, j, q) for q in range(TILES)]
        b = conv_tile(win, taps, j, TILES)
        c = conv_tile(win, taps, j, TILES + 1)
        c_ref[at : at + BLOCK] = c
        scores = lax.dot_general(c, b, (((1,), (1,)), ((), ())), preferred_element_type=F32)
        keep = t_at >= s_at
        if j == 0:
            keep = keep & (s_at >= TOP)
        scores = jnp.where(keep, scores, 0.0)
        cum, dt = cums[j], dts[j]
        last = cum[:, BLOCK - 1 :]
        grown = expand(jnp.exp(cum))
        if j > 1:
            past = past + cums[j - 1][:, BLOCK - 1 :]
        growth_ref[j] = jnp.exp(cum + past)
        if j > 0:
            carried = dot(jnp.concatenate([c, c], 1), stacked(local, 2)) * grown
        for q in range(TILES):
            lo = q * LANES
            mixes = []
            for h in (2 * q, 2 * q + 1):
                col = j * OWN + h
                gap = jnp.minimum(cols[:, col : col + 1] - cum[h : h + 1], 0.0)
                mixes.append((scores * jnp.exp(gap) * dt[h : h + 1]).astype(BF16))
            both = jnp.concatenate([jnp.where(left, x[q], zero), jnp.where(left, zero, x[q])], 0)
            part = dot(jnp.concatenate(mixes, 1), both)
            part_ref[at : at + BLOCK, lo : lo + LANES] = part if j == 0 else part + carried[:, lo : lo + LANES]
        tail = expand(jnp.exp(last - cum) * dt)
        if j == 0:
            tail_ref[...] = tail[:TOP]
            tail = jnp.where(iota((BLOCK, WIDE), 0) < TOP, 0.0, tail)
        if j + 1 < blocks:
            weighted = stacked(jnp.concatenate(x, 1).astype(F32) * tail, 2)
            fresh = dot_t(jnp.concatenate([b, b], 0), weighted)
            local = fresh if j == 0 else grown[BLOCK - 1 :] * local + fresh

    wide = OWN * TOP
    spread = one_hot(4 * OWN, TOP)
    cum_t = dot_t(stacked(cums[0], 4), spread)
    same = iota((TOP, wide), 0) == iota((TOP, wide), 1) % TOP
    cum_s = jnp.sum(jnp.where(same, cum_t[:TOP], 0.0), axis=0, keepdims=True)
    dt_s = jnp.sum(jnp.where(same, dot_t(stacked(dts[0], 4), spread)[:TOP], 0.0), axis=0, keepdims=True)
    decay = jnp.exp(jnp.minimum(cum_t - cum_s, 0.0))
    seen = iota((BLOCK, wide), 0) >= iota((BLOCK, wide), 1) % TOP
    factor_ref[0] = jnp.where(seen, decay, 0.0)
    factor_ref[1] = jnp.broadcast_to(dt_s, (BLOCK, wide))
    order_ref[...] = jnp.zeros_like(order_ref)
    fetch.wait()


def carry_body(before_ref, own_ref, c_ref, part_ref, growth_ref, factor_ref, tail_ref, top_ref, y_ref, win, c_first):
    blocks = c_ref.shape[0] // BLOCK
    taps = tiles_of(own_ref)
    first = TOP - taps[0].shape[0] + 1

    halo = before_ref[STATE:].astype(F32)
    upper = pltpu.roll(halo, TOP // 2, 0)
    tops = []
    for q in range(TILES + 2):
        lo = q * LANES
        win[q, :TOP] = upper[:, lo : lo + LANES] if q < TILES else halo[:, lo - WIDE : lo - WIDE + LANES]
        win[q, TOP:] = top_ref[q]
        done = conv(lambda k: win[q, first + k : first + k + TOP], taps[q])
        tops.append(done.astype(BF16).astype(F32))
    x_top = jnp.concatenate(tops[:TILES], 1)
    b_top = tops[TILES]
    b_twice = jnp.concatenate([b_top, b_top], 0).astype(BF16)
    head = dot_t(b_twice, stacked(x_top * tail_ref[...], 2))
    state = before_ref[:STATE]
    grown = expand(growth_ref[0])
    later = stacked(grown[BLOCK - 1 :] * state.astype(F32) + head, 2)

    c_first[...] = c_ref[:BLOCK].astype(F32)
    c_first[:TOP] = tops[TILES + 1]
    c = c_first[...].astype(BF16)
    wide = OWN * TOP
    scores = lax.dot_general(
        c, jnp.concatenate([b_top] * OWN, 0).astype(BF16), (((1,), (1,)), ((), ())), preferred_element_type=F32
    )
    mix = (scores * factor_ref[0] * factor_ref[1]).astype(BF16)
    shape = (wide, WIDE)
    own = iota(shape, 0) // TOP == iota(shape, 1) // HEAD_DIM
    added = dot(mix, jnp.where(own, jnp.concatenate([x_top] * OWN, 0), 0.0).astype(BF16))
    y_ref[:BLOCK] = (part_ref[:BLOCK] + added + dot(c, state) * grown).astype(BF16)
    for j in range(1, blocks):
        at = j * BLOCK
        c = c_ref[at : at + BLOCK]
        carried = dot(jnp.concatenate([c, c], 1), later)
        y_ref[at : at + BLOCK] = (part_ref[at : at + BLOCK] + carried * expand(growth_ref[j])).astype(BF16)


def unset_body(*refs):
    refs[-1][...] = jnp.zeros_like(refs[-1])


def norm_body(early_ref, late_ref, z_ref, gain_ref, out_hbm, out_v, sem):
    count = late_ref.shape[0]
    per = count // GROUPS
    leads = (lax.axis_index("outer") == 0) & (lax.axis_size("outer") == 2)
    half_turn = turned()
    copies = []
    for g in range(GROUPS):
        gated = []
        square = 0.0
        for k in range(g * per, (g + 1) * per):
            at = holder(k, half_turn, count)
            y = jnp.where(leads, early_ref[at].astype(F32), late_ref[at].astype(F32))
            v = y * silu(z_ref[:, k * WIDE : (k + 1) * WIDE].astype(F32))
            gated.append(v)
            square = square + jnp.sum(v * v, axis=1, keepdims=True)
        scale = lax.rsqrt(square / (per * WIDE) + eps_norm)
        for k in range(g * per, (g + 1) * per):
            at = k * WIDE
            gain = gain_ref[:, at : at + WIDE]
            out_v[:, at : at + WIDE] = (gated[k - g * per] * scale * gain).astype(BF16)
        part = pl.ds(g * per * WIDE, per * WIDE)
        copies.append(pltpu.make_async_copy(out_v.at[:, part], out_hbm.at[:, part], sem.at[g]))
        copies[-1].start()
    for copy in copies:
        copy.wait()


def shift(array, distance):
    outer, inner, head = (lax.axis_size(a) for a in AXES)
    count = inner * head

    def at(stretch, block):
        return stretch * count + holder(block, stretch % 2 * (count // 2), count)

    route = [(at(o, k), at(o + distance, k)) for o in range(outer - distance) for k in range(count)]
    return lax.ppermute(array, AXES, route)


def kernel(body, name, ins, outs, scratch=(), cost=None, out_specs=None):
    return pl.pallas_call(
        body,
        in_specs=ins,
        out_specs=out_specs or [IN_VMEM] * len(outs),
        out_shape=outs,
        scratch_shapes=list(scratch),
        compiler_params=pltpu.CompilerParams(vmem_limit_bytes=16 * 2**20),
        cost_estimate=cost,
        name=name,
    )


def shards(x_in, b_in, c_in, dt_in, z_in, conv_x, input_state_taps, conv_c, dt_bias, a_log, norm_gain):
    outer, inner, head = (lax.axis_size(a) for a in AXES)
    dests = inner * head
    rows = x_in.shape[0]
    tokens = rows * dests
    blocks = tokens // BLOCK

    def of(dtype, *shape):
        return jax.ShapeDtypeStruct(shape, dtype)

    total = (TILES + 2) * rows + OWN
    lead = conv_x.shape[0]
    hbm = pl.BlockSpec(memory_space=pltpu.HBM)
    rows_of = [v.reshape(1, -1) for v in (dt_bias, a_log, norm_gain)]
    operands = (x_in, b_in, c_in, dt_in, conv_x, input_state_taps, conv_c, *rows_of)
    z_pinned = pltpu.with_memory_space_constraint(z_in, pltpu.HBM)
    sent, own, gain = kernel(
        pack_body, "pack", [hbm] * len(operands),
        [of(BF16, dests, total, LANES), of(F32, lead + 2 * OWN, WIDE + 2 * STATE), of(F32, 1, norm_gain.size)],
        [
            pltpu.VMEM(x_in.shape, BF16), pltpu.VMEM(b_in.shape, BF16), pltpu.VMEM(c_in.shape, BF16),
            pltpu.VMEM(dt_in.shape, BF16), pltpu.VMEM((BLOCK, LANES), F32),
            pltpu.VMEM((lead, WIDE), F32), pltpu.VMEM((2, lead, STATE), F32), pltpu.VMEM((2, 1, LANES), F32),
            pltpu.SemaphoreType.DMA((7,)), pltpu.SemaphoreType.DMA((6,)),
        ],
    )(*(pltpu.with_memory_space_constraint(a, pltpu.HBM) for a in operands))

    def exchanged(array):
        return lax.all_to_all(array, ("inner", "head"), 0, 0, tiled=True)

    extra = STATE + TOP
    wide = OWN * TOP

    def total_of(got, halo):
        last_but_one = outer == 2
        return kernel(
            functools.partial(total_body, last_but_one=last_but_one), "total", [IN_VMEM] * 3,
            [pltpu.VMEM((extra, WIDE), BF16), of(BF16, *got.shape) if last_but_one else of(F32, 8, WIDE)],
            [pltpu.VMEM((TILES + 1, TOP + tokens, LANES), F32), pltpu.SemaphoreType.DMA],
            out_specs=[IN_VMEM, hbm if last_but_one else IN_VMEM],
        )(got, halo, own)

    def local_of(got, halo):
        return kernel(
            local_body, "local", [IN_VMEM] * 3 + [hbm],
            [
                of(BF16, tokens, STATE), of(F32, tokens, WIDE), of(F32, blocks, OWN, BLOCK), of(F32, 2, BLOCK, wide),
                of(F32, TOP, WIDE), of(F32, TILES + 2, TOP, LANES), of(BF16, *z_in.shape),
                of(F32, 8, LANES),
            ],
            [
                pltpu.VMEM((TILES + 2, TOP + tokens, LANES), F32), pltpu.VMEM((BLOCK, LANES), F32),
                pltpu.SemaphoreType.DMA,
            ],
            pl.CostEstimate(
                flops=2 * blocks * OWN * BLOCK * BLOCK * 160,
                bytes_accessed=tokens * WIDE * 12,
                transcendentals=blocks * OWN * BLOCK * BLOCK,
            ),
        )(got, halo, own, z_pinned)

    def unset(like, *after):
        return tuple(kernel(unset_body, "unset", [IN_VMEM] * len(after), [of(a.dtype, *a.shape) for a in like])(*after))

    def leaving(before, *done):
        [y] = kernel(
            carry_body, "carry", [IN_VMEM] * 8, [of(BF16, tokens, WIDE)],
            [pltpu.VMEM((TILES + 2, 2 * TOP, LANES), F32), pltpu.VMEM((BLOCK, STATE), F32)],
        )(before, own, *done)
        return exchanged(y.reshape(dests, rows, WIDE))

    if outer == 2:
        halo = jnp.zeros((TOP, (TILES + 2) * LANES), F32)
        leads = lax.axis_index("outer") == 0
        send, kept = lax.cond(
            leads,
            lambda array: tuple(total_of(exchanged(array), halo)),
            lambda array: unset([of(BF16, extra, WIDE), sent]),
            sent,
        )
        before = shift(send, 1)

        def first(array, kept):
            *done, z, order = local_of(kept, halo)
            *rest, nothing = unset([*done, send], order)
            return leaving(nothing, *done), tuple(rest), z

        def second(array, kept):
            *done, z, order = local_of(exchanged(array), halo)
            return unset([of(BF16, dests, rows, WIDE)], order)[0], tuple(done), z

        early, done, z = lax.cond(leads, first, second, sent, kept)
        late = lax.cond(
            leads,
            lambda before, done: unset([of(BF16, dests, rows, WIDE)])[0],
            lambda before, done: leaving(before, *done),
            before, done,
        )
    else:
        got = exchanged(sent)
        ends = got[-1, : (TILES + 2) * rows].reshape(TILES + 2, rows, LANES)[:, -TOP:]
        halo = shift(ends, 1).transpose(1, 0, 2).reshape(TOP, -1).astype(F32)
        send, fade = total_of(got, halo)
        before = shift(send, 1)
        entering, held, reach = before[:STATE].astype(F32), shift(fade, 1), 1
        while reach < outer - 1:
            entering = entering + held[:1] * shift(entering, reach)
            held = held * shift(held, reach)
            reach *= 2
        before = jnp.concatenate([entering.astype(BF16), before[STATE:]], 0)
        *done, z, _ = local_of(got, halo)
        early = late = leaving(before, *done)

    [out] = kernel(
        norm_body, "norm", [IN_VMEM] * 4, [of(BF16, rows, dests * WIDE)],
        [pltpu.VMEM((rows, dests * WIDE), BF16), pltpu.SemaphoreType.DMA((GROUPS,))], out_specs=[hbm],
    )(early, late, z, gain)
    return out


def solution(mesh):
    ctx, head = mesh.devices.shape
    inner = max(1, GROUPS * 16 // (OWN * head))
    cut = Mesh(mesh.devices.reshape(ctx // inner, inner, head), AXES)
    rows = P(AXES, None)
    return jax.shard_map(
        shards,
        mesh=cut,
        in_specs=(rows,) * 5 + (P(),) * 6,
        out_specs=rows,
        check_vma=False,
    )
```

```python
import functools
import jax
import jax.numpy as jnp
from jax import lax
from jax.experimental import pallas as pl
from jax.experimental.pallas import tpu as pltpu
from jax.sharding import Mesh
from jax.sharding import PartitionSpec as P

HEAD_DIM = 64
STATE = 128
GROUPS = 8
BLOCK = 128
OWN = 8
WIDE = OWN * HEAD_DIM
LANES = 128
TILES = WIDE // LANES
TOP = 8

eps_norm = 1e-05
F32 = jnp.float32
BF16 = jnp.bfloat16
IN_VMEM = pl.BlockSpec(memory_space=pltpu.VMEM)
AXES = ("outer", "inner", "head")


def dot(a, b):
    return jnp.dot(a, b, preferred_element_type=F32)


def dot_t(a, b):
    return lax.dot_general(a, b, (((0,), (0,)), ((), ())), preferred_element_type=F32)


def iota(shape, axis):
    return lax.broadcasted_iota(jnp.int32, shape, axis)


def parts_of(values, count):
    out = []
    for k in range(count):
        piece = values.astype(BF16).astype(F32)
        out.append(piece)
        if k + 1 < count:
            values = values - piece
    return out


def stacked(values, count):
    return jnp.concatenate(parts_of(values, count), 0).astype(BF16)


def one_hot(rows, width):
    shape = (rows, OWN * width)
    return (iota(shape, 0) % OWN == iota(shape, 1) // width).astype(F32).astype(BF16)


def expand(values):
    return dot_t(stacked(values, 2), one_hot(2 * OWN, HEAD_DIM))


def silu(v):
    return v * jax.nn.sigmoid(v)


def conv(window, tap):
    total = tap[0:1] * window(0)
    for k in range(1, tap.shape[0]):
        total = total + tap[k : k + 1] * window(k)
    return silu(total)


def turned():
    return lax.rem(lax.axis_index("outer"), 2) * (lax.axis_size("inner") * lax.axis_size("head") // 2)


def holder(block, turn, count):
    return block + turn if block < count // 2 else block - turn


def tiles_of(own_ref):
    return [own_ref[:lead_of(own_ref), q * LANES : (q + 1) * LANES] for q in range(TILES + 2)]


def lead_of(own_ref):
    return own_ref.shape[0] - 2 * OWN


def pack_body(
    x_hbm, b_hbm, c_hbm, dt_hbm, tap_x, tap_b, tap_c, bias_hbm, log_hbm, gain_hbm,
    out_v, own_ref, gain_ref, x_v, b_v, c_v, dt_v, turn, x_tap, s_taps, heads_v, sem_in, sem_own,
):
    place = lax.axis_index("inner") * lax.axis_size("head") + lax.axis_index("head")
    count = out_v.shape[0]
    half_turn = turned()
    mine = lax.rem(place + half_turn, count)
    rows = x_v.shape[0]
    share = count * STATE // b_v.shape[1]
    cuts = 4
    step = count // cuts
    wide = step * WIDE
    small = [
        pltpu.make_async_copy(src, dst, sem_in.at[k])
        for k, (src, dst) in enumerate(((dt_hbm, dt_v), (b_hbm, b_v), (c_hbm, c_v)))
    ]
    large = [
        pltpu.make_async_copy(x_hbm.at[:, pl.ds(i * wide, wide)], x_v.at[:, pl.ds(i * wide, wide)], sem_in.at[3 + i])
        for i in range(cuts)
    ]
    at_x = pl.multiple_of(mine * WIDE, WIDE)
    at_s = pl.multiple_of(mine // share * STATE, STATE)
    own = [
        pltpu.make_async_copy(src, dst, sem_own.at[k])
        for k, (src, dst) in enumerate((
            (tap_x.at[:, pl.ds(at_x, WIDE)], x_tap),
            (tap_b.at[:, pl.ds(at_s, STATE)], s_taps.at[0]),
            (tap_c.at[:, pl.ds(at_s, STATE)], s_taps.at[1]),
            (bias_hbm, heads_v.at[0]),
            (log_hbm, heads_v.at[1]),
            (gain_hbm, gain_ref),
        ))
    ]
    for copy in small + large + own:
        copy.start()
    small[0].wait()
    turn[...] = jnp.zeros_like(turn)
    at = pl.multiple_of(lax.rem(place, BLOCK // rows) * rows, rows)
    turn[pl.ds(at, rows), :] = dt_v[...].astype(F32)
    heads = turn[...].T
    small[1].wait()
    small[2].wait()
    for block in range(count):
        k = holder(block, half_turn, count)
        at = block // share * STATE
        out_v[k, TILES * rows : (TILES + 1) * rows, :] = b_v[:, at : at + STATE]
        out_v[k, (TILES + 1) * rows : (TILES + 2) * rows, :] = c_v[:, at : at + STATE]
        out_v[k, (TILES + 2) * rows :, :] = heads[block * OWN : (block + 1) * OWN].astype(BF16)
    for i in range(cuts):
        large[i].wait()
        for block in range(i * step, (i + 1) * step):
            k = holder(block, half_turn, count)
            for q in range(TILES):
                lo = block * WIDE + q * LANES
                out_v[k, q * rows : (q + 1) * rows, :] = x_v[:, lo : lo + LANES]
    for copy in own:
        copy.wait()
    taps = x_tap.shape[0]
    own_ref[:taps, :WIDE] = x_tap[...]
    own_ref[:taps, WIDE : WIDE + STATE] = s_taps[0]
    own_ref[:taps, WIDE + STATE :] = s_taps[1]
    mask = iota((OWN, LANES), 0) + mine * OWN == iota((OWN, LANES), 1)
    for k in range(2):
        column = jnp.sum(jnp.where(mask, heads_v[k], 0.0), axis=1, keepdims=True)
        at = taps + k * OWN
        own_ref[at : at + OWN, :LANES] = jnp.broadcast_to(column, (OWN, LANES))


def sizes_of(got_ref):
    sources, total, _ = got_ref.shape
    rows = (total - OWN) // (TILES + 2)
    return sources, rows, sources * rows // BLOCK


def fill(win, got_ref, halo_ref, tiles):
    sources, rows, _ = sizes_of(got_ref)
    for q in range(tiles):
        win[q, :TOP] = halo_ref[:, q * LANES : (q + 1) * LANES]
        for s in range(sources):
            at = TOP + s * rows
            win[q, at : at + rows] = got_ref[s, q * rows : (q + 1) * rows, :].astype(F32)


def conv_tile(win, taps, j, q):
    first = j * BLOCK + TOP - taps[q].shape[0] + 1
    return conv(lambda k: win[q, first + k : first + k + BLOCK], taps[q]).astype(BF16)


def steps_of(got_ref, own_ref):
    _, rows, blocks = sizes_of(got_ref)
    per = BLOCK // rows
    lead = lead_of(own_ref)
    at = got_ref.shape[1] - OWN
    raws = []
    for j in range(blocks):
        raw = got_ref[j * per, at:, :].astype(F32)
        for s in range(1, per):
            raw = raw + got_ref[j * per + s, at:, :].astype(F32)
        raws.append(raw + own_ref[lead : lead + OWN, :LANES])
    raw = jnp.concatenate(raws, 0)
    dt = jnp.maximum(raw, 0.0) + jnp.log1p(jnp.exp(-jnp.abs(raw)))
    rate = jnp.concatenate([-jnp.exp(own_ref[lead + OWN :, :LANES])] * blocks, 0)
    upto = (iota((BLOCK, BLOCK), 0) <= iota((BLOCK, BLOCK), 1)).astype(F32).astype(BF16)
    sums = dot(stacked(dt * rate, 4), upto)
    n = blocks * OWN
    cum = sums[:n] + sums[n : 2 * n] + sums[2 * n : 3 * n] + sums[3 * n :]
    return [[v[j * OWN : (j + 1) * OWN] for j in range(blocks)] for v in (dt, cum)]


def total_body(got_ref, halo_ref, own_ref, send_ref, other_ref, win, sem, *, last_but_one):
    sources, rows, blocks = sizes_of(got_ref)
    if last_but_one:
        copy = pltpu.make_async_copy(got_ref, other_ref, sem)
        copy.start()
    dts, cums = steps_of(got_ref, own_ref)
    taps = tiles_of(own_ref)
    fill(win, got_ref, halo_ref, TILES + 1)
    state = jnp.zeros((STATE, WIDE), F32)
    after = jnp.zeros((OWN, 1), F32)
    for j in reversed(range(blocks)):
        after = after + cums[j][:, BLOCK - 1 :]
        tail = expand(jnp.exp(after - cums[j]) * dts[j])
        x = jnp.concatenate([conv_tile(win, taps, j, q) for q in range(TILES)], 1)
        b = conv_tile(win, taps, j, TILES)
        state = state + dot_t(jnp.concatenate([b, b], 0), stacked(x.astype(F32) * tail, 2))
    send_ref[:STATE] = state.astype(BF16)
    ends = [got_ref[sources - 1, q * rows : (q + 1) * rows, :].astype(F32)[rows - TOP :] for q in range(TILES + 2)]
    ends += [jnp.zeros_like(ends[0])] * (TILES - 2)
    half = TOP // 2
    upper = pltpu.roll(jnp.concatenate(ends[:TILES], 1), half, 0)
    keep = iota((TOP, WIDE), 0) < half
    send_ref[STATE:] = jnp.where(keep, upper, jnp.concatenate(ends[TILES:], 1)).astype(BF16)
    if last_but_one:
        copy.wait()
    else:
        other_ref[...] = expand(jnp.broadcast_to(jnp.exp(after), (OWN, LANES)))[:8]


def local_body(
    got_ref, halo_ref, own_ref, z_hbm,
    c_ref, part_ref, growth_ref, factor_ref, tail_ref, top_ref, gate_ref, order_ref, win, turn, z_ref, sem,
):
    fetch = pltpu.make_async_copy(z_hbm, z_ref, sem)
    fetch.start()
    _, _, blocks = sizes_of(got_ref)
    dts, cums = steps_of(got_ref, own_ref)
    taps = tiles_of(own_ref)
    fill(win, got_ref, halo_ref, TILES + 2)
    for q in range(TILES + 2):
        top_ref[q] = win[q, TOP : 2 * TOP]
    turn[...] = jnp.zeros_like(turn)
    for j in range(blocks):
        turn[j * OWN : (j + 1) * OWN] = cums[j]
    cols = turn[...].T
    t_at = iota((BLOCK, BLOCK), 0)
    s_at = iota((BLOCK, BLOCK), 1)
    left = iota((BLOCK, LANES), 1) < HEAD_DIM
    zero = jnp.zeros((BLOCK, LANES), BF16)
    past = jnp.zeros((OWN, 1), F32)
    local = None
    for j in range(blocks):
        at = j * BLOCK
        x = [conv_tile(win, taps, j, q) for q in range(TILES)]
        b = conv_tile(win, taps, j, TILES)
        c = conv_tile(win, taps, j, TILES + 1)
        c_ref[at : at + BLOCK] = c
        scores = lax.dot_general(c, b, (((1,), (1,)), ((), ())), preferred_element_type=F32)
        keep = t_at >= s_at
        if j == 0:
            keep = keep & (s_at >= TOP)
        scores = jnp.where(keep, scores, 0.0)
        cum, dt = cums[j], dts[j]
        last = cum[:, BLOCK - 1 :]
        grown = expand(jnp.exp(cum))
        if j > 1:
            past = past + cums[j - 1][:, BLOCK - 1 :]
        growth_ref[at : at + BLOCK] = expand(jnp.exp(cum + past)) if j > 1 else grown
        if j > 0:
            carried = dot(jnp.concatenate([c, c], 1), stacked(local, 2)) * grown
        for q in range(TILES):
            lo = q * LANES
            mixes = []
            for h in (2 * q, 2 * q + 1):
                col = j * OWN + h
                gap = jnp.minimum(cols[:, col : col + 1] - cum[h : h + 1], 0.0)
                mixes.append((scores * jnp.exp(gap) * dt[h : h + 1]).astype(BF16))
            both = jnp.concatenate([jnp.where(left, x[q], zero), jnp.where(left, zero, x[q])], 0)
            part = dot(jnp.concatenate(mixes, 1), both)
            part_ref[at : at + BLOCK, lo : lo + LANES] = part if j == 0 else part + carried[:, lo : lo + LANES]
        tail = expand(jnp.exp(last - cum) * dt)
        if j == 0:
            tail_ref[...] = tail[:TOP]
            tail = jnp.where(iota((BLOCK, WIDE), 0) < TOP, 0.0, tail)
        if j + 1 < blocks:
            weighted = stacked(jnp.concatenate(x, 1).astype(F32) * tail, 2)
            fresh = dot_t(jnp.concatenate([b, b], 0), weighted)
            local = fresh if j == 0 else grown[BLOCK - 1 :] * local + fresh

    wide = OWN * TOP
    spread = one_hot(4 * OWN, TOP)
    cum_t = dot_t(stacked(cums[0], 4), spread)
    same = iota((TOP, wide), 0) == iota((TOP, wide), 1) % TOP
    cum_s = jnp.sum(jnp.where(same, cum_t[:TOP], 0.0), axis=0, keepdims=True)
    dt_s = jnp.sum(jnp.where(same, dot_t(stacked(dts[0], 4), spread)[:TOP], 0.0), axis=0, keepdims=True)
    decay = jnp.exp(jnp.minimum(cum_t - cum_s, 0.0))
    seen = iota((BLOCK, wide), 0) >= iota((BLOCK, wide), 1) % TOP
    factor_ref[0] = jnp.where(seen, decay, 0.0)
    factor_ref[1] = jnp.broadcast_to(dt_s, (BLOCK, wide))
    order_ref[...] = jnp.zeros_like(order_ref)
    fetch.wait()
    for lo in range(0, z_ref.shape[1], WIDE):
        gate_ref[:, lo : lo + WIDE] = silu(z_ref[:, lo : lo + WIDE].astype(F32))


def carry_body(before_ref, own_ref, c_ref, part_ref, growth_ref, factor_ref, tail_ref, top_ref, y_ref, win, c_first):
    blocks = c_ref.shape[0] // BLOCK
    taps = tiles_of(own_ref)
    first = TOP - taps[0].shape[0] + 1

    halo = before_ref[STATE:].astype(F32)
    upper = pltpu.roll(halo, TOP // 2, 0)
    tops = []
    for q in range(TILES + 2):
        lo = q * LANES
        win[q, :TOP] = upper[:, lo : lo + LANES] if q < TILES else halo[:, lo - WIDE : lo - WIDE + LANES]
        win[q, TOP:] = top_ref[q]
        done = conv(lambda k: win[q, first + k : first + k + TOP], taps[q])
        tops.append(done.astype(BF16).astype(F32))
    x_top = jnp.concatenate(tops[:TILES], 1)
    b_top = tops[TILES]
    b_twice = jnp.concatenate([b_top, b_top], 0).astype(BF16)
    head = dot_t(b_twice, stacked(x_top * tail_ref[...], 2))
    state = before_ref[:STATE]
    grown = growth_ref[:BLOCK]
    later = stacked(grown[BLOCK - 1 :] * state.astype(F32) + head, 2)

    c_first[...] = c_ref[:BLOCK].astype(F32)
    c_first[:TOP] = tops[TILES + 1]
    c = c_first[...].astype(BF16)
    wide = OWN * TOP
    scores = lax.dot_general(
        c, jnp.concatenate([b_top] * OWN, 0).astype(BF16), (((1,), (1,)), ((), ())), preferred_element_type=F32
    )
    mix = (scores * factor_ref[0] * factor_ref[1]).astype(BF16)
    shape = (wide, WIDE)
    own = iota(shape, 0) // TOP == iota(shape, 1) // HEAD_DIM
    added = dot(mix, jnp.where(own, jnp.concatenate([x_top] * OWN, 0), 0.0).astype(BF16))
    y_ref[:BLOCK] = (part_ref[:BLOCK] + added + dot(c, state) * grown).astype(BF16)
    for j in range(1, blocks):
        at = j * BLOCK
        c = c_ref[at : at + BLOCK]
        carried = dot(jnp.concatenate([c, c], 1), later)
        y_ref[at : at + BLOCK] = (part_ref[at : at + BLOCK] + carried * growth_ref[at : at + BLOCK]).astype(BF16)


def unset_body(*refs):
    refs[-1][...] = jnp.zeros_like(refs[-1])


def norm_body(early_ref, late_ref, gate_ref, gain_ref, out_hbm, out_v, sem):
    count = late_ref.shape[0]
    per = count // GROUPS
    leads = (lax.axis_index("outer") == 0) & (lax.axis_size("outer") == 2)
    half_turn = turned()
    copies = []
    for g in range(GROUPS):
        gated = []
        square = 0.0
        for k in range(g * per, (g + 1) * per):
            at = holder(k, half_turn, count)
            y = jnp.where(leads, early_ref[at].astype(F32), late_ref[at].astype(F32))
            v = y * gate_ref[:, k * WIDE : (k + 1) * WIDE]
            gated.append(v)
            square = square + jnp.sum(v * v, axis=1, keepdims=True)
        scale = lax.rsqrt(square / (per * WIDE) + eps_norm)
        for k in range(g * per, (g + 1) * per):
            at = k * WIDE
            gain = gain_ref[:, at : at + WIDE]
            out_v[:, at : at + WIDE] = (gated[k - g * per] * scale * gain).astype(BF16)
        part = pl.ds(g * per * WIDE, per * WIDE)
        copies.append(pltpu.make_async_copy(out_v.at[:, part], out_hbm.at[:, part], sem.at[g]))
        copies[-1].start()
    for copy in copies:
        copy.wait()


def shift(array, distance):
    outer, inner, head = (lax.axis_size(a) for a in AXES)
    count = inner * head

    def at(stretch, block):
        return stretch * count + holder(block, stretch % 2 * (count // 2), count)

    route = [(at(o, k), at(o + distance, k)) for o in range(outer - distance) for k in range(count)]
    return lax.ppermute(array, AXES, route)


def kernel(body, name, ins, outs, scratch=(), cost=None, out_specs=None):
    return pl.pallas_call(
        body,
        in_specs=ins,
        out_specs=out_specs or [IN_VMEM] * len(outs),
        out_shape=outs,
        scratch_shapes=list(scratch),
        compiler_params=pltpu.CompilerParams(vmem_limit_bytes=16 * 2**20),
        cost_estimate=cost,
        name=name,
    )


def shards(x_in, b_in, c_in, dt_in, z_in, conv_x, input_state_taps, conv_c, dt_bias, a_log, norm_gain):
    outer, inner, head = (lax.axis_size(a) for a in AXES)
    dests = inner * head
    rows = x_in.shape[0]
    tokens = rows * dests
    blocks = tokens // BLOCK

    def of(dtype, *shape):
        return jax.ShapeDtypeStruct(shape, dtype)

    total = (TILES + 2) * rows + OWN
    lead = conv_x.shape[0]
    hbm = pl.BlockSpec(memory_space=pltpu.HBM)
    rows_of = [v.reshape(1, -1) for v in (dt_bias, a_log, norm_gain)]
    operands = (x_in, b_in, c_in, dt_in, conv_x, input_state_taps, conv_c, *rows_of)
    z_pinned = pltpu.with_memory_space_constraint(z_in, pltpu.HBM)
    sent, own, gain = kernel(
        pack_body, "pack", [hbm] * len(operands),
        [of(BF16, dests, total, LANES), of(F32, lead + 2 * OWN, WIDE + 2 * STATE), of(F32, 1, norm_gain.size)],
        [
            pltpu.VMEM(x_in.shape, BF16), pltpu.VMEM(b_in.shape, BF16), pltpu.VMEM(c_in.shape, BF16),
            pltpu.VMEM(dt_in.shape, BF16), pltpu.VMEM((BLOCK, LANES), F32),
            pltpu.VMEM((lead, WIDE), F32), pltpu.VMEM((2, lead, STATE), F32), pltpu.VMEM((2, 1, LANES), F32),
            pltpu.SemaphoreType.DMA((7,)), pltpu.SemaphoreType.DMA((6,)),
        ],
    )(*(pltpu.with_memory_space_constraint(a, pltpu.HBM) for a in operands))

    def exchanged(array):
        return lax.all_to_all(array, ("inner", "head"), 0, 0, tiled=True)

    extra = STATE + TOP
    wide = OWN * TOP

    def total_of(got, halo):
        last_but_one = outer == 2
        return kernel(
            functools.partial(total_body, last_but_one=last_but_one), "total", [IN_VMEM] * 3,
            [pltpu.VMEM((extra, WIDE), BF16), of(BF16, *got.shape) if last_but_one else of(F32, 8, WIDE)],
            [pltpu.VMEM((TILES + 1, TOP + tokens, LANES), F32), pltpu.SemaphoreType.DMA],
            out_specs=[IN_VMEM, hbm if last_but_one else IN_VMEM],
        )(got, halo, own)

    def local_of(got, halo):
        return kernel(
            local_body, "local", [IN_VMEM] * 3 + [hbm],
            [
                of(BF16, tokens, STATE), of(F32, tokens, WIDE), pltpu.VMEM((tokens, WIDE), F32), of(F32, 2, BLOCK, wide),
                of(F32, TOP, WIDE), of(F32, TILES + 2, TOP, LANES), pltpu.VMEM(z_in.shape, F32),
                of(F32, 8, LANES),
            ],
            [
                pltpu.VMEM((TILES + 2, TOP + tokens, LANES), F32), pltpu.VMEM((BLOCK, LANES), F32),
                pltpu.VMEM(z_in.shape, BF16), pltpu.SemaphoreType.DMA,
            ],
            pl.CostEstimate(
                flops=2 * blocks * OWN * BLOCK * BLOCK * 160,
                bytes_accessed=tokens * WIDE * 12,
                transcendentals=blocks * OWN * BLOCK * BLOCK,
            ),
        )(got, halo, own, z_pinned)

    def unset(like, *after):
        return tuple(kernel(unset_body, "unset", [IN_VMEM] * len(after), [of(a.dtype, *a.shape) for a in like])(*after))

    def leaving(before, *done):
        [y] = kernel(
            carry_body, "carry", [IN_VMEM] * 8, [of(BF16, tokens, WIDE)],
            [pltpu.VMEM((TILES + 2, 2 * TOP, LANES), F32), pltpu.VMEM((BLOCK, STATE), F32)],
        )(before, own, *done)
        return exchanged(y.reshape(dests, rows, WIDE))

    if outer == 2:
        halo = jnp.zeros((TOP, (TILES + 2) * LANES), F32)
        leads = lax.axis_index("outer") == 0
        send, kept = lax.cond(
            leads,
            lambda array: tuple(total_of(exchanged(array), halo)),
            lambda array: unset([of(BF16, extra, WIDE), sent]),
            sent,
        )
        before = shift(send, 1)

        def first(array, kept):
            *done, gate, order = local_of(kept, halo)
            *rest, nothing = unset([*done, send], order)
            return leaving(nothing, *done), tuple(rest), gate

        def second(array, kept):
            *done, gate, order = local_of(exchanged(array), halo)
            return unset([of(BF16, dests, rows, WIDE)], order)[0], tuple(done), gate

        early, done, gate = lax.cond(leads, first, second, sent, kept)
        late = lax.cond(
            leads,
            lambda before, done: unset([of(BF16, dests, rows, WIDE)])[0],
            lambda before, done: leaving(before, *done),
            before, done,
        )
    else:
        got = exchanged(sent)
        ends = got[-1, : (TILES + 2) * rows].reshape(TILES + 2, rows, LANES)[:, -TOP:]
        halo = shift(ends, 1).transpose(1, 0, 2).reshape(TOP, -1).astype(F32)
        send, fade = total_of(got, halo)
        before = shift(send, 1)
        entering, held, reach = before[:STATE].astype(F32), shift(fade, 1), 1
        while reach < outer - 1:
            entering = entering + held[:1] * shift(entering, reach)
            held = held * shift(held, reach)
            reach *= 2
        before = jnp.concatenate([entering.astype(BF16), before[STATE:]], 0)
        *done, gate, _ = local_of(got, halo)
        early = late = leaving(before, *done)

    [out] = kernel(
        norm_body, "norm", [IN_VMEM] * 4, [of(BF16, rows, dests * WIDE)],
        [pltpu.VMEM((rows, dests * WIDE), BF16), pltpu.SemaphoreType.DMA((GROUPS,))], out_specs=[hbm],
    )(early, late, gate, gain)
    return out


def solution(mesh):
    ctx, head = mesh.devices.shape
    inner = max(1, GROUPS * 16 // (OWN * head))
    cut = Mesh(mesh.devices.reshape(ctx // inner, inner, head), AXES)
    rows = P(AXES, None)
    return jax.shard_map(
        shards,
        mesh=cut,
        in_specs=(rows,) * 5 + (P(),) * 6,
        out_specs=rows,
        check_vma=False,
    )
```

```python
import functools
import jax
import jax.numpy as jnp
from jax import lax
from jax.experimental import pallas as pl
from jax.experimental.pallas import tpu as pltpu
from jax.sharding import Mesh
from jax.sharding import PartitionSpec as P

HEAD_DIM = 64
STATE = 128
GROUPS = 8
BLOCK = 128
OWN = 8
WIDE = OWN * HEAD_DIM
LANES = 128
TILES = WIDE // LANES
TOP = 8

eps_norm = 1e-05
F32 = jnp.float32
BF16 = jnp.bfloat16
IN_VMEM = pl.BlockSpec(memory_space=pltpu.VMEM)
AXES = ("outer", "inner", "head")


def dot(a, b):
    return jnp.dot(a, b, preferred_element_type=F32)


def dot_t(a, b):
    return lax.dot_general(a, b, (((0,), (0,)), ((), ())), preferred_element_type=F32)


def iota(shape, axis):
    return lax.broadcasted_iota(jnp.int32, shape, axis)


def parts_of(values, count):
    out = []
    for k in range(count):
        piece = values.astype(BF16).astype(F32)
        out.append(piece)
        if k + 1 < count:
            values = values - piece
    return out


def stacked(values, count):
    return jnp.concatenate(parts_of(values, count), 0).astype(BF16)


def one_hot(rows, width):
    shape = (rows, OWN * width)
    return (iota(shape, 0) % OWN == iota(shape, 1) // width).astype(F32).astype(BF16)


def expand(values):
    return dot_t(stacked(values, 2), one_hot(2 * OWN, HEAD_DIM))


def silu(v):
    return v * jax.nn.sigmoid(v)


def conv(window, tap):
    total = tap[0:1] * window(0)
    for k in range(1, tap.shape[0]):
        total = total + tap[k : k + 1] * window(k)
    return silu(total)


def turned():
    return lax.rem(lax.axis_index("outer"), 2) * (lax.axis_size("inner") * lax.axis_size("head") // 2)


def holder(block, turn, count):
    return block + turn if block < count // 2 else block - turn


def tiles_of(own_ref):
    return [own_ref[:lead_of(own_ref), q * LANES : (q + 1) * LANES] for q in range(TILES + 2)]


def lead_of(own_ref):
    return own_ref.shape[0] - 2 * OWN


def pack_body(
    x_hbm, b_hbm, c_hbm, dt_hbm, tap_x, tap_b, tap_c, bias_hbm, log_hbm, gain_hbm,
    out_v, own_ref, gain_ref, x_v, b_v, c_v, dt_v, turn, x_tap, s_taps, heads_v, sem_in, sem_own,
):
    place = lax.axis_index("inner") * lax.axis_size("head") + lax.axis_index("head")
    count = out_v.shape[0]
    half_turn = turned()
    mine = lax.rem(place + half_turn, count)
    rows = x_v.shape[0]
    share = count * STATE // b_v.shape[1]
    cuts = 4
    step = count // cuts
    wide = step * WIDE
    small = [
        pltpu.make_async_copy(src, dst, sem_in.at[k])
        for k, (src, dst) in enumerate(((dt_hbm, dt_v), (b_hbm, b_v), (c_hbm, c_v)))
    ]
    large = [
        pltpu.make_async_copy(x_hbm.at[:, pl.ds(i * wide, wide)], x_v.at[:, pl.ds(i * wide, wide)], sem_in.at[3 + i])
        for i in range(cuts)
    ]
    at_x = pl.multiple_of(mine * WIDE, WIDE)
    at_s = pl.multiple_of(mine // share * STATE, STATE)
    own = [
        pltpu.make_async_copy(src, dst, sem_own.at[k])
        for k, (src, dst) in enumerate((
            (tap_x.at[:, pl.ds(at_x, WIDE)], x_tap),
            (tap_b.at[:, pl.ds(at_s, STATE)], s_taps.at[0]),
            (tap_c.at[:, pl.ds(at_s, STATE)], s_taps.at[1]),
            (bias_hbm, heads_v.at[0]),
            (log_hbm, heads_v.at[1]),
            (gain_hbm, gain_ref),
        ))
    ]
    for copy in small + large + own:
        copy.start()
    small[0].wait()
    turn[...] = jnp.zeros_like(turn)
    at = pl.multiple_of(lax.rem(place, BLOCK // rows) * rows, rows)
    turn[pl.ds(at, rows), :] = dt_v[...].astype(F32)
    heads = turn[...].T
    small[1].wait()
    small[2].wait()
    for block in range(count):
        k = holder(block, half_turn, count)
        at = block // share * STATE
        out_v[k, TILES * rows : (TILES + 1) * rows, :] = b_v[:, at : at + STATE]
        out_v[k, (TILES + 1) * rows : (TILES + 2) * rows, :] = c_v[:, at : at + STATE]
        out_v[k, (TILES + 2) * rows :, :] = heads[block * OWN : (block + 1) * OWN].astype(BF16)
    for i in range(cuts):
        large[i].wait()
        for block in range(i * step, (i + 1) * step):
            k = holder(block, half_turn, count)
            for q in range(TILES):
                lo = block * WIDE + q * LANES
                out_v[k, q * rows : (q + 1) * rows, :] = x_v[:, lo : lo + LANES]
    for copy in own:
        copy.wait()
    taps = x_tap.shape[0]
    own_ref[:taps, :WIDE] = x_tap[...]
    own_ref[:taps, WIDE : WIDE + STATE] = s_taps[0]
    own_ref[:taps, WIDE + STATE :] = s_taps[1]
    mask = iota((OWN, LANES), 0) + mine * OWN == iota((OWN, LANES), 1)
    for k in range(2):
        column = jnp.sum(jnp.where(mask, heads_v[k], 0.0), axis=1, keepdims=True)
        at = taps + k * OWN
        own_ref[at : at + OWN, :LANES] = jnp.broadcast_to(column, (OWN, LANES))


def sizes_of(got_ref):
    sources, total, _ = got_ref.shape
    rows = (total - OWN) // (TILES + 2)
    return sources, rows, sources * rows // BLOCK


def fill(win, got_ref, halo_ref, tiles):
    sources, rows, _ = sizes_of(got_ref)
    for q in range(tiles):
        win[q, :TOP] = halo_ref[:, q * LANES : (q + 1) * LANES]
        for s in range(sources):
            at = TOP + s * rows
            win[q, at : at + rows] = got_ref[s, q * rows : (q + 1) * rows, :].astype(F32)


def conv_tile(win, taps, j, q):
    first = j * BLOCK + TOP - taps[q].shape[0] + 1
    return conv(lambda k: win[q, first + k : first + k + BLOCK], taps[q]).astype(BF16)


def steps_of(got_ref, own_ref):
    _, rows, blocks = sizes_of(got_ref)
    per = BLOCK // rows
    lead = lead_of(own_ref)
    at = got_ref.shape[1] - OWN
    raws = []
    for j in range(blocks):
        raw = got_ref[j * per, at:, :].astype(F32)
        for s in range(1, per):
            raw = raw + got_ref[j * per + s, at:, :].astype(F32)
        raws.append(raw + own_ref[lead : lead + OWN, :LANES])
    raw = jnp.concatenate(raws, 0)
    dt = jnp.maximum(raw, 0.0) + jnp.log1p(jnp.exp(-jnp.abs(raw)))
    rate = jnp.concatenate([-jnp.exp(own_ref[lead + OWN :, :LANES])] * blocks, 0)
    upto = (iota((BLOCK, BLOCK), 0) <= iota((BLOCK, BLOCK), 1)).astype(F32).astype(BF16)
    sums = dot(stacked(dt * rate, 4), upto)
    n = blocks * OWN
    cum = sums[:n] + sums[n : 2 * n] + sums[2 * n : 3 * n] + sums[3 * n :]
    return [[v[j * OWN : (j + 1) * OWN] for j in range(blocks)] for v in (dt, cum)]


def total_body(got_ref, halo_ref, own_ref, send_ref, other_ref, win, sem, *, last_but_one):
    sources, rows, blocks = sizes_of(got_ref)
    if last_but_one:
        copy = pltpu.make_async_copy(got_ref, other_ref, sem)
        copy.start()
    dts, cums = steps_of(got_ref, own_ref)
    taps = tiles_of(own_ref)
    fill(win, got_ref, halo_ref, TILES + 1)
    lefts, rights = [], []
    after = jnp.zeros((OWN, 1), F32)
    for j in reversed(range(blocks)):
        after = after + cums[j][:, BLOCK - 1 :]
        tail = expand(jnp.exp(after - cums[j]) * dts[j])
        x = jnp.concatenate([conv_tile(win, taps, j, q) for q in range(TILES)], 1)
        b = conv_tile(win, taps, j, TILES)
        lefts += [b, b]
        rights.append(stacked(x.astype(F32) * tail, 2))
    state = dot_t(jnp.concatenate(lefts, 0), jnp.concatenate(rights, 0))
    send_ref[:STATE] = state.astype(BF16)
    ends = [got_ref[sources - 1, q * rows : (q + 1) * rows, :].astype(F32)[rows - TOP :] for q in range(TILES + 2)]
    ends += [jnp.zeros_like(ends[0])] * (TILES - 2)
    half = TOP // 2
    upper = pltpu.roll(jnp.concatenate(ends[:TILES], 1), half, 0)
    keep = iota((TOP, WIDE), 0) < half
    send_ref[STATE:] = jnp.where(keep, upper, jnp.concatenate(ends[TILES:], 1)).astype(BF16)
    if last_but_one:
        copy.wait()
    else:
        other_ref[...] = expand(jnp.broadcast_to(jnp.exp(after), (OWN, LANES)))[:8]


def local_body(
    got_ref, halo_ref, own_ref, z_hbm,
    c_ref, part_ref, growth_ref, factor_ref, tail_ref, top_ref, gate_ref, order_ref, win, turn, z_ref, sem,
):
    fetch = pltpu.make_async_copy(z_hbm, z_ref, sem)
    fetch.start()
    _, _, blocks = sizes_of(got_ref)
    dts, cums = steps_of(got_ref, own_ref)
    taps = tiles_of(own_ref)
    fill(win, got_ref, halo_ref, TILES + 2)
    for q in range(TILES + 2):
        top_ref[q] = win[q, TOP : 2 * TOP]
    turn[...] = jnp.zeros_like(turn)
    for j in range(blocks):
        turn[j * OWN : (j + 1) * OWN] = cums[j]
    cols = turn[...].T
    t_at = iota((BLOCK, BLOCK), 0)
    s_at = iota((BLOCK, BLOCK), 1)
    left = iota((BLOCK, LANES), 1) < HEAD_DIM
    zero = jnp.zeros((BLOCK, LANES), BF16)
    past = jnp.zeros((OWN, 1), F32)
    local = None
    for j in range(blocks):
        at = j * BLOCK
        x = [conv_tile(win, taps, j, q) for q in range(TILES)]
        b = conv_tile(win, taps, j, TILES)
        c = conv_tile(win, taps, j, TILES + 1)
        c_ref[at : at + BLOCK] = c
        scores = lax.dot_general(c, b, (((1,), (1,)), ((), ())), preferred_element_type=F32)
        keep = t_at >= s_at
        if j == 0:
            keep = keep & (s_at >= TOP)
        scores = jnp.where(keep, scores, 0.0)
        cum, dt = cums[j], dts[j]
        last = cum[:, BLOCK - 1 :]
        grown = expand(jnp.exp(cum))
        if j > 1:
            past = past + cums[j - 1][:, BLOCK - 1 :]
        growth_ref[at : at + BLOCK] = expand(jnp.exp(cum + past)) if j > 1 else grown
        if j > 0:
            carried = dot(jnp.concatenate([c, c], 1), stacked(local, 2)) * grown
        for q in range(TILES):
            lo = q * LANES
            mixes = []
            for h in (2 * q, 2 * q + 1):
                col = j * OWN + h
                gap = jnp.minimum(cols[:, col : col + 1] - cum[h : h + 1], 0.0)
                mixes.append((scores * jnp.exp(gap) * dt[h : h + 1]).astype(BF16))
            both = jnp.concatenate([jnp.where(left, x[q], zero), jnp.where(left, zero, x[q])], 0)
            part = dot(jnp.concatenate(mixes, 1), both)
            part_ref[at : at + BLOCK, lo : lo + LANES] = part if j == 0 else part + carried[:, lo : lo + LANES]
        tail = expand(jnp.exp(last - cum) * dt)
        if j == 0:
            tail_ref[...] = tail[:TOP]
            tail = jnp.where(iota((BLOCK, WIDE), 0) < TOP, 0.0, tail)
        if j + 1 < blocks:
            weighted = stacked(jnp.concatenate(x, 1).astype(F32) * tail, 2)
            fresh = dot_t(jnp.concatenate([b, b], 0), weighted)
            local = fresh if j == 0 else grown[BLOCK - 1 :] * local + fresh

    wide = OWN * TOP
    spread = one_hot(4 * OWN, TOP)
    cum_t = dot_t(stacked(cums[0], 4), spread)
    same = iota((TOP, wide), 0) == iota((TOP, wide), 1) % TOP
    cum_s = jnp.sum(jnp.where(same, cum_t[:TOP], 0.0), axis=0, keepdims=True)
    dt_s = jnp.sum(jnp.where(same, dot_t(stacked(dts[0], 4), spread)[:TOP], 0.0), axis=0, keepdims=True)
    decay = jnp.exp(jnp.minimum(cum_t - cum_s, 0.0))
    seen = iota((BLOCK, wide), 0) >= iota((BLOCK, wide), 1) % TOP
    factor_ref[0] = jnp.where(seen, decay, 0.0)
    factor_ref[1] = jnp.broadcast_to(dt_s, (BLOCK, wide))
    order_ref[...] = jnp.zeros_like(order_ref)
    fetch.wait()
    for lo in range(0, z_ref.shape[1], WIDE):
        gate_ref[:, lo : lo + WIDE] = silu(z_ref[:, lo : lo + WIDE].astype(F32))


def carry_body(before_ref, own_ref, c_ref, part_ref, growth_ref, factor_ref, tail_ref, top_ref, y_ref, win, c_first):
    blocks = c_ref.shape[0] // BLOCK
    taps = tiles_of(own_ref)
    first = TOP - taps[0].shape[0] + 1

    halo = before_ref[STATE:].astype(F32)
    upper = pltpu.roll(halo, TOP // 2, 0)
    tops = []
    for q in range(TILES + 2):
        lo = q * LANES
        win[q, :TOP] = upper[:, lo : lo + LANES] if q < TILES else halo[:, lo - WIDE : lo - WIDE + LANES]
        win[q, TOP:] = top_ref[q]
        done = conv(lambda k: win[q, first + k : first + k + TOP], taps[q])
        tops.append(done.astype(BF16).astype(F32))
    x_top = jnp.concatenate(tops[:TILES], 1)
    b_top = tops[TILES]
    b_twice = jnp.concatenate([b_top, b_top], 0).astype(BF16)
    head = dot_t(b_twice, stacked(x_top * tail_ref[...], 2))
    state = before_ref[:STATE]
    grown = growth_ref[:BLOCK]
    later = stacked(grown[BLOCK - 1 :] * state.astype(F32) + head, 2)

    c_first[...] = c_ref[:BLOCK].astype(F32)
    c_first[:TOP] = tops[TILES + 1]
    c = c_first[...].astype(BF16)
    wide = OWN * TOP
    scores = lax.dot_general(
        c, jnp.concatenate([b_top] * OWN, 0).astype(BF16), (((1,), (1,)), ((), ())), preferred_element_type=F32
    )
    mix = (scores * factor_ref[0] * factor_ref[1]).astype(BF16)
    shape = (wide, WIDE)
    own = iota(shape, 0) // TOP == iota(shape, 1) // HEAD_DIM
    added = dot(mix, jnp.where(own, jnp.concatenate([x_top] * OWN, 0), 0.0).astype(BF16))
    y_ref[:BLOCK] = (part_ref[:BLOCK] + added + dot(c, state) * grown).astype(BF16)
    for j in range(1, blocks):
        at = j * BLOCK
        c = c_ref[at : at + BLOCK]
        carried = dot(jnp.concatenate([c, c], 1), later)
        y_ref[at : at + BLOCK] = (part_ref[at : at + BLOCK] + carried * growth_ref[at : at + BLOCK]).astype(BF16)


def unset_body(*refs):
    refs[-1][...] = jnp.zeros_like(refs[-1])


def norm_body(early_ref, late_ref, gate_ref, gain_ref, out_hbm, out_v, sem):
    count = late_ref.shape[0]
    per = count // GROUPS
    leads = (lax.axis_index("outer") == 0) & (lax.axis_size("outer") == 2)
    half_turn = turned()
    copies = []
    for g in range(GROUPS):
        gated = []
        square = 0.0
        for k in range(g * per, (g + 1) * per):
            at = holder(k, half_turn, count)
            y = jnp.where(leads, early_ref[at].astype(F32), late_ref[at].astype(F32))
            v = y * gate_ref[:, k * WIDE : (k + 1) * WIDE]
            gated.append(v)
            square = square + jnp.sum(v * v, axis=1, keepdims=True)
        scale = lax.rsqrt(square / (per * WIDE) + eps_norm)
        for k in range(g * per, (g + 1) * per):
            at = k * WIDE
            gain = gain_ref[:, at : at + WIDE]
            out_v[:, at : at + WIDE] = (gated[k - g * per] * scale * gain).astype(BF16)
        part = pl.ds(g * per * WIDE, per * WIDE)
        copies.append(pltpu.make_async_copy(out_v.at[:, part], out_hbm.at[:, part], sem.at[g]))
        copies[-1].start()
    for copy in copies:
        copy.wait()


def shift(array, distance):
    outer, inner, head = (lax.axis_size(a) for a in AXES)
    count = inner * head

    def at(stretch, block):
        return stretch * count + holder(block, stretch % 2 * (count // 2), count)

    route = [(at(o, k), at(o + distance, k)) for o in range(outer - distance) for k in range(count)]
    return lax.ppermute(array, AXES, route)


def kernel(body, name, ins, outs, scratch=(), cost=None, out_specs=None):
    return pl.pallas_call(
        body,
        in_specs=ins,
        out_specs=out_specs or [IN_VMEM] * len(outs),
        out_shape=outs,
        scratch_shapes=list(scratch),
        compiler_params=pltpu.CompilerParams(vmem_limit_bytes=16 * 2**20),
        cost_estimate=cost,
        name=name,
    )


def shards(x_in, b_in, c_in, dt_in, z_in, conv_x, input_state_taps, conv_c, dt_bias, a_log, norm_gain):
    outer, inner, head = (lax.axis_size(a) for a in AXES)
    dests = inner * head
    rows = x_in.shape[0]
    tokens = rows * dests
    blocks = tokens // BLOCK

    def of(dtype, *shape):
        return jax.ShapeDtypeStruct(shape, dtype)

    total = (TILES + 2) * rows + OWN
    lead = conv_x.shape[0]
    hbm = pl.BlockSpec(memory_space=pltpu.HBM)
    rows_of = [v.reshape(1, -1) for v in (dt_bias, a_log, norm_gain)]
    operands = (x_in, b_in, c_in, dt_in, conv_x, input_state_taps, conv_c, *rows_of)
    z_pinned = pltpu.with_memory_space_constraint(z_in, pltpu.HBM)
    sent, own, gain = kernel(
        pack_body, "pack", [hbm] * len(operands),
        [of(BF16, dests, total, LANES), of(F32, lead + 2 * OWN, WIDE + 2 * STATE), of(F32, 1, norm_gain.size)],
        [
            pltpu.VMEM(x_in.shape, BF16), pltpu.VMEM(b_in.shape, BF16), pltpu.VMEM(c_in.shape, BF16),
            pltpu.VMEM(dt_in.shape, BF16), pltpu.VMEM((BLOCK, LANES), F32),
            pltpu.VMEM((lead, WIDE), F32), pltpu.VMEM((2, lead, STATE), F32), pltpu.VMEM((2, 1, LANES), F32),
            pltpu.SemaphoreType.DMA((7,)), pltpu.SemaphoreType.DMA((6,)),
        ],
    )(*(pltpu.with_memory_space_constraint(a, pltpu.HBM) for a in operands))

    def exchanged(array):
        return lax.all_to_all(array, ("inner", "head"), 0, 0, tiled=True)

    extra = STATE + TOP
    wide = OWN * TOP

    def total_of(got, halo):
        last_but_one = outer == 2
        return kernel(
            functools.partial(total_body, last_but_one=last_but_one), "total", [IN_VMEM] * 3,
            [pltpu.VMEM((extra, WIDE), BF16), of(BF16, *got.shape) if last_but_one else of(F32, 8, WIDE)],
            [pltpu.VMEM((TILES + 1, TOP + tokens, LANES), F32), pltpu.SemaphoreType.DMA],
            out_specs=[IN_VMEM, hbm if last_but_one else IN_VMEM],
        )(got, halo, own)

    def local_of(got, halo):
        return kernel(
            local_body, "local", [IN_VMEM] * 3 + [hbm],
            [
                of(BF16, tokens, STATE), of(F32, tokens, WIDE), pltpu.VMEM((tokens, WIDE), F32), of(F32, 2, BLOCK, wide),
                of(F32, TOP, WIDE), of(F32, TILES + 2, TOP, LANES), pltpu.VMEM(z_in.shape, F32),
                of(F32, 8, LANES),
            ],
            [
                pltpu.VMEM((TILES + 2, TOP + tokens, LANES), F32), pltpu.VMEM((BLOCK, LANES), F32),
                pltpu.VMEM(z_in.shape, BF16), pltpu.SemaphoreType.DMA,
            ],
            pl.CostEstimate(
                flops=2 * blocks * OWN * BLOCK * BLOCK * 160,
                bytes_accessed=tokens * WIDE * 12,
                transcendentals=blocks * OWN * BLOCK * BLOCK,
            ),
        )(got, halo, own, z_pinned)

    def unset(like, *after):
        return tuple(kernel(unset_body, "unset", [IN_VMEM] * len(after), [of(a.dtype, *a.shape) for a in like])(*after))

    def leaving(before, *done):
        [y] = kernel(
            carry_body, "carry", [IN_VMEM] * 8, [of(BF16, tokens, WIDE)],
            [pltpu.VMEM((TILES + 2, 2 * TOP, LANES), F32), pltpu.VMEM((BLOCK, STATE), F32)],
        )(before, own, *done)
        return exchanged(y.reshape(dests, rows, WIDE))

    if outer == 2:
        halo = jnp.zeros((TOP, (TILES + 2) * LANES), F32)
        leads = lax.axis_index("outer") == 0
        send, kept = lax.cond(
            leads,
            lambda array: tuple(total_of(exchanged(array), halo)),
            lambda array: unset([of(BF16, extra, WIDE), sent]),
            sent,
        )
        before = shift(send, 1)

        def first(array, kept):
            *done, gate, order = local_of(kept, halo)
            *rest, nothing = unset([*done, send], order)
            return leaving(nothing, *done), tuple(rest), gate

        def second(array, kept):
            *done, gate, order = local_of(exchanged(array), halo)
            return unset([of(BF16, dests, rows, WIDE)], order)[0], tuple(done), gate

        early, done, gate = lax.cond(leads, first, second, sent, kept)
        late = lax.cond(
            leads,
            lambda before, done: unset([of(BF16, dests, rows, WIDE)])[0],
            lambda before, done: leaving(before, *done),
            before, done,
        )
    else:
        got = exchanged(sent)
        ends = got[-1, : (TILES + 2) * rows].reshape(TILES + 2, rows, LANES)[:, -TOP:]
        halo = shift(ends, 1).transpose(1, 0, 2).reshape(TOP, -1).astype(F32)
        send, fade = total_of(got, halo)
        before = shift(send, 1)
        entering, held, reach = before[:STATE].astype(F32), shift(fade, 1), 1
        while reach < outer - 1:
            entering = entering + held[:1] * shift(entering, reach)
            held = held * shift(held, reach)
            reach *= 2
        before = jnp.concatenate([entering.astype(BF16), before[STATE:]], 0)
        *done, gate, _ = local_of(got, halo)
        early = late = leaving(before, *done)

    [out] = kernel(
        norm_body, "norm", [IN_VMEM] * 4, [of(BF16, rows, dests * WIDE)],
        [pltpu.VMEM((rows, dests * WIDE), BF16), pltpu.SemaphoreType.DMA((GROUPS,))], out_specs=[hbm],
    )(early, late, gate, gain)
    return out


def solution(mesh):
    ctx, head = mesh.devices.shape
    inner = max(1, GROUPS * 16 // (OWN * head))
    cut = Mesh(mesh.devices.reshape(ctx // inner, inner, head), AXES)
    rows = P(AXES, None)
    return jax.shard_map(
        shards,
        mesh=cut,
        in_specs=(rows,) * 5 + (P(),) * 6,
        out_specs=rows,
        check_vma=False,
    )
```
